32 devices in a mesh: dp: 8 (over z, core), tensor: 4 (over y, x).
Axes of the slice: x: 2, y: 2, z: 4, core: 2. Of those that a mesh axis runs over, the one named last changes fastest.
Arguments:
- tokens: bfloat16 [16384, 2048], P('dp', 'tensor'), may hold values from -6 to 6
- lengths: int32 [8], P('dp'), may hold values from 512 to 2048, as said below
- cotangent: bfloat16 [16384, 2048], P('dp', 'tensor'), may hold values from -6 to 6
- w_norm_in: bfloat16 [2048], P('tensor'), may hold values from 0.099609375 to 1.8984375
- w_input: bfloat16 [2048, 2048], P(None, 'tensor'), may hold values from -0.125 to 0.125
- w_forget: bfloat16 [2048, 2048], P(None, 'tensor'), may hold values from -0.125 to 0.125
- w_gproj: bfloat16 [2048, 2048], P(None, 'tensor'), may hold values from -0.125 to 0.125
- lower_bound: bfloat16 [2048], P('tensor'), may hold values from 0 to 0.9765625
- w_gate_norm: bfloat16 [2048], P('tensor'), may hold values from 0.099609375 to 1.8984375
- w_output: bfloat16 [2048, 2048], P('tensor'), may hold values from -0.125 to 0.125
- w_norm_mid: bfloat16 [2048], P('tensor'), may hold values from 0.099609375 to 1.8984375
- w_gate: bfloat16 [2048, 5632], P(None, 'tensor'), may hold values from -0.125 to 0.125
- w_up: bfloat16 [2048, 5632], P(None, 'tensor'), may hold values from -0.125 to 0.125
- w_down: bfloat16 [5632, 2048], P('tensor'), may hold values from -0.078125 to 0.078125
Outputs:
- output: bfloat16 [16384, 2048], P('dp', 'tensor')
- grad_tokens: float32 [16384, 2048], P('dp', 'tensor')
- grad_norm_in: float32 [2048], P('tensor')
- grad_input: float32 [2048, 2048], P(None, 'tensor')
- grad_forget: float32 [2048, 2048], P(None, 'tensor')
- grad_gproj: float32 [2048, 2048], P(None, 'tensor')
- grad_lower: float32 [2048], P('tensor')
- grad_gate_norm: float32 [2048], P('tensor')
- grad_output: float32 [2048, 2048], P('tensor')
- grad_norm_mid: float32 [2048], P('tensor')
- grad_gate: float32 [2048, 5632], P(None, 'tensor')
- grad_up: float32 [2048, 5632], P(None, 'tensor')
- grad_down: float32 [5632, 2048], P('tensor')
The draws below stay inside these ranges and needn't reach their ends.
Inputs may be any that keep to these rules, and one draw needn't show every extreme that they name: `lengths`: some sequence has exactly 2048 used slots and some has exactly 512.
All inputs are finite; a program needn't handle non-finite values.
Results may differ from the reference program's by a relative error of at most 0.013.
Values may be sent and summed in bfloat16 or wider, within the bound.
A program may use at most 320 MiB of HBM per device.

```python
import jax
import jax.numpy as jnp
from jax import lax

D = 2048
FF = 5632
SLOTS = 2048
SEQS = 8
TOKENS = 16384


def draw_lengths(key, part):
    first_key, second_key = jax.random.split(jax.random.fold_in(key, 17))
    values = jax.random.randint(first_key, (SEQS,), SLOTS // 4, SLOTS + 1, dtype=jnp.int32)
    order = jax.random.permutation(second_key, SEQS)
    values = values.at[order[0]].set(SLOTS)
    values = values.at[order[1]].set(SLOTS // 4)
    return values.astype(jnp.int32)


def shard_levels(own_key, extent, cuts, low, high):
    def one(position, blocks):
        heights = jax.random.uniform(jax.random.fold_in(jax.random.fold_in(own_key, 6), position), (blocks,), jnp.float32, low / len(cuts), high / len(cuts))
        return jnp.repeat(jnp.exp(heights), extent[position] // blocks).reshape((-1,) + (1,) * (len(extent) - position - 1))

    loudness = one(*cuts[0])
    for cut in cuts[1:]:
        loudness = loudness * one(*cut)
    return loudness


def centred(rng, shape, spread, bound, pieces=(), kind=jnp.bfloat16):
    values = spread * jax.random.normal(rng, shape, jnp.float32)
    if pieces:
        values = values * shard_levels(rng, shape, pieces, -0.22, 0.18)
    return jnp.clip(values, -bound, bound).astype(kind)


def setup_inputs(seed: int = 0) -> dict:
    key_of = jax.random.split(jax.random.key(seed), 15)
    return {
        "tokens": centred(key_of[0], (TOKENS, D), 1.0, 6.0, ((0, 8), (1, 4))),
        "lengths": draw_lengths(jax.random.fold_in(key_of[14], 71), 0),
        "cotangent": centred(key_of[2], (TOKENS, D), 1.0, 6.0, ((0, 8), (1, 4))),
        "w_norm_in": jnp.clip(1.0 + 0.18 * jax.random.normal(key_of[3], (D,), jnp.float32), 0.099609375, 1.8984375).astype(jnp.bfloat16),
        "w_input": centred(key_of[4], (D, D), D ** -0.5, 0.125, ((1, 4),)),
        "w_forget": centred(key_of[5], (D, D), D ** -0.5, 0.125, ((1, 4),)),
        "w_gproj": centred(key_of[6], (D, D), D ** -0.5, 0.125, ((1, 4),)),
        "lower_bound": jnp.clip(0.9765625 * jax.random.uniform(key_of[7], (D,), jnp.float32) ** shard_levels(key_of[7], (D,), ((0, 4),), -0.2, 0.2), 0.0, 0.9765625).astype(jnp.bfloat16),
        "w_gate_norm": jnp.clip(1.0 + 0.18 * jax.random.normal(key_of[8], (D,), jnp.float32), 0.099609375, 1.8984375).astype(jnp.bfloat16),
        "w_output": centred(key_of[9], (D, D), D ** -0.5, 0.125, ((0, 4),)),
        "w_norm_mid": jnp.clip(1.0 + 0.18 * jax.random.normal(key_of[10], (D,), jnp.float32), 0.099609375, 1.8984375).astype(jnp.bfloat16),
        "w_gate": centred(key_of[11], (D, FF), D ** -0.5, 0.125, ((1, 4),)),
        "w_up": centred(key_of[12], (D, FF), D ** -0.5, 0.125, ((1, 4),)),
        "w_down": centred(key_of[13], (FF, D), FF ** -0.5, 0.078125, ((0, 4),)),
    }


EPSILON = 1e-06

@jax.custom_vjp
def low(v):
    return lax.optimization_barrier(v.astype(jnp.bfloat16)).astype(jnp.float32)

@jax.custom_vjp
def low_back(v):
    return v

def low_keep(v):
    return (low(v), None)

def low_pass(kept, grad):
    return (grad,)

def back_keep(v):
    return (v, None)

def back_low(kept, grad):
    return (low(grad),)
low.defvjp(low_keep, low_pass)
low_back.defvjp(back_keep, back_low)

def matmul(left, right):
    return jnp.dot(left, right, precision=lax.Precision.HIGHEST, preferred_element_type=jnp.float32)

def linear_scan(decay, source):

    def compose(earlier, later):
        return (earlier[0] * later[0], later[0] * earlier[1] + later[1])
    return lax.associative_scan(compose, (decay, source), axis=0)[1]

def block_forward(rows, w_norm_in, w_input, w_forget, w_gproj, lower_bound, w_gate_norm, w_output, w_norm_mid, w_gate, w_up, w_down):
    scale_in = lax.rsqrt(lax.optimization_barrier(jnp.mean(rows * rows, axis=-1, keepdims=True)) + EPSILON)
    normed_in = low(rows * scale_in * w_norm_in)
    in_pre = low_back(matmul(normed_in, w_input))
    forget_pre = low_back(matmul(normed_in, w_forget))
    gate_pre = low_back(matmul(normed_in, w_gproj))
    inner = jax.nn.silu(in_pre)
    decay = lower_bound + (1.0 - lower_bound) * jax.nn.sigmoid(forget_pre)
    state = linear_scan(decay, (1.0 - decay) * inner)
    gate_scale = lax.rsqrt(lax.optimization_barrier(jnp.mean(state * state, axis=-1, keepdims=True)) + EPSILON)
    mixed = low(state * gate_scale * w_gate_norm * jax.nn.silu(gate_pre))
    resid = rows + low_back(matmul(mixed, w_output))
    scale_mid = lax.rsqrt(lax.optimization_barrier(jnp.mean(resid * resid, axis=-1, keepdims=True)) + EPSILON)
    normed_mid = low(resid * scale_mid * w_norm_mid)
    ffn_gate = low_back(matmul(normed_mid, w_gate))
    ffn_up = low_back(matmul(normed_mid, w_up))
    hidden = low(jax.nn.silu(ffn_gate) * ffn_up)
    return resid + low_back(matmul(hidden, w_down))

def reference(tokens, lengths, cotangent, w_norm_in, w_input, w_forget, w_gproj, lower_bound, w_gate_norm, w_output, w_norm_mid, w_gate, w_up, w_down):
    params = tuple((p.astype(jnp.float32) for p in (w_norm_in, w_input, w_forget, w_gproj, lower_bound, w_gate_norm, w_output, w_norm_mid, w_gate, w_up, w_down)))
    seq_tokens = tokens.astype(jnp.float32).reshape(SEQS, SLOTS, D)
    valid = (jnp.arange(SLOTS, dtype=jnp.int32)[None, :] < lengths[:, None]).astype(jnp.float32)
    seq_cots = cotangent.astype(jnp.float32).reshape(SEQS, SLOTS, D) * valid[:, :, None]

    def per_sequence(totals, item):
        seq_rows, seq_cot = item
        result, pullback = jax.vjp(block_forward, seq_rows, *params)
        gradients = pullback(seq_cot)
        totals = tuple((a + b for a, b in zip(totals, gradients[1:])))
        return (totals, (result.astype(jnp.bfloat16), gradients[0]))
    empty_sums = tuple((jnp.zeros_like(p) for p in params))
    totals, (results, grad_rows) = lax.scan(per_sequence, empty_sums, (seq_tokens, seq_cots))
    return (results.reshape(TOKENS, D), grad_rows.reshape(TOKENS, D), totals[0], totals[1], totals[2], totals[3], totals[4], totals[5], totals[6], totals[7], totals[8], totals[9], totals[10])
```

```python
import functools

import jax
import jax.numpy as jnp
from jax import lax
from jax.experimental import pallas as pl
from jax.experimental.pallas import tpu as pltpu
from jax.sharding import PartitionSpec as P

EPSILON = 1e-06
MESH = pl.DeviceIdType.MESH
CHUNKS = 8
AHEAD = 2
VMEM_BYTES = 64_000_000
F32 = jnp.float32
BF16 = jnp.bfloat16
ANY = pl.BlockSpec(memory_space=pl.ANY)
WHOLE = pl.BlockSpec(memory_space=pltpu.VMEM)


def silu_slope(value):
    sigma = jax.nn.sigmoid(value)
    return sigma * (1.0 + value * (1.0 - sigma))


def plain_dot(left, right):
    return jnp.dot(left, right, preferred_element_type=F32)


def trans_dot(left, right):
    return lax.dot_general(left, right, (((0,), (0,)), ((), ())), preferred_element_type=F32)


def back_dot(left, right):
    return lax.dot_general(left, right, (((1,), (1,)), ((), ())), preferred_element_type=F32)


def rows_to_lanes(values):
    ones = jnp.ones((8, values.shape[1]), F32)
    return lax.dot_general(
        ones, values, (((1,), (1,)), ((), ())), precision=lax.Precision.HIGHEST,
        preferred_element_type=F32,
    )


def lanes_to_rows(values):
    ones = jnp.full((8, 128), 0.125, F32)
    wide = lax.dot_general(
        values, ones, (((0,), (0,)), ((), ())), precision=lax.Precision.HIGHEST,
        preferred_element_type=F32,
    )
    return wide[:, :1]


def neighbours():
    t = lax.axis_index("tensor")
    return t, t + 1 - 2 * (t % 2), t + 2 - 4 * (t // 2), 3 - t


def block(start, size):
    return pl.ds(pl.multiple_of(start * size, size), size)


def greet(devices):
    barrier = pltpu.get_barrier_semaphore()
    for device in devices:
        pl.semaphore_signal(barrier, inc=1, device_id=device, device_id_type=MESH)
    pl.semaphore_wait(barrier, len(devices))


def each(count, step):
    def body(i, carry):
        step(i)
        return carry

    lax.fori_loop(0, count, body, 0)


class Gather:
    def __init__(self, source, full, send, recv, rows, width):
        self.source, self.full, self.send, self.recv = source, full, send, recv
        self.rows, self.width = rows, width
        self.t, self.xn, self.yn, self.dg = neighbours()

    def direct(self, c, k):
        rows = block(c, self.rows)
        return pltpu.make_async_remote_copy(
            self.source.at[rows, :],
            self.full.at[rows, block(self.t, self.width)],
            self.send.at[k, c],
            self.recv.at[k, c],
            device_id={"tensor": self.xn if k == 0 else self.yn},
            device_id_type=MESH,
        )

    def relay(self, c, k):
        rows = block(2 * c + k, self.rows // 2)
        part = self.full.at[rows, block(self.xn if k == 0 else self.yn, self.width)]
        return pltpu.make_async_remote_copy(
            part,
            part,
            self.send.at[2 + k, c],
            self.recv.at[2 + k, c],
            device_id={"tensor": self.yn if k == 0 else self.xn},
            device_id_type=MESH,
        )

    def start(self, c):
        self.direct(c, 0).start()
        self.direct(c, 1).start()

    def forward(self, c):
        for k in range(2):
            self.direct(c, k).wait_recv()
            self.relay(c, k).start()

    def finish(self, c):
        self.relay(c, 0).wait_recv()
        self.relay(c, 1).wait_recv()

    def drain(self, c):
        for k in range(2):
            self.direct(c, k).wait_send()
            self.relay(c, k).wait_send()


LANES = 128


def scan_rows(decay, source, state, product, head):
    planes, rows, _ = decay.shape
    seg = rows // 8

    def first(j, held):
        out = []
        for q in range(planes):
            now, prod = held[q]
            d = decay[q, pl.ds(j, 8, stride=seg), :]
            now = d * now + source[q, pl.ds(j, 8, stride=seg), :]
            prod = d * prod
            state[q, pl.ds(head + j, 8, stride=seg), :] = now
            product[q, pl.ds(j, 8, stride=seg), :] = prod
            out.append((now, prod))
        return tuple(out)

    zero, one = jnp.zeros((8, LANES), F32), jnp.ones((8, LANES), F32)
    ends = lax.fori_loop(0, seg, first, ((zero, one),) * planes, unroll=4)
    entries = []
    for q in range(planes):
        last, prod = ends[q]
        carry = state[q, head - 1 : head, :]
        parts = []
        for s in range(8):
            parts.append(carry)
            carry = prod[s : s + 1] * carry + last[s : s + 1]
        entries.append(jnp.concatenate(parts, axis=0))

    def second(j, held):
        for q in range(planes):
            state[q, pl.ds(head + j, 8, stride=seg), :] += (
                product[q, pl.ds(j, 8, stride=seg), :] * entries[q]
            )
        return held

    lax.fori_loop(0, seg, second, 0, unroll=4)


def to_planes(ref, rows, value):
    for q in range(value.shape[1] // LANES):
        ref[q, rows, :] = value[:, q * LANES : (q + 1) * LANES]


def from_planes(ref, rows):
    return jnp.concatenate([ref[q, rows, :] for q in range(ref.shape[0])], axis=1)


def mixer_kernel(
    tok, wout, gains, w_in, w_for, w_gp, lower, gain_gate,
    normed, tok_full, wout_full, gains_full, scale_in, pre_in, pre_for, pre_gp, state, diff, mixed, squares,
    full, wfull, vin, vfor, vgp, gbuf, dec, src, prod, hbuf,
    send, recv, wsend, wrecv, xsend, xrecv, gsend, grecv, lsem, osem,
):
    s = pl.program_id(0)
    chunks = pl.num_programs(0) - 1
    rows, width = pre_in.shape
    feats = full.shape[1]
    t, xn, yn, dg = neighbours()
    me = lax.axis_index("dp")
    core = me % 2
    partner = {"dp": me + 1 - 2 * core}
    peers = ({"tensor": xn}, {"tensor": yn}, {"tensor": dg})
    gather = Gather(tok, full, send, recv, rows, width)
    planes = width // LANES
    half = width // 2
    piece = width // 4

    def w_direct(k, p):
        return pltpu.make_async_remote_copy(
            wout.at[block(2 * core + p, piece), :],
            wfull.at[block(4 * t + 2 * core + p, piece), :],
            wsend.at[k, p],
            wrecv.at[k, p],
            device_id=peers[k],
            device_id_type=MESH,
        )

    def w_relay(k):
        part = wfull.at[block(4 * (xn if k == 0 else yn) + 2 * core + k, piece), :]
        return pltpu.make_async_remote_copy(
            part, part, wsend.at[2, k], wrecv.at[2, k], device_id=peers[1 - k], device_id_type=MESH
        )

    def w_swap(k):
        part = wfull.at[block(2 * (xn, yn, dg)[k] + core, half), :]
        return pltpu.make_async_remote_copy(
            part, part, xsend.at[k], xrecv.at[k], device_id=partner, device_id_type=MESH
        )

    def gain_copy(k):
        return pltpu.make_async_remote_copy(
            gains, gbuf.at[t], gsend.at[k], grecv.at[k], device_id=peers[k], device_id_type=MESH
        )

    loads = (
        pltpu.make_async_copy(tok, full.at[:, block(t, width)], lsem.at[0]),
        pltpu.make_async_copy(wout, wfull.at[block(t, width), :], lsem.at[1]),
        pltpu.make_async_copy(w_in, vin, lsem.at[2]),
        pltpu.make_async_copy(w_for, vfor, lsem.at[3]),
        pltpu.make_async_copy(w_gp, vgp, lsem.at[4]),
        pltpu.make_async_copy(gains, gbuf.at[t], lsem.at[5]),
    )

    def tok_out(c):
        return pltpu.make_async_copy(
            full.at[block(c, rows), :], tok_full.at[block(c, rows), :], osem.at[c]
        )

    w_out = pltpu.make_async_copy(wfull, wout_full, lsem.at[6])

    @pl.when(s == 0)
    def _():
        for load in loads:
            load.start()
        greet(peers + (partner,))
        for k in range(3):
            gain_copy(k).start()
        for p in range(2):
            w_direct(0, p).start()
            w_direct(1, p).start()
        for c in range(AHEAD):
            gather.start(c)
        hbuf[:, 0:8, :] = jnp.zeros((planes, 8, LANES), F32)
        for p in range(2):
            w_direct(0, p).wait_recv()
            w_direct(1, p).wait_recv()
        w_relay(0).start()
        w_relay(1).start()
        w_swap(0).start()
        w_swap(1).start()
        for load in loads:
            load.wait()
        for k in range(3):
            gain_copy(k).wait_recv()
        for j in range(4):
            gains_full[:, j * width : (j + 1) * width] = gbuf[j]

    @pl.when(s == 2)
    def _():
        w_relay(0).wait_recv()
        w_relay(1).wait_recv()
        w_swap(2).start()

    @pl.when(s == chunks - 1)
    def _():
        for k in range(3):
            w_swap(k).wait_recv()
        w_out.start()

    @pl.when(s < chunks)
    def _():
        gather.forward(s)

        @pl.when(s + AHEAD < chunks)
        def _():
            gather.start(s + AHEAD)

    @pl.when(s >= 1)
    def _():
        c = s - 1
        gather.finish(c)
        tok_out(c).start()
        gain_in = gains_full[0:1, :]
        low = lower[...]
        gain = gain_gate[...]

        def norm_rows(i):
            x = full[block(c * (rows // 32) + i, 32), :].astype(F32)
            scale = lax.rsqrt(jnp.sum(x * x, axis=1, keepdims=True) / feats + EPSILON)
            here = block(i, 32)
            normed[here, :] = (x * scale * gain_in).astype(BF16)
            scale_in[here, :] = jnp.broadcast_to(scale, (32, 128))

        each(rows // 32, norm_rows)
        pre_in[...] = plain_dot(normed[...], vin[...])
        pre_for[...] = plain_dot(normed[...], vfor[...])
        pre_gp[...] = plain_dot(normed[...], vgp[...])

        def gate_rows(i):
            here = block(i, 32)
            decay = low + (1.0 - low) * jax.nn.sigmoid(pre_for[here, :])
            to_planes(dec, here, decay)
            to_planes(src, here, (1.0 - decay) * jax.nn.silu(pre_in[here, :]))

        each(rows // 32, gate_rows)
        scan_rows(dec, src, hbuf, prod, 8)
        diff[...] = from_planes(hbuf, slice(7, 7 + rows))

        def mix_rows(i):
            here = block(i, 32)
            h = from_planes(hbuf, pl.ds(pl.multiple_of(8 + i * 32, 8), 32))
            state[here, :] = h
            diff[here, :] -= jax.nn.silu(pre_in[here, :])
            mixed[here, :] = (h * gain * jax.nn.silu(pre_gp[here, :])).astype(BF16)

        each(rows // 32, mix_rows)
        h = state[...]
        squares[0] = rows_to_lanes(h * h)
        hbuf[:, 7:8, :] = hbuf[:, 7 + rows : 8 + rows, :]

    @pl.when(s == chunks)
    def _():
        each(chunks, gather.drain)
        each(chunks, lambda c: tok_out(c).wait())
        for k in range(3):
            gain_copy(k).wait_send()
            w_swap(k).wait_send()
        for p in range(2):
            w_direct(0, p).wait_send()
            w_direct(1, p).wait_send()
            w_relay(p).wait_send()
        w_out.wait()


def later(s):
    return (jnp.maximum(s - 1, 0), 0)


def mixer_forward(tok, wout, gains, w_in, w_for, w_gp, lower, gain_gate):
    total, width = tok.shape
    feats = w_in.shape[0]
    rows = total // CHUNKS

    def out(n, dtype):
        return jax.ShapeDtypeStruct((total, n), dtype), pl.BlockSpec((rows, n), later)

    outs = [
        out(feats, BF16),
        (jax.ShapeDtypeStruct((total, feats), BF16), ANY),
        (jax.ShapeDtypeStruct((feats, feats), BF16), ANY),
        (jax.ShapeDtypeStruct((8, feats), F32), WHOLE),
        out(128, F32),
        out(width, F32),
        out(width, F32),
        out(width, F32),
        out(width, F32),
        out(width, F32),
        out(width, BF16),
        (
            jax.ShapeDtypeStruct((CHUNKS, 8, rows), F32),
            pl.BlockSpec((1, 8, rows), lambda s: (jnp.maximum(s - 1, 0), 0, 0)),
        ),
    ]
    dma = pltpu.SemaphoreType.DMA
    return pl.pallas_call(
        mixer_kernel,
        grid=(CHUNKS + 1,),
        out_shape=[o[0] for o in outs],
        out_specs=[o[1] for o in outs],
        in_specs=[ANY, ANY, WHOLE, ANY, ANY, ANY, WHOLE, WHOLE],
        scratch_shapes=[
            pltpu.VMEM((total, feats), BF16),
            pltpu.VMEM((feats, feats), BF16),
            pltpu.VMEM((feats, width), BF16),
            pltpu.VMEM((feats, width), BF16),
            pltpu.VMEM((feats, width), BF16),
            pltpu.VMEM((4, 8, width), F32),
            pltpu.VMEM((width // LANES, rows, LANES), F32),
            pltpu.VMEM((width // LANES, rows, LANES), F32),
            pltpu.VMEM((width // LANES, rows, LANES), F32),
            pltpu.VMEM((width // LANES, rows + 8, LANES), F32),
            dma((4, CHUNKS)),
            dma((4, CHUNKS)),
            dma((3, 2)),
            dma((3, 2)),
            dma((3,)),
            dma((3,)),
            dma((3,)),
            dma((3,)),
            dma((7,)),
            dma((CHUNKS,)),
        ],
        compiler_params=pltpu.CompilerParams(
            collective_id=1, has_side_effects=True, vmem_limit_bytes=VMEM_BYTES
        ),
        name="mixer_forward",
    )(tok, wout, gains, w_in, w_for, w_gp, lower, gain_gate)


def ffn_kernel(
    lens, mixed, cot, squares, gains, tok_full, wout, w_gate, w_up, w_down,
    normed, hidden, g_gate, g_up, cot_out, mix_out, scale_gate, scale_mid,
    mfull, cfull, vout, vgate, vup, vdown, sbuf, mo, res, gbuf, ubuf, hbuf,
    send, recv, csend, crecv, ssend, srecv, lsem,
):
    s = pl.program_id(0)
    chunks = pl.num_programs(0) - 1
    width = mixed.shape[1]
    rows, feats = normed.shape
    hid = hidden.shape[1]
    t, xn, yn, dg = neighbours()
    peers = ({"tensor": xn}, {"tensor": yn}, {"tensor": dg})
    gather = Gather(mixed, mfull, send, recv, rows, width)
    cgather = Gather(cot, cfull, csend, crecv, rows, width)

    def square_copy(k):
        return pltpu.make_async_remote_copy(
            squares, sbuf.at[t], ssend.at[k], srecv.at[k], device_id=peers[k], device_id_type=MESH
        )

    loads = (
        pltpu.make_async_copy(mixed, mfull.at[:, block(t, width)], lsem.at[0]),
        pltpu.make_async_copy(cot, cfull.at[:, block(t, width)], lsem.at[1]),
        pltpu.make_async_copy(squares, sbuf.at[t], lsem.at[2]),
        pltpu.make_async_copy(wout, vout, lsem.at[3]),
        pltpu.make_async_copy(w_gate, vgate, lsem.at[4]),
        pltpu.make_async_copy(w_up, vup, lsem.at[5]),
        pltpu.make_async_copy(w_down, vdown, lsem.at[6]),
    )

    @pl.when(s == 0)
    def _():
        greet(peers)
        for k in range(3):
            square_copy(k).start()
        for c in range(AHEAD):
            gather.start(c)
            cgather.start(c)
        for load in loads:
            load.start()
        for load in loads:
            load.wait()
        for k in range(3):
            square_copy(k).wait_recv()

    @pl.when(s < chunks)
    def _():
        gather.forward(s)
        cgather.forward(s)

        @pl.when(s + AHEAD < chunks)
        def _():
            gather.start(s + AHEAD)
            cgather.start(s + AHEAD)

    @pl.when(s >= 1)
    def _():
        c = s - 1
        gain_mid = gains[1:2, :]
        gather.finish(c)
        here = block(c, rows)
        each(
            feats // width,
            lambda b: mo.__setitem__(
                (slice(None), block(b, width)), plain_dot(mfull[here, :], vout[:, block(b, width)])
            ),
        )
        total = sbuf[0, c] + sbuf[1, c] + sbuf[2, c] + sbuf[3, c]
        scale = lax.rsqrt(lanes_to_rows(total) / feats + EPSILON)
        scale_gate[...] = jnp.broadcast_to(scale, (rows, 128))

        def norm_rows(i):
            part = block(i, 32)
            m = mo[part, :] * scale_gate[part, 0:1]
            mix_out[part, :] = m.astype(BF16)
            r = m + tok_full[part, :].astype(F32)
            mid = lax.rsqrt(jnp.sum(r * r, axis=1, keepdims=True) / feats + EPSILON)
            scale_mid[part, :] = jnp.broadcast_to(mid, (32, 128))
            normed[part, :] = (r * mid * gain_mid).astype(BF16)

        each(rows // 32, norm_rows)
        gbuf[...] = plain_dot(normed[...], vgate[...])
        ubuf[...] = plain_dot(normed[...], vup[...])
        cgather.finish(c)
        length = lens[0]

        def mask_rows(i):
            part = block(i, 32)
            position = c * rows + i * 32 + lax.broadcasted_iota(jnp.int32, (32, feats), 0)
            value = cfull[block(c * (rows // 32) + i, 32), :]
            cot_out[part, :] = jnp.where(position < length, value.astype(F32), 0.0).astype(BF16)

        each(rows // 32, mask_rows)
        hbuf[...] = back_dot(cot_out[...], vdown[...])

        def ffn_rows(i):
            part = block(i, 16)
            g = gbuf[part, :]
            u = ubuf[part, :]
            back = hbuf[part, :]
            sigma = jax.nn.sigmoid(g)
            act = g * sigma
            hidden[part, :] = (act * u).astype(BF16)
            g_gate[part, :] = (back * u * (sigma * (1.0 + g * (1.0 - sigma)))).astype(BF16)
            g_up[part, :] = (back * act).astype(BF16)

        each(rows // 16, ffn_rows)

    @pl.when(s == chunks)
    def _():
        each(chunks, gather.drain)
        each(chunks, cgather.drain)
        for k in range(3):
            square_copy(k).wait_send()


def ffn_forward(lens, mixed, cot, squares, gains, tok_full, wout, w_gate, w_up, w_down):
    total, width = mixed.shape
    feats, hid = w_gate.shape
    rows = total // CHUNKS

    def out(n, dtype):
        return jax.ShapeDtypeStruct((total, n), dtype), pl.BlockSpec((rows, n), later)

    outs = [
        out(feats, BF16),
        out(hid, BF16),
        out(hid, BF16),
        out(hid, BF16),
        out(feats, BF16),
        out(feats, BF16),
        out(128, F32),
        out(128, F32),
    ]
    dma = pltpu.SemaphoreType.DMA
    return pl.pallas_call(
        ffn_kernel,
        grid=(CHUNKS + 1,),
        out_shape=[o[0] for o in outs],
        out_specs=[o[1] for o in outs],
        in_specs=[
            pl.BlockSpec(memory_space=pltpu.SMEM),
            ANY, ANY, WHOLE, WHOLE,
            pl.BlockSpec((rows, feats), later),
            ANY, ANY, ANY, ANY,
        ],
        scratch_shapes=[
            pltpu.VMEM((total, feats), BF16),
            pltpu.VMEM((total, feats), BF16),
            pltpu.VMEM((feats, feats), BF16),
            pltpu.VMEM((feats, hid), BF16),
            pltpu.VMEM((feats, hid), BF16),
            pltpu.VMEM((hid, feats), BF16),
            pltpu.VMEM((4, CHUNKS, 8, rows), F32),
            pltpu.VMEM((rows, feats), F32),
            pltpu.VMEM((8, 128), F32),
            pltpu.VMEM((rows, hid), F32),
            pltpu.VMEM((rows, hid), F32),
            pltpu.VMEM((rows, hid), F32),
            dma((4, CHUNKS)),
            dma((4, CHUNKS)),
            dma((4, CHUNKS)),
            dma((4, CHUNKS)),
            dma((3,)),
            dma((3,)),
            dma((7,)),
        ],
        compiler_params=pltpu.CompilerParams(
            collective_id=2, has_side_effects=True, vmem_limit_bytes=VMEM_BYTES
        ),
        name="ffn_forward",
    )(lens, mixed, cot, squares, gains, tok_full, wout, w_gate, w_up, w_down)


def linear_scan(decay, source):

    def compose(earlier, later):
        return (earlier[0] * later[0], later[0] * earlier[1] + later[1])

    return lax.associative_scan(compose, (decay, source), axis=1)[1]


def on_device(
    tokens, lengths, cotangent, w_norm_in, w_input, w_forget, w_gproj, lower_bound, w_gate_norm,
    w_output, w_norm_mid, w_gate, w_up, w_down,
):
    D = tokens.shape[1] * 4
    row_count = tokens.shape[0]
    channels = w_input.shape[1]
    block_shape = (1, row_count, channels)
    gains = jnp.concatenate([w_norm_in[None], w_norm_mid[None], jnp.zeros((6, w_norm_in.shape[0]), BF16)], 0).astype(F32)
    lower = lower_bound.astype(F32)[None]
    gain_gate = w_gate_norm.astype(F32)[None]
    (normed_in, tok_full, wout_full, gains_full, scale_in, in_pre, forget_pre, gate_pre, state, diff, mixed_raw, squares) = mixer_forward(
        tokens, w_output, gains, w_input, w_forget, w_gproj, lower, gain_gate)
    (normed_mid, hidden, grad_ffn_gate, grad_ffn_up, cot_full, mix_out, scale_gate, scale_mid) = ffn_forward(
        lengths, mixed_raw, cotangent, squares, gains_full, tok_full, wout_full, w_gate, w_up, w_down)
    t = lax.axis_index("tensor")
    own = lambda a: lax.dynamic_slice_in_dim(a, t * channels, channels, 1)
    gate_scale = scale_gate[:, :1]
    scale_mid = scale_mid[:, :1]
    scale_in = scale_in[:, :1]
    inner = jax.nn.silu(in_pre)
    forget_sig = jax.nn.sigmoid(forget_pre)
    decay = lower + (1.0 - lower) * forget_sig
    decay_blocks = decay.reshape(block_shape)
    normed_state = state * gate_scale
    swish_gate = jax.nn.silu(gate_pre)
    mixed = (normed_state * gain_gate * swish_gate).astype(BF16)
    token_share = tokens.astype(F32)
    resid = token_share + own(mix_out).astype(F32)
    gain_mid = w_norm_mid.astype(F32)
    ffn_share = lax.psum_scatter(
        plain_dot(hidden, w_down).astype(BF16), "tensor", scatter_dimension=1, tiled=True
    ).astype(F32)
    output = (resid + ffn_share).astype(BF16)
    masked_cot = own(cot_full)
    grad_down_w = trans_dot(hidden, cot_full)
    grad_gate_w = trans_dot(normed_mid, grad_ffn_gate)
    grad_up_w = trans_dot(normed_mid, grad_ffn_up)
    grad_normed_mid = lax.psum_scatter(
        (back_dot(grad_ffn_gate, w_gate) + back_dot(grad_ffn_up, w_up)).astype(BF16),
        "tensor", scatter_dimension=1, tiled=True,
    ).astype(F32)
    grad_gain_mid = jnp.sum(grad_normed_mid * resid * scale_mid, axis=0)
    weighted_mid = grad_normed_mid * gain_mid
    mid_total = lax.psum(jnp.sum(weighted_mid * resid, axis=1), "tensor")
    grad_resid = masked_cot.astype(F32) + scale_mid * weighted_mid - resid * scale_mid**3 * (mid_total / D)[:, None]
    grad_mix = lax.all_gather(grad_resid.astype(BF16), "tensor", axis=1, tiled=True)
    grad_output_w = trans_dot(mixed, grad_mix)
    grad_mixed = back_dot(grad_mix, w_output)
    grad_gain_gate = jnp.sum(grad_mixed * normed_state * swish_gate, axis=0)
    grad_gate_pre = (grad_mixed * normed_state * gain_gate * silu_slope(gate_pre)).astype(BF16)
    grad_normed_state = grad_mixed * gain_gate * swish_gate
    state_inner = lax.psum(jnp.sum(grad_normed_state * state, axis=1), "tensor")
    grad_state = gate_scale * grad_normed_state - state * gate_scale**3 * (state_inner / D)[:, None]
    next_decay = jnp.concatenate([decay_blocks[:, 1:], jnp.zeros((1, 1, channels), F32)], axis=1)
    adjoint = jnp.flip(
        linear_scan(jnp.flip(next_decay, 1), jnp.flip(grad_state.reshape(block_shape), 1)), 1
    ).reshape(row_count, channels)
    grad_decay = adjoint * diff
    grad_in_pre = (adjoint * (1.0 - decay) * silu_slope(in_pre)).astype(BF16)
    grad_forget_pre = (grad_decay * (1.0 - lower) * forget_sig * (1.0 - forget_sig)).astype(BF16)
    grad_lower = jnp.sum(grad_decay * (1.0 - forget_sig), axis=0)
    grad_input_w = trans_dot(normed_in, grad_in_pre)
    grad_forget_w = trans_dot(normed_in, grad_forget_pre)
    grad_gproj_w = trans_dot(normed_in, grad_gate_pre)
    grad_normed_in = lax.psum_scatter(
        (back_dot(grad_in_pre, w_input) + back_dot(grad_forget_pre, w_forget) + back_dot(grad_gate_pre, w_gproj)).astype(BF16),
        "tensor", scatter_dimension=1, tiled=True,
    ).astype(F32)
    grad_gain_in = jnp.sum(grad_normed_in * token_share * scale_in, axis=0)
    weighted_in = grad_normed_in * w_norm_in.astype(F32)
    in_total = lax.psum(jnp.sum(weighted_in * token_share, axis=1), "tensor")
    grad_tokens = grad_resid + scale_in * weighted_in - token_share * scale_in**3 * (in_total / D)[:, None]
    small = lax.psum(jnp.stack([grad_gain_in, grad_lower, grad_gain_gate, grad_gain_mid]), "dp")
    big = [lax.psum(g.astype(BF16), "dp").astype(F32) for g in (grad_input_w, grad_forget_w, grad_gproj_w, grad_output_w, grad_gate_w, grad_up_w, grad_down_w)]
    return (output, grad_tokens, small[0], big[0], big[1], big[2], small[1], small[2], big[3], small[3], big[4], big[5], big[6])


def solution(mesh):
    rows, cols, vec = P(None, "tensor"), P("tensor", None), P("tensor")
    both = P("dp", "tensor")
    in_specs = (both, P("dp"), both, vec, rows, rows, rows, vec, vec, cols, vec, rows, rows, cols)
    out_specs = (both, both, vec, rows, rows, rows, vec, vec, cols, vec, rows, rows, cols)
    return jax.shard_map(on_device, mesh=mesh, in_specs=in_specs, out_specs=out_specs, check_vma=False)
```

```python
import functools

import jax
import jax.numpy as jnp
from jax import lax
from jax.experimental import pallas as pl
from jax.experimental.pallas import tpu as pltpu
from jax.sharding import PartitionSpec as P

EPSILON = 1e-06
MESH = pl.DeviceIdType.MESH
CHUNKS = 8
AHEAD = 2
VMEM_BYTES = 67_000_000
F32 = jnp.float32
BF16 = jnp.bfloat16
ANY = pl.BlockSpec(memory_space=pl.ANY)
WHOLE = pl.BlockSpec(memory_space=pltpu.VMEM)


def silu_slope(value):
    sigma = jax.nn.sigmoid(value)
    return sigma * (1.0 + value * (1.0 - sigma))


def plain_dot(left, right):
    return jnp.dot(left, right, preferred_element_type=F32)


def trans_dot(left, right):
    return lax.dot_general(left, right, (((0,), (0,)), ((), ())), preferred_element_type=F32)


def back_dot(left, right):
    return lax.dot_general(left, right, (((1,), (1,)), ((), ())), preferred_element_type=F32)


def rows_to_lanes(values):
    ones = jnp.ones((8, values.shape[1]), F32)
    return lax.dot_general(
        ones, values, (((1,), (1,)), ((), ())), precision=lax.Precision.HIGHEST,
        preferred_element_type=F32,
    )


def lanes_to_rows(values):
    ones = jnp.full((8, 128), 0.125, F32)
    wide = lax.dot_general(
        values, ones, (((0,), (0,)), ((), ())), precision=lax.Precision.HIGHEST,
        preferred_element_type=F32,
    )
    return wide[:, :1]


def neighbours():
    t = lax.axis_index("tensor")
    return t, t + 1 - 2 * (t % 2), t + 2 - 4 * (t // 2), 3 - t


def block(start, size):
    return pl.ds(pl.multiple_of(start * size, size), size)


def greet(devices):
    barrier = pltpu.get_barrier_semaphore()
    for device in devices:
        pl.semaphore_signal(barrier, inc=1, device_id=device, device_id_type=MESH)
    pl.semaphore_wait(barrier, len(devices))


def each(count, step):
    def body(i, carry):
        step(i)
        return carry

    lax.fori_loop(0, count, body, 0)


class Gather:
    def __init__(self, source, full, send, recv, rows, width):
        self.source, self.full, self.send, self.recv = source, full, send, recv
        self.rows, self.width = rows, width
        self.t, self.xn, self.yn, self.dg = neighbours()

    def direct(self, c, k):
        rows = block(c, self.rows)
        place = self.full.at[rows, block(self.t, self.width)]
        return pltpu.make_async_remote_copy(
            place if self.source is None else self.source.at[rows, :],
            place,
            self.send.at[k, c],
            self.recv.at[k, c],
            device_id={"tensor": self.xn if k == 0 else self.yn},
            device_id_type=MESH,
        )

    def relay(self, c, k):
        rows = block(2 * c + k, self.rows // 2)
        part = self.full.at[rows, block(self.xn if k == 0 else self.yn, self.width)]
        return pltpu.make_async_remote_copy(
            part,
            part,
            self.send.at[2 + k, c],
            self.recv.at[2 + k, c],
            device_id={"tensor": self.yn if k == 0 else self.xn},
            device_id_type=MESH,
        )

    def start(self, c):
        self.direct(c, 0).start()
        self.direct(c, 1).start()

    def forward(self, c):
        for k in range(2):
            self.direct(c, k).wait_recv()
            self.relay(c, k).start()

    def finish(self, c):
        self.relay(c, 0).wait_recv()
        self.relay(c, 1).wait_recv()

    def drain(self, c):
        for k in range(2):
            self.direct(c, k).wait_send()
            self.relay(c, k).wait_send()


LANES = 128


def scan_rows(decay, source, state, product, head):
    planes, rows, _ = decay.shape
    seg = rows // 8

    def first(j, held):
        out = []
        for q in range(planes):
            now, prod = held[q]
            d = decay[q, pl.ds(j, 8, stride=seg), :]
            now = d * now + source[q, pl.ds(j, 8, stride=seg), :]
            prod = d * prod
            state[q, pl.ds(head + j, 8, stride=seg), :] = now
            product[q, pl.ds(j, 8, stride=seg), :] = prod
            out.append((now, prod))
        return tuple(out)

    zero, one = jnp.zeros((8, LANES), F32), jnp.ones((8, LANES), F32)
    ends = lax.fori_loop(0, seg, first, ((zero, one),) * planes, unroll=4)
    entries = []
    for q in range(planes):
        last, prod = ends[q]
        carry = state[q, head - 1 : head, :]
        parts = []
        for s in range(8):
            parts.append(carry)
            carry = prod[s : s + 1] * carry + last[s : s + 1]
        entries.append(jnp.concatenate(parts, axis=0))

    def second(j, held):
        for q in range(planes):
            state[q, pl.ds(head + j, 8, stride=seg), :] += (
                product[q, pl.ds(j, 8, stride=seg), :] * entries[q]
            )
        return held

    lax.fori_loop(0, seg, second, 0, unroll=4)


def to_planes(ref, rows, value):
    for q in range(value.shape[1] // LANES):
        ref[q, rows, :] = value[:, q * LANES : (q + 1) * LANES]


def from_planes(ref, rows):
    return jnp.concatenate([ref[q, rows, :] for q in range(ref.shape[0])], axis=1)


def mixer_kernel(
    tok, wout, gains, w_in, w_for, w_gp, lower, gain_gate,
    normed, tok_full, wout_full, gains_full, scale_in, pre_in, pre_for, pre_gp, state, diff, mixed, squares,
    full, wfull, vin, vfor, vgp, gbuf, dec, src, prod, hbuf,
    send, recv, wsend, wrecv, xsend, xrecv, gsend, grecv, lsem, osem,
):
    s = pl.program_id(0)
    chunks = pl.num_programs(0) - 1
    rows, width = pre_in.shape
    feats = full.shape[1]
    t, xn, yn, dg = neighbours()
    me = lax.axis_index("dp")
    core = me % 2
    partner = {"dp": me + 1 - 2 * core}
    peers = ({"tensor": xn}, {"tensor": yn}, {"tensor": dg})
    gather = Gather(tok, full, send, recv, rows, width)
    planes = width // LANES
    half = width // 2
    piece = width // 4

    def w_direct(k, p):
        return pltpu.make_async_remote_copy(
            wout.at[block(2 * core + p, piece), :],
            wfull.at[block(4 * t + 2 * core + p, piece), :],
            wsend.at[k, p],
            wrecv.at[k, p],
            device_id=peers[k],
            device_id_type=MESH,
        )

    def w_relay(k):
        part = wfull.at[block(4 * (xn if k == 0 else yn) + 2 * core + k, piece), :]
        return pltpu.make_async_remote_copy(
            part, part, wsend.at[2, k], wrecv.at[2, k], device_id=peers[1 - k], device_id_type=MESH
        )

    def w_swap(k):
        part = wfull.at[block(2 * (xn, yn, dg)[k] + core, half), :]
        return pltpu.make_async_remote_copy(
            part, part, xsend.at[k], xrecv.at[k], device_id=partner, device_id_type=MESH
        )

    def gain_copy(k):
        return pltpu.make_async_remote_copy(
            gains, gbuf.at[t], gsend.at[k], grecv.at[k], device_id=peers[k], device_id_type=MESH
        )

    loads = (
        pltpu.make_async_copy(tok, full.at[:, block(t, width)], lsem.at[0]),
        pltpu.make_async_copy(wout, wfull.at[block(t, width), :], lsem.at[1]),
        pltpu.make_async_copy(w_in, vin, lsem.at[2]),
        pltpu.make_async_copy(w_for, vfor, lsem.at[3]),
        pltpu.make_async_copy(w_gp, vgp, lsem.at[4]),
        pltpu.make_async_copy(gains, gbuf.at[t], lsem.at[5]),
    )

    def tok_out(c):
        return pltpu.make_async_copy(
            full.at[block(c, rows), :], tok_full.at[block(c, rows), :], osem.at[c]
        )

    w_out = pltpu.make_async_copy(wfull, wout_full, lsem.at[6])

    @pl.when(s == 0)
    def _():
        for load in loads:
            load.start()
        greet(peers + (partner,))
        for k in range(3):
            gain_copy(k).start()
        for p in range(2):
            w_direct(0, p).start()
            w_direct(1, p).start()
        for c in range(AHEAD):
            gather.start(c)
        hbuf[:, 0:8, :] = jnp.zeros((planes, 8, LANES), F32)
        for p in range(2):
            w_direct(0, p).wait_recv()
            w_direct(1, p).wait_recv()
        w_relay(0).start()
        w_relay(1).start()
        w_swap(0).start()
        w_swap(1).start()
        for load in loads:
            load.wait()
        for k in range(3):
            gain_copy(k).wait_recv()
        for j in range(4):
            gains_full[:, j * width : (j + 1) * width] = gbuf[j]

    @pl.when(s == 2)
    def _():
        w_relay(0).wait_recv()
        w_relay(1).wait_recv()
        w_swap(2).start()

    @pl.when(s == chunks - 1)
    def _():
        for k in range(3):
            w_swap(k).wait_recv()
        w_out.start()

    @pl.when(s < chunks)
    def _():
        gather.forward(s)

        @pl.when(s + AHEAD < chunks)
        def _():
            gather.start(s + AHEAD)

    @pl.when(s >= 1)
    def _():
        c = s - 1
        gather.finish(c)
        tok_out(c).start()
        gain_in = gains_full[0:1, :]
        low = lower[...]
        gain = gain_gate[...]

        def norm_rows(i):
            x = full[block(c * (rows // 32) + i, 32), :].astype(F32)
            scale = lax.rsqrt(jnp.sum(x * x, axis=1, keepdims=True) / feats + EPSILON)
            here = block(i, 32)
            normed[here, :] = (x * scale * gain_in).astype(BF16)
            scale_in[here, :] = jnp.broadcast_to(scale, (32, 128))

        each(rows // 32, norm_rows)
        pre_in[...] = plain_dot(normed[...], vin[...])
        pre_for[...] = plain_dot(normed[...], vfor[...])
        pre_gp[...] = plain_dot(normed[...], vgp[...])

        def gate_rows(i):
            here = block(i, 32)
            decay = low + (1.0 - low) * jax.nn.sigmoid(pre_for[here, :])
            to_planes(dec, here, decay)
            to_planes(src, here, (1.0 - decay) * jax.nn.silu(pre_in[here, :]))

        each(rows // 32, gate_rows)
        scan_rows(dec, src, hbuf, prod, 8)
        diff[...] = from_planes(hbuf, slice(7, 7 + rows))

        def mix_rows(i):
            here = block(i, 32)
            h = from_planes(hbuf, pl.ds(pl.multiple_of(8 + i * 32, 8), 32))
            state[here, :] = h
            diff[here, :] -= jax.nn.silu(pre_in[here, :])
            mixed[here, :] = (h * gain * jax.nn.silu(pre_gp[here, :])).astype(BF16)

        each(rows // 32, mix_rows)
        h = state[...]
        squares[0] = rows_to_lanes(h * h)
        hbuf[:, 7:8, :] = hbuf[:, 7 + rows : 8 + rows, :]

    @pl.when(s == chunks)
    def _():
        each(chunks, gather.drain)
        each(chunks, lambda c: tok_out(c).wait())
        for k in range(3):
            gain_copy(k).wait_send()
            w_swap(k).wait_send()
        for p in range(2):
            w_direct(0, p).wait_send()
            w_direct(1, p).wait_send()
            w_relay(p).wait_send()
        w_out.wait()


def later(s):
    return (jnp.maximum(s - 1, 0), 0)


def mixer_forward(tok, wout, gains, w_in, w_for, w_gp, lower, gain_gate):
    total, width = tok.shape
    feats = w_in.shape[0]
    rows = total // CHUNKS

    def out(n, dtype):
        return jax.ShapeDtypeStruct((total, n), dtype), pl.BlockSpec((rows, n), later)

    outs = [
        out(feats, BF16),
        (jax.ShapeDtypeStruct((total, feats), BF16), ANY),
        (jax.ShapeDtypeStruct((feats, feats), BF16), ANY),
        (jax.ShapeDtypeStruct((8, feats), F32), WHOLE),
        out(128, F32),
        out(width, F32),
        out(width, F32),
        out(width, F32),
        out(width, F32),
        out(width, F32),
        out(width, BF16),
        (
            jax.ShapeDtypeStruct((CHUNKS, 8, rows), F32),
            pl.BlockSpec((1, 8, rows), lambda s: (jnp.maximum(s - 1, 0), 0, 0)),
        ),
    ]
    dma = pltpu.SemaphoreType.DMA
    return pl.pallas_call(
        mixer_kernel,
        grid=(CHUNKS + 1,),
        out_shape=[o[0] for o in outs],
        out_specs=[o[1] for o in outs],
        in_specs=[ANY, ANY, WHOLE, ANY, ANY, ANY, WHOLE, WHOLE],
        scratch_shapes=[
            pltpu.VMEM((total, feats), BF16),
            pltpu.VMEM((feats, feats), BF16),
            pltpu.VMEM((feats, width), BF16),
            pltpu.VMEM((feats, width), BF16),
            pltpu.VMEM((feats, width), BF16),
            pltpu.VMEM((4, 8, width), F32),
            pltpu.VMEM((width // LANES, rows, LANES), F32),
            pltpu.VMEM((width // LANES, rows, LANES), F32),
            pltpu.VMEM((width // LANES, rows, LANES), F32),
            pltpu.VMEM((width // LANES, rows + 8, LANES), F32),
            dma((4, CHUNKS)),
            dma((4, CHUNKS)),
            dma((3, 2)),
            dma((3, 2)),
            dma((3,)),
            dma((3,)),
            dma((3,)),
            dma((3,)),
            dma((7,)),
            dma((CHUNKS,)),
        ],
        compiler_params=pltpu.CompilerParams(
            collective_id=1, has_side_effects=True, vmem_limit_bytes=VMEM_BYTES
        ),
        name="mixer_forward",
    )(tok, wout, gains, w_in, w_for, w_gp, lower, gain_gate)


def ffn_kernel(
    lens, mixed, cot, squares, gains, tok_full, wout, w_gate, w_up, w_down,
    normed, hidden, g_gate, g_up, cot_out, mix_out, scale_gate, scale_mid, resid,
    mfull, cfull, vout, vgate, vup, vdown, sbuf, mo, gbuf, ubuf, hbuf,
    send, recv, csend, crecv, ssend, srecv, lsem,
):
    s = pl.program_id(0)
    chunks = pl.num_programs(0) - 1
    width = mixed.shape[1]
    rows, feats = normed.shape
    hid = hidden.shape[1]
    t, xn, yn, dg = neighbours()
    peers = ({"tensor": xn}, {"tensor": yn}, {"tensor": dg})
    gather = Gather(mixed, mfull, send, recv, rows, width)
    cgather = Gather(cot, cfull, csend, crecv, rows, width)

    def square_copy(k):
        return pltpu.make_async_remote_copy(
            squares, sbuf.at[t], ssend.at[k], srecv.at[k], device_id=peers[k], device_id_type=MESH
        )

    loads = (
        pltpu.make_async_copy(mixed, mfull.at[:, block(t, width)], lsem.at[0]),
        pltpu.make_async_copy(cot, cfull.at[:, block(t, width)], lsem.at[1]),
        pltpu.make_async_copy(squares, sbuf.at[t], lsem.at[2]),
        pltpu.make_async_copy(wout, vout, lsem.at[3]),
        pltpu.make_async_copy(w_gate, vgate, lsem.at[4]),
        pltpu.make_async_copy(w_up, vup, lsem.at[5]),
        pltpu.make_async_copy(w_down, vdown, lsem.at[6]),
    )

    @pl.when(s == 0)
    def _():
        greet(peers)
        for k in range(3):
            square_copy(k).start()
        for c in range(AHEAD):
            gather.start(c)
            cgather.start(c)
        for load in loads:
            load.start()
        for load in loads:
            load.wait()
        for k in range(3):
            square_copy(k).wait_recv()

    @pl.when(s < chunks)
    def _():
        gather.forward(s)
        cgather.forward(s)

        @pl.when(s + AHEAD < chunks)
        def _():
            gather.start(s + AHEAD)
            cgather.start(s + AHEAD)

    @pl.when(s >= 1)
    def _():
        c = s - 1
        gain_mid = gains[1:2, :]
        gather.finish(c)
        here = block(c, rows)
        each(
            feats // width,
            lambda b: mo.__setitem__(
                (slice(None), block(b, width)), plain_dot(mfull[here, :], vout[:, block(b, width)])
            ),
        )
        total = sbuf[0, c] + sbuf[1, c] + sbuf[2, c] + sbuf[3, c]
        scale = lax.rsqrt(lanes_to_rows(total) / feats + EPSILON)
        scale_gate[...] = jnp.broadcast_to(scale, (rows, 128))

        def norm_rows(i):
            part = block(i, 32)
            m = mo[part, :] * scale_gate[part, 0:1]
            mix_out[part, :] = m.astype(BF16)
            r = m + tok_full[part, :].astype(F32)
            mid = lax.rsqrt(jnp.sum(r * r, axis=1, keepdims=True) / feats + EPSILON)
            scale_mid[part, :] = jnp.broadcast_to(mid, (32, 128))
            normed[part, :] = (r * mid * gain_mid).astype(BF16)
            mo[part, :] = r

        each(rows // 32, norm_rows)
        resid[...] = mo[:, block(t, width)]
        gbuf[...] = plain_dot(normed[...], vgate[...])
        ubuf[...] = plain_dot(normed[...], vup[...])
        cgather.finish(c)
        length = lens[0]

        def mask_rows(i):
            part = block(i, 32)
            position = c * rows + i * 32 + lax.broadcasted_iota(jnp.int32, (32, feats), 0)
            value = cfull[block(c * (rows // 32) + i, 32), :]
            cot_out[part, :] = jnp.where(position < length, value.astype(F32), 0.0).astype(BF16)

        each(rows // 32, mask_rows)
        hbuf[...] = back_dot(cot_out[...], vdown[...])

        def ffn_rows(i):
            part = block(i, 16)
            g = gbuf[part, :]
            u = ubuf[part, :]
            back = hbuf[part, :]
            sigma = jax.nn.sigmoid(g)
            act = g * sigma
            hidden[part, :] = (act * u).astype(BF16)
            g_gate[part, :] = (back * u * (sigma * (1.0 + g * (1.0 - sigma)))).astype(BF16)
            g_up[part, :] = (back * act).astype(BF16)

        each(rows // 16, ffn_rows)

    @pl.when(s == chunks)
    def _():
        each(chunks, gather.drain)
        each(chunks, cgather.drain)
        for k in range(3):
            square_copy(k).wait_send()


def ffn_forward(lens, mixed, cot, squares, gains, tok_full, wout, w_gate, w_up, w_down):
    total, width = mixed.shape
    feats, hid = w_gate.shape
    rows = total // CHUNKS

    def out(n, dtype):
        return jax.ShapeDtypeStruct((total, n), dtype), pl.BlockSpec((rows, n), later)

    outs = [
        out(feats, BF16),
        out(hid, BF16),
        out(hid, BF16),
        out(hid, BF16),
        out(feats, BF16),
        out(feats, BF16),
        out(128, F32),
        out(128, F32),
        out(width, F32),
    ]
    dma = pltpu.SemaphoreType.DMA
    return pl.pallas_call(
        ffn_kernel,
        grid=(CHUNKS + 1,),
        out_shape=[o[0] for o in outs],
        out_specs=[o[1] for o in outs],
        in_specs=[
            pl.BlockSpec(memory_space=pltpu.SMEM),
            ANY, ANY, WHOLE, WHOLE,
            pl.BlockSpec((rows, feats), later),
            ANY, ANY, ANY, ANY,
        ],
        scratch_shapes=[
            pltpu.VMEM((total, feats), BF16),
            pltpu.VMEM((total, feats), BF16),
            pltpu.VMEM((feats, feats), BF16),
            pltpu.VMEM((feats, hid), BF16),
            pltpu.VMEM((feats, hid), BF16),
            pltpu.VMEM((hid, feats), BF16),
            pltpu.VMEM((4, CHUNKS, 8, rows), F32),
            pltpu.VMEM((rows, feats), F32),
            pltpu.VMEM((rows, hid), F32),
            pltpu.VMEM((rows, hid), F32),
            pltpu.VMEM((rows, hid), F32),
            dma((4, CHUNKS)),
            dma((4, CHUNKS)),
            dma((4, CHUNKS)),
            dma((4, CHUNKS)),
            dma((3,)),
            dma((3,)),
            dma((7,)),
        ],
        compiler_params=pltpu.CompilerParams(
            collective_id=2, has_side_effects=True, vmem_limit_bytes=VMEM_BYTES
        ),
        name="ffn_forward",
    )(lens, mixed, cot, squares, gains, tok_full, wout, w_gate, w_up, w_down)


class Scatter:
    def __init__(self, share, keep, out1, in1, out2, in2, sems):
        self.share, self.keep = share, keep
        self.out1, self.in1, self.out2, self.in2 = out1, in1, out2, in2
        self.send1, self.recv1, self.send2, self.recv2 = sems
        self.t, xn, yn, self.dg = neighbours()
        self.order = ((xn, yn), (yn, xn))
        self.slots = keep.shape[0]
        self.outs = out1.shape[0]
        self.half = keep.shape[3]
        self.count = self.half // 32

    def hop1(self, c, h):
        return pltpu.make_async_remote_copy(
            self.out1.at[c % self.outs, h],
            self.in1.at[c, h],
            self.send1.at[h, c],
            self.recv1.at[h, c],
            device_id={"tensor": self.order[h][0]},
            device_id_type=MESH,
        )

    def hop2(self, c, h):
        return pltpu.make_async_remote_copy(
            self.out2.at[c % self.outs, h],
            self.in2.at[c, h],
            self.send2.at[h, c],
            self.recv2.at[h, c],
            device_id={"tensor": self.order[h][1]},
            device_id_type=MESH,
        )

    def begin(self, c):
        slot, place = c % self.slots, c % self.outs

        @pl.when(c >= self.outs)
        def _():
            for h in range(2):
                self.hop1(c - self.outs, h).wait_send()

        for h in range(2):
            one, two = self.order[h]

            def move(i, h=h, one=one, two=two):
                here = block(i, 32)
                there = block(h * self.count + i, 32)
                self.out1[place, h, 0, here, :] = self.share[one, there, :].astype(BF16)
                self.out1[place, h, 1, here, :] = self.share[self.dg, there, :].astype(BF16)
                self.keep[slot, h, 0, here, :] = self.share[self.t, there, :]
                self.keep[slot, h, 1, here, :] = self.share[two, there, :]

            each(self.count, move)
        for h in range(2):
            self.hop1(c, h).start()

    def middle(self, c):
        slot, place = c % self.slots, c % self.outs

        @pl.when(c >= self.outs)
        def _():
            for h in range(2):
                self.hop2(c - self.outs, h).wait_send()

        for h in range(2):
            self.hop1(c, h).wait_recv()

            def add(i, h=h):
                here = block(i, 32)
                self.out2[place, h, here, :] = (
                    self.keep[slot, h, 1, here, :] + self.in1[c, h, 1, here, :].astype(F32)
                ).astype(BF16)
                self.keep[slot, h, 0, here, :] += self.in1[c, h, 0, here, :].astype(F32)

            each(self.count, add)
        for h in range(2):
            self.hop2(c, h).start()

    def end(self, c, use):
        slot = c % self.slots
        for h in range(2):
            self.hop2(c, h).wait_recv()

            def give(i, h=h):
                here = block(i, 32)
                use(
                    h * self.count + i,
                    self.keep[slot, h, 0, here, :] + self.in2[c, h, here, :].astype(F32),
                )

            each(self.count, give)

    def drain(self, chunks):
        for c in range(max(chunks - self.outs, 0), chunks):
            for h in range(2):
                self.hop1(c, h).wait_send()
                self.hop2(c, h).wait_send()

    @staticmethod
    def scratch(chunks, rows, width):
        dma = pltpu.SemaphoreType.DMA
        return [
            pltpu.VMEM((4, rows, width), F32),
            pltpu.VMEM((3, 2, 2, rows // 2, width), F32),
            pltpu.VMEM((3, 2, 2, rows // 2, width), BF16),
            pltpu.VMEM((chunks, 2, 2, rows // 2, width), BF16),
            pltpu.VMEM((3, 2, rows // 2, width), BF16),
            pltpu.VMEM((chunks, 2, rows // 2, width), BF16),
            dma((2, chunks)),
            dma((2, chunks)),
            dma((2, chunks)),
            dma((2, chunks)),
        ]


def scan_rows_back(decay, source, state, product, carry):
    planes, rows, _ = decay.shape
    seg = rows // 8

    def first(n, held):
        j = seg - 1 - n
        out = []
        for q in range(planes):
            now, prod = held[q]
            here = pl.ds(j, 8, stride=seg)
            d = decay[q, here, :]
            now = source[q, here, :] + now
            state[q, here, :] = now
            product[q, here, :] = prod
            out.append((d * now, d * prod))
        return tuple(out)

    zero, one = jnp.zeros((8, LANES), F32), jnp.ones((8, LANES), F32)
    ends = lax.fori_loop(0, seg, first, ((zero, one),) * planes, unroll=4)
    entries = []
    for q in range(planes):
        last, prod = ends[q]
        value = carry[q, 0:1, :]
        parts = []
        for s in range(7, -1, -1):
            parts.append(value)
            value = prod[s : s + 1] * value + last[s : s + 1]
        entries.append(jnp.concatenate(parts[::-1], axis=0))
        carry[q, 0:1, :] = value

    def second(j, held):
        for q in range(planes):
            here = pl.ds(j, 8, stride=seg)
            state[q, here, :] += product[q, here, :] * entries[q]
        return held

    lax.fori_loop(0, seg, second, 0, unroll=4)


def fold_rows(value):
    return value[0:8] + value[8:16] + value[16:24] + value[24:32]


STAGES = 4


def back_kernel(
    g_gate, g_up, w_gate, w_up, w_out, gains, gain_gate, lower,
    cot, mix, tok, scale_mid, scale_gate, pre_in, pre_for, pre_gp, state, diff,
    g_mix, g_resid, g_in, g_for, g_gp, mixed, inner, sum_mid, sum_gate, sum_low,
    vgate, vup, vout, full, line, dots, gm, dec, src, prod, adj, carry,
    share, keep, out1, in1, out2, in2, send1, recv1, send2, recv2, send, recv, lsem,
):
    s = pl.program_id(0)
    chunks = pl.num_programs(0) - STAGES
    rows, width = g_resid.shape
    feats = full.shape[1]
    t, xn, yn, dg = neighbours()
    peers = ({"tensor": xn}, {"tensor": yn})
    gather = Gather(None, full, send, recv, rows, width)
    scatter = Scatter(share, keep, out1, in1, out2, in2, (send1, recv1, send2, recv2))
    loads = (
        pltpu.make_async_copy(w_gate, vgate, lsem.at[0]),
        pltpu.make_async_copy(w_up, vup, lsem.at[1]),
        pltpu.make_async_copy(w_out, vout, lsem.at[2]),
    )

    def place(c):
        return chunks - 1 - c

    def at_stage(n, act):
        @pl.when((s >= n) & (s - n < chunks))
        def _():
            act(s - n)

    @pl.when(s == 0)
    def _():
        for load in loads:
            load.start()
        greet(peers)
        carry[...] = jnp.zeros(carry.shape, F32)
        sum_mid[...] = jnp.zeros(sum_mid.shape, F32)
        sum_gate[...] = jnp.zeros(sum_gate.shape, F32)
        sum_low[...] = jnp.zeros(sum_low.shape, F32)
        for load in loads:
            load.wait()

    at_stage(3, lambda c: gather.forward(place(c)))

    def summed(c):
        def use(i, value):
            full[block(place(c) * (rows // 32) + i, 32), block(t, width)] = value.astype(BF16)

        scatter.end(c, use)
        gather.start(place(c))

    at_stage(2, summed)
    at_stage(1, scatter.middle)

    def terms(c):
        def part(b):
            here = block(b, width)
            share[b] = back_dot(g_gate[...], vgate[here, :]) + back_dot(g_up[...], vup[here, :])

        each(feats // width, part)
        scatter.begin(c)

    at_stage(0, terms)

    def finish(c):
        p = place(c)
        gather.finish(p)
        gain_mid = gains[1:2, :]
        gain = gain_gate[...]
        low = lower[...]

        def resid_rows(i):
            here = block(i, 32)
            g = full[block(p * (rows // 32) + i, 32), :].astype(F32)
            m = mix[here, :].astype(F32)
            r = tok[here, :].astype(F32) + m
            mid = scale_mid[here, 0:1]
            weighted = g * gain_mid
            total = jnp.sum(weighted * r, axis=1, keepdims=True) / feats
            grad = cot[here, :].astype(F32) + mid * weighted - r * (mid * mid * mid * total)
            low_grad = grad.astype(BF16)
            g_mix[here, :] = low_grad
            line[...] = grad
            g_resid[here, :] = line[:, block(t, width)]
            dots[here, :] = jnp.broadcast_to(
                jnp.sum(low_grad.astype(F32) * m, axis=1, keepdims=True), (32, 128)
            )
            sum_mid[...] += fold_rows(g * r * mid)

        each(rows // 32, resid_rows)
        gm[...] = back_dot(g_mix[...], vout[...])

        def state_rows(i):
            here = block(i, 32)
            h = state[here, :]
            scale = scale_gate[here, 0:1]
            ns = h * scale
            gp = pre_gp[here, :]
            sigma = jax.nn.sigmoid(gp)
            swish = gp * sigma
            grad = gm[here, :]
            sum_gate[...] += fold_rows(grad * ns * swish)
            g_gp[here, :] = (grad * ns * gain * (sigma * (1.0 + gp * (1.0 - sigma)))).astype(BF16)
            mixed[here, :] = (ns * gain * swish).astype(BF16)
            factor = scale * scale * dots[here, 0:1] / feats
            to_planes(src, here, scale * (grad * gain * swish) - h * factor)
            to_planes(dec, here, low + (1.0 - low) * jax.nn.sigmoid(pre_for[here, :]))

        each(rows // 32, state_rows)
        scan_rows_back(dec, src, adj, prod, carry)

        def gate_rows(i):
            here = block(i, 32)
            a = from_planes(adj, here)
            x, f = pre_in[here, :], pre_for[here, :]
            sig = jax.nn.sigmoid(f)
            decay = low + (1.0 - low) * sig
            grad_decay = a * diff[here, :]
            gi = (a * (1.0 - decay) * silu_slope(x)).astype(BF16)
            gf = (grad_decay * (1.0 - low) * sig * (1.0 - sig)).astype(BF16)
            g_in[here, :] = gi
            g_for[here, :] = gf
            sum_low[...] += fold_rows(grad_decay * (1.0 - sig))
            gm[here, :] = (
                gi.astype(F32) * x + gf.astype(F32) * f + g_gp[here, :].astype(F32) * pre_gp[here, :]
            )

        each(rows // 32, gate_rows)
        inner[0] = rows_to_lanes(gm[...])

    at_stage(STAGES, finish)

    @pl.when(s == pl.num_programs(0) - 1)
    def _():
        each(chunks, gather.drain)
        scatter.drain(CHUNKS)


def backward(
    g_gate, g_up, w_gate, w_up, w_out, gains, gain_gate, lower,
    cot, mix, tok, scale_mid, scale_gate, pre_in, pre_for, pre_gp, state, diff,
):
    total, hid = g_gate.shape
    feats, width = mix.shape[1], pre_in.shape[1]
    rows = total // CHUNKS

    def early(s):
        return (CHUNKS - 1 - jnp.minimum(s, CHUNKS - 1), 0)

    def late(s):
        return (CHUNKS - 1 - jnp.maximum(s - STAGES, 0), 0)

    def out(n, dtype):
        return jax.ShapeDtypeStruct((total, n), dtype), pl.BlockSpec((rows, n), late)

    def small(n):
        return jax.ShapeDtypeStruct((8, n), F32), pl.BlockSpec((8, n), lambda s: (0, 0))

    outs = [
        out(feats, BF16),
        out(width, F32),
        out(width, BF16),
        out(width, BF16),
        out(width, BF16),
        out(width, BF16),
        (
            jax.ShapeDtypeStruct((CHUNKS, 8, rows), F32),
            pl.BlockSpec((1, 8, rows), lambda s: late(s) + (0,)),
        ),
        small(feats),
        small(width),
        small(width),
    ]
    planes = width // LANES
    dma = pltpu.SemaphoreType.DMA
    return pl.pallas_call(
        back_kernel,
        grid=(CHUNKS + STAGES,),
        out_shape=[o[0] for o in outs],
        out_specs=[o[1] for o in outs],
        in_specs=[
            pl.BlockSpec((rows, hid), early),
            pl.BlockSpec((rows, hid), early),
            ANY, ANY, ANY, WHOLE, WHOLE, WHOLE,
            pl.BlockSpec((rows, feats), late),
            pl.BlockSpec((rows, feats), late),
            pl.BlockSpec((rows, feats), late),
            pl.BlockSpec((rows, 128), late),
            pl.BlockSpec((rows, 128), late),
        ]
        + [pl.BlockSpec((rows, width), late)] * 5,
        scratch_shapes=[
            pltpu.VMEM((feats, hid), BF16),
            pltpu.VMEM((feats, hid), BF16),
            pltpu.VMEM((width, feats), BF16),
            pltpu.VMEM((total, feats), BF16),
            pltpu.VMEM((32, feats), F32),
            pltpu.VMEM((rows, 128), F32),
            pltpu.VMEM((rows, width), F32),
            pltpu.VMEM((planes, rows, LANES), F32),
            pltpu.VMEM((planes, rows, LANES), F32),
            pltpu.VMEM((planes, rows, LANES), F32),
            pltpu.VMEM((planes, rows, LANES), F32),
            pltpu.VMEM((planes, 8, LANES), F32),
        ]
        + Scatter.scratch(CHUNKS, rows, width)
        + [dma((4, CHUNKS)), dma((4, CHUNKS)), dma((3,))],
        compiler_params=pltpu.CompilerParams(
            collective_id=3, has_side_effects=True, vmem_limit_bytes=VMEM_BYTES
        ),
        name="backward",
    )(
        g_gate, g_up, w_gate, w_up, w_out, gains, gain_gate, lower,
        cot, mix, tok, scale_mid, scale_gate, pre_in, pre_for, pre_gp, state, diff,
    )


def last_kernel(
    g_in, g_for, g_gp, w_in, w_for, w_gp, hidden, w_down, inner, gain_in,
    tok, scale_in, g_resid, resid,
    out, g_tok, sum_in,
    vin, vfor, vgp, vdown, ibuf, col,
    share, keep, out1, in1, out2, in2, send1, recv1, send2, recv2,
    fshare, fkeep, fout1, fin1, fout2, fin2, fsend1, frecv1, fsend2, frecv2,
    isend, irecv, lsem,
):
    s = pl.program_id(0)
    chunks = pl.num_programs(0) - 2
    rows, width = out.shape
    feats = w_down.shape[1]
    t, xn, yn, dg = neighbours()
    peers = ({"tensor": xn}, {"tensor": yn}, {"tensor": dg})
    scatter = Scatter(share, keep, out1, in1, out2, in2, (send1, recv1, send2, recv2))
    fscatter = Scatter(fshare, fkeep, fout1, fin1, fout2, fin2, (fsend1, frecv1, fsend2, frecv2))

    def inner_copy(k):
        return pltpu.make_async_remote_copy(
            inner, ibuf.at[t], isend.at[k], irecv.at[k], device_id=peers[k], device_id_type=MESH
        )

    loads = (
        pltpu.make_async_copy(w_in, vin, lsem.at[0]),
        pltpu.make_async_copy(w_for, vfor, lsem.at[1]),
        pltpu.make_async_copy(w_gp, vgp, lsem.at[2]),
        pltpu.make_async_copy(w_down, vdown, lsem.at[3]),
        pltpu.make_async_copy(inner, ibuf.at[t], lsem.at[4]),
    )

    def at_stage(n, act):
        @pl.when((s >= n) & (s - n < chunks))
        def _():
            act(s - n)

    @pl.when(s == 0)
    def _():
        for load in loads:
            load.start()
        greet(peers)
        for k in range(3):
            inner_copy(k).start()
        sum_in[...] = jnp.zeros(sum_in.shape, F32)
        for load in loads:
            load.wait()

    @pl.when(s == 2)
    def _():
        for k in range(3):
            inner_copy(k).wait_recv()

    def finish(c):
        total = ibuf[0, c] + ibuf[1, c] + ibuf[2, c] + ibuf[3, c]
        col[...] = jnp.broadcast_to(lanes_to_rows(total) / feats, (rows, 128))
        gain = gain_in[...]

        def give(i, value):
            here = block(i, 32)
            x = tok[here, :].astype(F32)
            scale = scale_in[here, 0:1]
            g_tok[here, :] = (
                g_resid[here, :] + scale * (value * gain) - x * (scale * scale * col[here, 0:1])
            )
            sum_in[...] += fold_rows(value * x * scale)

        scatter.end(c, give)

        def give_out(i, value):
            here = block(i, 32)
            out[here, :] = (resid[here, :] + value).astype(BF16)

        fscatter.end(c, give_out)

    at_stage(2, finish)

    def middle(c):
        scatter.middle(c)
        fscatter.middle(c)

    at_stage(1, middle)

    def terms(c):
        def part(b):
            here = block(b, width)
            share[b] = (
                back_dot(g_in[...], vin[here, :])
                + back_dot(g_for[...], vfor[here, :])
                + back_dot(g_gp[...], vgp[here, :])
            )

        each(feats // width, part)
        scatter.begin(c)

        def fpart(b):
            fshare[b] = plain_dot(hidden[...], vdown[:, block(b, width)])

        each(feats // width, fpart)
        fscatter.begin(c)

    at_stage(0, terms)

    @pl.when(s == pl.num_programs(0) - 1)
    def _():
        scatter.drain(CHUNKS)
        fscatter.drain(CHUNKS)
        for k in range(3):
            inner_copy(k).wait_send()


def last_sums(
    g_in, g_for, g_gp, w_in, w_for, w_gp, hidden, w_down, inner, gain_in, tok, scale_in, g_resid, resid
):
    total, hid = hidden.shape
    feats, width = w_in.shape
    rows = total // CHUNKS

    def early(s):
        return (jnp.minimum(s, CHUNKS - 1), 0)

    def late(s):
        return (jnp.maximum(s - 2, 0), 0)

    near = pl.BlockSpec((rows, width), early)
    far = pl.BlockSpec((rows, width), late)
    dma = pltpu.SemaphoreType.DMA
    return pl.pallas_call(
        last_kernel,
        grid=(CHUNKS + 2,),
        out_shape=[
            jax.ShapeDtypeStruct((total, width), BF16),
            jax.ShapeDtypeStruct((total, width), F32),
            jax.ShapeDtypeStruct((8, width), F32),
        ],
        out_specs=[far, far, pl.BlockSpec((8, width), lambda s: (0, 0))],
        in_specs=[
            near, near, near, ANY, ANY, ANY,
            pl.BlockSpec((rows, hid), early),
            ANY, WHOLE, WHOLE, far,
            pl.BlockSpec((rows, 128), late),
            far, far,
        ],
        scratch_shapes=[
            pltpu.VMEM((feats, width), BF16),
            pltpu.VMEM((feats, width), BF16),
            pltpu.VMEM((feats, width), BF16),
            pltpu.VMEM((hid, feats), BF16),
            pltpu.VMEM((4, CHUNKS, 8, rows), F32),
            pltpu.VMEM((rows, 128), F32),
        ]
        + Scatter.scratch(CHUNKS, rows, width)
        + Scatter.scratch(CHUNKS, rows, width)
        + [dma((3,)), dma((3,)), dma((5,))],
        compiler_params=pltpu.CompilerParams(
            collective_id=4, has_side_effects=True, vmem_limit_bytes=VMEM_BYTES
        ),
        name="last_sums",
    )(g_in, g_for, g_gp, w_in, w_for, w_gp, hidden, w_down, inner, gain_in, tok, scale_in, g_resid, resid)


def sum_over_data(grads):
    return tuple(lax.psum(g, "dp") for g in grads)


def on_device(
    tokens, lengths, cotangent, w_norm_in, w_input, w_forget, w_gproj, lower_bound, w_gate_norm,
    w_output, w_norm_mid, w_gate, w_up, w_down,
):
    channels = w_input.shape[1]
    gain_in = w_norm_in.astype(F32)[None]
    gains = jnp.concatenate([gain_in, w_norm_mid.astype(F32)[None], jnp.zeros((6, channels), F32)], 0)
    lower = lower_bound.astype(F32)[None]
    gain_gate = w_gate_norm.astype(F32)[None]
    (
        normed_in, tok_full, wout_full, gains_full, scale_in, pre_in, pre_for, pre_gp, state, diff, raw, squares,
    ) = mixer_forward(tokens, w_output, gains, w_input, w_forget, w_gproj, lower, gain_gate)
    normed_mid, hidden, g_gate, g_up, cot, mix, scale_gate, scale_mid, resid = ffn_forward(
        lengths, raw, cotangent, squares, gains_full, tok_full, wout_full, w_gate, w_up, w_down
    )
    ffn_grads = tuple(
        trans_dot(a, b).astype(BF16) for a, b in ((normed_mid, g_gate), (normed_mid, g_up), (hidden, cot))
    )
    ffn_grads, g_gate = lax.optimization_barrier((ffn_grads, g_gate))
    ffn_sums = sum_over_data(ffn_grads)
    g_mix, g_resid, g_in, g_for, g_gp, mixed, inner, sum_mid, sum_gate, sum_low = backward(
        g_gate, g_up, w_gate, w_up, w_output, gains_full, gain_gate, lower,
        cot, mix, tok_full, scale_mid, scale_gate, pre_in, pre_for, pre_gp, state, diff,
    )
    mixer_grads = tuple(
        trans_dot(a, b).astype(BF16)
        for a, b in ((normed_in, g_in), (normed_in, g_for), (normed_in, g_gp), (mixed, g_mix))
    )
    mixer_grads, g_in = lax.optimization_barrier((mixer_grads, g_in))
    output, g_tok, sum_in = last_sums(
        g_in, g_for, g_gp, w_input, w_forget, w_gproj, hidden, w_down, inner, gain_in,
        tokens, scale_in, g_resid, resid,
    )
    mixer_grads, ffn_sums = lax.optimization_barrier((mixer_grads, ffn_sums))
    mixer_sums = sum_over_data(mixer_grads)
    t = lax.axis_index("tensor")
    own_mid = lax.dynamic_slice_in_dim(sum_mid, t * channels, channels, 1)
    small = lax.psum(jnp.stack([jnp.sum(a, axis=0) for a in (sum_in, sum_low, sum_gate, own_mid)]), "dp")
    m = [g.astype(F32) for g in mixer_sums]
    f = [g.astype(F32) for g in ffn_sums]
    return (output, g_tok, small[0], m[0], m[1], m[2], small[1], small[2], m[3], small[3], f[0], f[1], f[2])


def solution(mesh):
    rows, cols, vec = P(None, "tensor"), P("tensor", None), P("tensor")
    both = P("dp", "tensor")
    in_specs = (both, P("dp"), both, vec, rows, rows, rows, vec, vec, cols, vec, rows, rows, cols)
    out_specs = (both, both, vec, rows, rows, rows, vec, vec, cols, vec, rows, rows, cols)
    return jax.shard_map(on_device, mesh=mesh, in_specs=in_specs, out_specs=out_specs, check_vma=False)
```

```python
import functools

import jax
import jax.numpy as jnp
from jax import lax
from jax.experimental import pallas as pl
from jax.experimental.pallas import tpu as pltpu
from jax.sharding import PartitionSpec as P

EPSILON = 1e-06
MESH = pl.DeviceIdType.MESH
CHUNKS = 8
AHEAD = 2
VMEM_BYTES = 67_000_000
F32 = jnp.float32
BF16 = jnp.bfloat16
ANY = pl.BlockSpec(memory_space=pl.ANY)
WHOLE = pl.BlockSpec(memory_space=pltpu.VMEM)


def silu_slope(value):
    sigma = jax.nn.sigmoid(value)
    return sigma * (1.0 + value * (1.0 - sigma))


def plain_dot(left, right):
    return jnp.dot(left, right, preferred_element_type=F32)


def trans_dot(left, right):
    return lax.dot_general(left, right, (((0,), (0,)), ((), ())), preferred_element_type=F32)


def back_dot(left, right):
    return lax.dot_general(left, right, (((1,), (1,)), ((), ())), preferred_element_type=F32)


def rows_to_lanes(values):
    ones = jnp.ones((8, values.shape[1]), F32)
    return lax.dot_general(
        ones, values, (((1,), (1,)), ((), ())), precision=lax.Precision.HIGHEST,
        preferred_element_type=F32,
    )


def lanes_to_rows(values):
    ones = jnp.full((8, 128), 0.125, F32)
    wide = lax.dot_general(
        values, ones, (((0,), (0,)), ((), ())), precision=lax.Precision.HIGHEST,
        preferred_element_type=F32,
    )
    return wide[:, :1]


def neighbours():
    t = lax.axis_index("tensor")
    return t, t + 1 - 2 * (t % 2), t + 2 - 4 * (t // 2), 3 - t


def block(start, size):
    return pl.ds(pl.multiple_of(start * size, size), size)


def greet(devices):
    barrier = pltpu.get_barrier_semaphore()
    for device in devices:
        pl.semaphore_signal(barrier, inc=1, device_id=device, device_id_type=MESH)
    pl.semaphore_wait(barrier, len(devices))


def each(count, step):
    def body(i, carry):
        step(i)
        return carry

    lax.fori_loop(0, count, body, 0)


class Gather:
    def __init__(self, source, full, send, recv, rows, width):
        self.source, self.full, self.send, self.recv = source, full, send, recv
        self.rows, self.width = rows, width
        self.t, self.xn, self.yn, self.dg = neighbours()

    def direct(self, c, k):
        rows = block(c, self.rows)
        place = self.full.at[rows, block(self.t, self.width)]
        return pltpu.make_async_remote_copy(
            place if self.source is None else self.source.at[rows, :],
            place,
            self.send.at[k, c],
            self.recv.at[k, c],
            device_id={"tensor": self.xn if k == 0 else self.yn},
            device_id_type=MESH,
        )

    def relay(self, c, k):
        rows = block(2 * c + k, self.rows // 2)
        part = self.full.at[rows, block(self.xn if k == 0 else self.yn, self.width)]
        return pltpu.make_async_remote_copy(
            part,
            part,
            self.send.at[2 + k, c],
            self.recv.at[2 + k, c],
            device_id={"tensor": self.yn if k == 0 else self.xn},
            device_id_type=MESH,
        )

    def start(self, c):
        self.direct(c, 0).start()
        self.direct(c, 1).start()

    def forward(self, c):
        for k in range(2):
            self.direct(c, k).wait_recv()
            self.relay(c, k).start()

    def finish(self, c):
        self.relay(c, 0).wait_recv()
        self.relay(c, 1).wait_recv()

    def drain(self, c):
        for k in range(2):
            self.direct(c, k).wait_send()
            self.relay(c, k).wait_send()


LANES = 128


def scan_rows(decay, source, state, product, head):
    planes, rows, _ = decay.shape
    seg = rows // 8

    def first(j, held):
        out = []
        for q in range(planes):
            now, prod = held[q]
            d = decay[q, pl.ds(j, 8, stride=seg), :]
            now = d * now + source[q, pl.ds(j, 8, stride=seg), :]
            prod = d * prod
            state[q, pl.ds(head + j, 8, stride=seg), :] = now
            product[q, pl.ds(j, 8, stride=seg), :] = prod
            out.append((now, prod))
        return tuple(out)

    zero, one = jnp.zeros((8, LANES), F32), jnp.ones((8, LANES), F32)
    ends = lax.fori_loop(0, seg, first, ((zero, one),) * planes, unroll=4)
    entries = []
    for q in range(planes):
        last, prod = ends[q]
        carry = state[q, head - 1 : head, :]
        parts = []
        for s in range(8):
            parts.append(carry)
            carry = prod[s : s + 1] * carry + last[s : s + 1]
        entries.append(jnp.concatenate(parts, axis=0))

    def second(j, held):
        for q in range(planes):
            state[q, pl.ds(head + j, 8, stride=seg), :] += (
                product[q, pl.ds(j, 8, stride=seg), :] * entries[q]
            )
        return held

    lax.fori_loop(0, seg, second, 0, unroll=4)


def to_planes(ref, rows, value):
    for q in range(value.shape[1] // LANES):
        ref[q, rows, :] = value[:, q * LANES : (q + 1) * LANES]


def from_planes(ref, rows):
    return jnp.concatenate([ref[q, rows, :] for q in range(ref.shape[0])], axis=1)


UNIT = 32
LAG = 2


class Chain:
    def __init__(self, grads, spans, sums, lows, highs, peers, buf, sems, count):
        self.grads, self.spans, self.sums, self.peers, self.buf = grads, spans, sums, peers, buf
        self.parts = (lows, highs)
        (
            self.peer_send, self.peer_recv, self.part_send, self.low_recv, self.high_recv,
            self.low_send, self.up_send, self.fin_recv, self.twin_send, self.twin_recv, self.load_sem, self.put_sem,
        ) = sems
        me = lax.axis_index("dp")
        self.core = me % 2
        self.z = me // 2
        self.chips = count // 2
        self.left = {"dp": (me + count - 2) % count}
        self.right = {"dp": (me + 2) % count}
        self.twin = {"dp": me + 1 - 2 * self.core}
        self.first = []
        start = 0
        for _, n in spans:
            self.first.append(start)
            start += n
        self.units = start
        self.far = self.chips // 2
        self.ticks = 2 * ((self.units - 1) // 2 + 2 * LAG * self.far + 4)

    def near(self):
        return [self.left, self.right, self.twin]

    def rows(self, i, u, core):
        per_core = self.grads[i].shape[0] // (2 * UNIT)
        return block(core * per_core + self.spans[i][0] + u - self.first[i], UNIT)

    def inside(self, i, u):
        return (u >= self.first[i]) & (u < self.first[i] + self.spans[i][1])

    def slot(self, i, u, k):
        return self.buf.at[u % 4, k, :, 0 : self.grads[i].shape[1]]

    def swap(self, i, u, core):
        rows = self.rows(i, u, core)
        return pltpu.make_async_remote_copy(
            self.grads[i].at[rows, :], self.peers[i].at[rows, :], self.peer_send.at[u], self.peer_recv.at[u],
            device_id=self.twin, device_id_type=MESH,
        )

    def partial(self, i, u, way):
        rows = self.rows(i, u, self.core)
        return pltpu.make_async_remote_copy(
            self.slot(i, u, 4), self.parts[way][i].at[rows, :], self.part_send.at[u],
            (self.low_recv, self.high_recv)[way].at[u],
            device_id=(self.right, self.left)[way], device_id_type=MESH,
        )

    def final(self, i, u, way, staged):
        rows = self.rows(i, u, self.core)
        place = self.sums[i].at[rows, :]
        return pltpu.make_async_remote_copy(
            self.slot(i, u, 4) if staged else place, place,
            (self.up_send, self.low_send)[way].at[u], self.fin_recv.at[u],
            device_id=(self.right, self.left)[way], device_id_type=MESH,
        )

    def share(self, i, u, staged):
        rows = self.rows(i, u, self.core)
        place = self.sums[i].at[rows, :]
        return pltpu.make_async_remote_copy(
            self.slot(i, u, 4) if staged else place, place, self.twin_send.at[u], self.twin_recv.at[u],
            device_id=self.twin, device_id_type=MESH,
        )

    def load(self, i, u, k):
        rows = self.rows(i, u, self.core)
        refs = (self.grads[i], self.peers[i], self.parts[0][i], self.parts[1][i])
        return pltpu.make_async_copy(refs[k].at[rows, :], self.slot(i, u, k), self.load_sem.at[u % 4, k])

    def put(self, i, u):
        return pltpu.make_async_copy(
            self.slot(i, u, 4), self.sums[i].at[self.rows(i, u, self.core), :], self.put_sem.at[u % 4]
        )

    def over(self, act):
        for i, (_, n) in enumerate(self.spans):
            each(n, lambda j, i=i: act(i, self.first[i] + j))

    def begin(self):
        self.over(lambda i, u: self.swap(i, u, 1 - self.core).start())

    def owner(self, u):
        return self.chips // 2 - 1 + u % 2

    def from_low(self, u):
        return (self.z > 0) & (self.z <= self.owner(u))

    def from_high(self, u):
        return (self.z < self.chips - 1) & (self.z >= self.owner(u))

    def fetch(self, i, u):
        self.load(i, u, 0).start()
        self.swap(i, u, self.core).wait_recv()
        self.load(i, u, 1).start()

        @pl.when(self.from_low(u))
        def _():
            self.partial(i, u, 0).wait_recv()
            self.load(i, u, 2).start()

        @pl.when(self.from_high(u))
        def _():
            self.partial(i, u, 1).wait_recv()
            self.load(i, u, 3).start()

    def settle(self, i, u):
        o = self.owner(u)

        @pl.when(self.z != o)
        def _():
            self.partial(i, u, 0).wait_send()

        @pl.when(self.z == o)
        def _():
            @pl.when(self.z < self.chips - 1)
            def _():
                self.final(i, u, 0, True).wait_send()

            @pl.when(self.z > 0)
            def _():
                self.final(i, u, 1, True).wait_send()

            self.share(i, u, True).wait_send()
            self.put(i, u).wait()

    def reduce(self, i, u):
        o = self.owner(u)
        self.load(i, u, 0).wait()
        self.load(i, u, 1).wait()
        width = self.grads[i].shape[1]
        here = u % 4

        def value(k, r):
            return self.buf[here, k, r, 0:width].astype(F32)

        def total(ks):
            def add(j):
                r = block(j, 16)
                self.buf[here, 4, r, 0:width] = sum(value(k, r) for k in ks).astype(BF16)

            each(UNIT // 16, add)

        low, high = self.from_low(u), self.from_high(u)

        @pl.when(low)
        def _():
            self.load(i, u, 2).wait()

        @pl.when(high)
        def _():
            self.load(i, u, 3).wait()

        @pl.when(low & high)
        def _():
            total((0, 1, 2, 3))

        @pl.when(low & (self.z < o))
        def _():
            total((0, 1, 2))

        @pl.when(high & (self.z > o))
        def _():
            total((0, 1, 3))

        @pl.when((self.z == 0) & (self.z < o))
        def _():
            total((0, 1))

        @pl.when((self.z == self.chips - 1) & (self.z > o))
        def _():
            total((0, 1))

        @pl.when((self.z == o) & (self.z == 0))
        def _():
            total((0, 1, 3))

        @pl.when((self.z == o) & (self.z == self.chips - 1) & (self.z > 0))
        def _():
            total((0, 1, 2))

        @pl.when(self.z < o)
        def _():
            self.partial(i, u, 0).start()

        @pl.when(self.z > o)
        def _():
            self.partial(i, u, 1).start()

        @pl.when(self.z == o)
        def _():
            @pl.when(self.z < self.chips - 1)
            def _():
                self.final(i, u, 0, True).start()

            @pl.when(self.z > 0)
            def _():
                self.final(i, u, 1, True).start()

            self.share(i, u, True).start()
            self.put(i, u).start()

    def pass_on(self, i, u):
        o = self.owner(u)
        self.final(i, u, 0, False).wait_recv()

        @pl.when((self.z < o) & (self.z > 0))
        def _():
            self.final(i, u, 1, False).start()

        @pl.when((self.z > o) & (self.z < self.chips - 1))
        def _():
            self.final(i, u, 0, False).start()

        self.share(i, u, False).start()

    def tick(self, tau):
        stream = tau % 2
        k = tau // 2 - 1
        away = jnp.abs(self.z - self.owner(stream))
        now = 2 * (k - LAG * (self.far - away)) + stream
        back = 2 * (k - LAG * (self.far + away)) + stream

        def pick(u, act, also=True):
            for i in range(len(self.grads)):

                @pl.when(self.inside(i, u) & also)
                def _(i=i):
                    act(i, u)

        pick(now - 4, self.settle)
        pick(now, self.reduce)
        pick(back, self.pass_on, away > 0)
        pick(now + 2, self.fetch)

    def close(self, tau):
        each(self.ticks - tau, lambda j: self.tick(tau + j))

        def done(i, u):
            o = self.owner(u)
            self.swap(i, u, 1 - self.core).wait_send()

            @pl.when(self.z != o)
            def _():
                self.share(i, u, False).wait_send()

            @pl.when((self.z < o) & (self.z > 0))
            def _():
                self.final(i, u, 1, False).wait_send()

            @pl.when((self.z > o) & (self.z < self.chips - 1))
            def _():
                self.final(i, u, 0, False).wait_send()

            rows = self.rows(i, u, 1 - self.core)
            place = self.sums[i].at[rows, :]
            pltpu.make_async_remote_copy(
                place, place, self.twin_send.at[u], self.twin_recv.at[u],
                device_id=self.twin, device_id_type=MESH,
            ).wait_recv()

        self.over(done)

    @staticmethod
    def scratch(arrays, spans):
        units = sum(n for _, n in spans)
        dma = pltpu.SemaphoreType.DMA
        return [pltpu.VMEM((4, 5, UNIT, max(a.shape[1] for a in arrays)), BF16)] + [dma((units,))] * 10 + [
            dma((4, 4)),
            dma((4,)),
        ]


def mixer_kernel(
    tok, wout, gains, w_in, w_for, w_gp, lower, gain_gate,
    normed, tok_full, wout_full, gains_full, scale_in, pre_in, pre_for, pre_gp, state, diff, mixed, squares,
    full, wfull, vin, vfor, vgp, gbuf, dec, src, prod, hbuf,
    send, recv, wsend, wrecv, xsend, xrecv, gsend, grecv, lsem, osem,
):
    s = pl.program_id(0)
    chunks = pl.num_programs(0) - 1
    rows, width = pre_in.shape
    feats = full.shape[1]
    t, xn, yn, dg = neighbours()
    me = lax.axis_index("dp")
    core = me % 2
    partner = {"dp": me + 1 - 2 * core}
    peers = ({"tensor": xn}, {"tensor": yn}, {"tensor": dg})
    gather = Gather(tok, full, send, recv, rows, width)
    planes = width // LANES
    half = width // 2
    piece = width // 4

    def w_direct(k, p):
        return pltpu.make_async_remote_copy(
            wout.at[block(2 * core + p, piece), :],
            wfull.at[block(4 * t + 2 * core + p, piece), :],
            wsend.at[k, p],
            wrecv.at[k, p],
            device_id=peers[k],
            device_id_type=MESH,
        )

    def w_relay(k):
        part = wfull.at[block(4 * (xn if k == 0 else yn) + 2 * core + k, piece), :]
        return pltpu.make_async_remote_copy(
            part, part, wsend.at[2, k], wrecv.at[2, k], device_id=peers[1 - k], device_id_type=MESH
        )

    def w_swap(k):
        part = wfull.at[block(2 * (xn, yn, dg)[k] + core, half), :]
        return pltpu.make_async_remote_copy(
            part, part, xsend.at[k], xrecv.at[k], device_id=partner, device_id_type=MESH
        )

    def gain_copy(k):
        return pltpu.make_async_remote_copy(
            gains, gbuf.at[t], gsend.at[k], grecv.at[k], device_id=peers[k], device_id_type=MESH
        )

    loads = (
        pltpu.make_async_copy(tok, full.at[:, block(t, width)], lsem.at[0]),
        pltpu.make_async_copy(wout, wfull.at[block(t, width), :], lsem.at[1]),
        pltpu.make_async_copy(w_in, vin, lsem.at[2]),
        pltpu.make_async_copy(w_for, vfor, lsem.at[3]),
        pltpu.make_async_copy(w_gp, vgp, lsem.at[4]),
        pltpu.make_async_copy(gains, gbuf.at[t], lsem.at[5]),
    )

    def tok_out(c):
        return pltpu.make_async_copy(
            full.at[block(c, rows), :], tok_full.at[block(c, rows), :], osem.at[c]
        )

    w_out = pltpu.make_async_copy(wfull, wout_full, lsem.at[6])

    @pl.when(s == 0)
    def _():
        for load in loads:
            load.start()
        greet(peers + (partner,))
        for k in range(3):
            gain_copy(k).start()
        for p in range(2):
            w_direct(0, p).start()
            w_direct(1, p).start()
        for c in range(AHEAD):
            gather.start(c)
        hbuf[:, 0:8, :] = jnp.zeros((planes, 8, LANES), F32)
        for p in range(2):
            w_direct(0, p).wait_recv()
            w_direct(1, p).wait_recv()
        w_relay(0).start()
        w_relay(1).start()
        w_swap(0).start()
        w_swap(1).start()
        for load in loads:
            load.wait()
        for k in range(3):
            gain_copy(k).wait_recv()
        for j in range(4):
            gains_full[:, j * width : (j + 1) * width] = gbuf[j]

    @pl.when(s == 2)
    def _():
        w_relay(0).wait_recv()
        w_relay(1).wait_recv()
        w_swap(2).start()

    @pl.when(s == chunks - 1)
    def _():
        for k in range(3):
            w_swap(k).wait_recv()
        w_out.start()

    @pl.when(s < chunks)
    def _():
        gather.forward(s)

        @pl.when(s + AHEAD < chunks)
        def _():
            gather.start(s + AHEAD)

    @pl.when(s >= 1)
    def _():
        c = s - 1
        gather.finish(c)
        tok_out(c).start()
        gain_in = gains_full[0:1, :]
        low = lower[...]
        gain = gain_gate[...]

        def norm_rows(i):
            x = full[block(c * (rows // 32) + i, 32), :].astype(F32)
            scale = lax.rsqrt(jnp.sum(x * x, axis=1, keepdims=True) / feats + EPSILON)
            here = block(i, 32)
            normed[here, :] = (x * scale * gain_in).astype(BF16)
            scale_in[here, :] = jnp.broadcast_to(scale, (32, 128))

        each(rows // 32, norm_rows)
        pre_in[...] = plain_dot(normed[...], vin[...])
        pre_for[...] = plain_dot(normed[...], vfor[...])
        pre_gp[...] = plain_dot(normed[...], vgp[...])

        def gate_rows(i):
            here = block(i, 32)
            decay = low + (1.0 - low) * jax.nn.sigmoid(pre_for[here, :])
            to_planes(dec, here, decay)
            to_planes(src, here, (1.0 - decay) * jax.nn.silu(pre_in[here, :]))

        each(rows // 32, gate_rows)
        scan_rows(dec, src, hbuf, prod, 8)
        diff[...] = from_planes(hbuf, slice(7, 7 + rows))

        def mix_rows(i):
            here = block(i, 32)
            h = from_planes(hbuf, pl.ds(pl.multiple_of(8 + i * 32, 8), 32))
            state[here, :] = h
            diff[here, :] -= jax.nn.silu(pre_in[here, :])
            mixed[here, :] = (h * gain * jax.nn.silu(pre_gp[here, :])).astype(BF16)

        each(rows // 32, mix_rows)
        h = state[...]
        squares[0] = rows_to_lanes(h * h)
        hbuf[:, 7:8, :] = hbuf[:, 7 + rows : 8 + rows, :]

    @pl.when(s == chunks)
    def _():
        each(chunks, gather.drain)
        each(chunks, lambda c: tok_out(c).wait())
        for k in range(3):
            gain_copy(k).wait_send()
            w_swap(k).wait_send()
        for p in range(2):
            w_direct(0, p).wait_send()
            w_direct(1, p).wait_send()
            w_relay(p).wait_send()
        w_out.wait()


def later(s):
    return (jnp.maximum(s - 1, 0), 0)


def mixer_forward(tok, wout, gains, w_in, w_for, w_gp, lower, gain_gate):
    total, width = tok.shape
    feats = w_in.shape[0]
    rows = total // CHUNKS

    def out(n, dtype):
        return jax.ShapeDtypeStruct((total, n), dtype), pl.BlockSpec((rows, n), later)

    outs = [
        out(feats, BF16),
        (jax.ShapeDtypeStruct((total, feats), BF16), ANY),
        (jax.ShapeDtypeStruct((feats, feats), BF16), ANY),
        (jax.ShapeDtypeStruct((8, feats), F32), WHOLE),
        out(128, F32),
        out(width, F32),
        out(width, F32),
        out(width, F32),
        out(width, F32),
        out(width, F32),
        out(width, BF16),
        (
            jax.ShapeDtypeStruct((CHUNKS, 8, rows), F32),
            pl.BlockSpec((1, 8, rows), lambda s: (jnp.maximum(s - 1, 0), 0, 0)),
        ),
    ]
    dma = pltpu.SemaphoreType.DMA
    return pl.pallas_call(
        mixer_kernel,
        grid=(CHUNKS + 1,),
        out_shape=[o[0] for o in outs],
        out_specs=[o[1] for o in outs],
        in_specs=[ANY, ANY, WHOLE, ANY, ANY, ANY, WHOLE, WHOLE],
        scratch_shapes=[
            pltpu.VMEM((total, feats), BF16),
            pltpu.VMEM((feats, feats), BF16),
            pltpu.VMEM((feats, width), BF16),
            pltpu.VMEM((feats, width), BF16),
            pltpu.VMEM((feats, width), BF16),
            pltpu.VMEM((4, 8, width), F32),
            pltpu.VMEM((width // LANES, rows, LANES), F32),
            pltpu.VMEM((width // LANES, rows, LANES), F32),
            pltpu.VMEM((width // LANES, rows, LANES), F32),
            pltpu.VMEM((width // LANES, rows + 8, LANES), F32),
            dma((4, CHUNKS)),
            dma((4, CHUNKS)),
            dma((3, 2)),
            dma((3, 2)),
            dma((3,)),
            dma((3,)),
            dma((3,)),
            dma((3,)),
            dma((7,)),
            dma((CHUNKS,)),
        ],
        compiler_params=pltpu.CompilerParams(
            collective_id=1, has_side_effects=True, vmem_limit_bytes=VMEM_BYTES
        ),
        name="mixer_forward",
    )(tok, wout, gains, w_in, w_for, w_gp, lower, gain_gate)


def ffn_kernel(
    lens, mixed, cot, squares, gains, tok_full, wout, w_gate, w_up, w_down,
    normed, hidden, g_gate, g_up, cot_out, mix_out, scale_gate, scale_mid, resid,
    mfull, cfull, vout, vgate, vup, vdown, sbuf, mo, gbuf, ubuf, hbuf,
    send, recv, csend, crecv, ssend, srecv, lsem,
):
    s = pl.program_id(0)
    chunks = pl.num_programs(0) - 1
    width = mixed.shape[1]
    rows, feats = normed.shape
    hid = hidden.shape[1]
    t, xn, yn, dg = neighbours()
    peers = ({"tensor": xn}, {"tensor": yn}, {"tensor": dg})
    gather = Gather(mixed, mfull, send, recv, rows, width)
    cgather = Gather(cot, cfull, csend, crecv, rows, width)

    def square_copy(k):
        return pltpu.make_async_remote_copy(
            squares, sbuf.at[t], ssend.at[k], srecv.at[k], device_id=peers[k], device_id_type=MESH
        )

    loads = (
        pltpu.make_async_copy(mixed, mfull.at[:, block(t, width)], lsem.at[0]),
        pltpu.make_async_copy(cot, cfull.at[:, block(t, width)], lsem.at[1]),
        pltpu.make_async_copy(squares, sbuf.at[t], lsem.at[2]),
        pltpu.make_async_copy(wout, vout, lsem.at[3]),
        pltpu.make_async_copy(w_gate, vgate, lsem.at[4]),
        pltpu.make_async_copy(w_up, vup, lsem.at[5]),
        pltpu.make_async_copy(w_down, vdown, lsem.at[6]),
    )

    @pl.when(s == 0)
    def _():
        greet(peers)
        for k in range(3):
            square_copy(k).start()
        for c in range(AHEAD):
            gather.start(c)
            cgather.start(c)
        for load in loads:
            load.start()
        for load in loads:
            load.wait()
        for k in range(3):
            square_copy(k).wait_recv()

    @pl.when(s < chunks)
    def _():
        gather.forward(s)
        cgather.forward(s)

        @pl.when(s + AHEAD < chunks)
        def _():
            gather.start(s + AHEAD)
            cgather.start(s + AHEAD)

    @pl.when(s >= 1)
    def _():
        c = s - 1
        gain_mid = gains[1:2, :]
        gather.finish(c)
        here = block(c, rows)
        each(
            feats // width,
            lambda b: mo.__setitem__(
                (slice(None), block(b, width)), plain_dot(mfull[here, :], vout[:, block(b, width)])
            ),
        )
        total = sbuf[0, c] + sbuf[1, c] + sbuf[2, c] + sbuf[3, c]
        scale = lax.rsqrt(lanes_to_rows(total) / feats + EPSILON)
        scale_gate[...] = jnp.broadcast_to(scale, (rows, 128))

        def norm_rows(i):
            part = block(i, 32)
            m = mo[part, :] * scale_gate[part, 0:1]
            mix_out[part, :] = m.astype(BF16)
            r = m + tok_full[part, :].astype(F32)
            mid = lax.rsqrt(jnp.sum(r * r, axis=1, keepdims=True) / feats + EPSILON)
            scale_mid[part, :] = jnp.broadcast_to(mid, (32, 128))
            normed[part, :] = (r * mid * gain_mid).astype(BF16)
            mo[part, :] = r

        each(rows // 32, norm_rows)
        resid[...] = mo[:, block(t, width)]
        gbuf[...] = plain_dot(normed[...], vgate[...])
        ubuf[...] = plain_dot(normed[...], vup[...])
        cgather.finish(c)
        length = lens[0]

        def mask_rows(i):
            part = block(i, 32)
            position = c * rows + i * 32 + lax.broadcasted_iota(jnp.int32, (32, feats), 0)
            value = cfull[block(c * (rows // 32) + i, 32), :]
            cot_out[part, :] = jnp.where(position < length, value.astype(F32), 0.0).astype(BF16)

        each(rows // 32, mask_rows)
        hbuf[...] = back_dot(cot_out[...], vdown[...])

        def ffn_rows(i):
            part = block(i, 16)
            g = gbuf[part, :]
            u = ubuf[part, :]
            back = hbuf[part, :]
            sigma = jax.nn.sigmoid(g)
            act = g * sigma
            hidden[part, :] = (act * u).astype(BF16)
            g_gate[part, :] = (back * u * (sigma * (1.0 + g * (1.0 - sigma)))).astype(BF16)
            g_up[part, :] = (back * act).astype(BF16)

        each(rows // 16, ffn_rows)

    @pl.when(s == chunks)
    def _():
        each(chunks, gather.drain)
        each(chunks, cgather.drain)
        for k in range(3):
            square_copy(k).wait_send()


def ffn_forward(lens, mixed, cot, squares, gains, tok_full, wout, w_gate, w_up, w_down):
    total, width = mixed.shape
    feats, hid = w_gate.shape
    rows = total // CHUNKS

    def out(n, dtype):
        return jax.ShapeDtypeStruct((total, n), dtype), pl.BlockSpec((rows, n), later)

    outs = [
        out(feats, BF16),
        out(hid, BF16),
        out(hid, BF16),
        out(hid, BF16),
        out(feats, BF16),
        out(feats, BF16),
        out(128, F32),
        out(128, F32),
        out(width, F32),
    ]
    dma = pltpu.SemaphoreType.DMA
    return pl.pallas_call(
        ffn_kernel,
        grid=(CHUNKS + 1,),
        out_shape=[o[0] for o in outs],
        out_specs=[o[1] for o in outs],
        in_specs=[
            pl.BlockSpec(memory_space=pltpu.SMEM),
            ANY, ANY, WHOLE, WHOLE,
            pl.BlockSpec((rows, feats), later),
            ANY, ANY, ANY, ANY,
        ],
        scratch_shapes=[
            pltpu.VMEM((total, feats), BF16),
            pltpu.VMEM((total, feats), BF16),
            pltpu.VMEM((feats, feats), BF16),
            pltpu.VMEM((feats, hid), BF16),
            pltpu.VMEM((feats, hid), BF16),
            pltpu.VMEM((hid, feats), BF16),
            pltpu.VMEM((4, CHUNKS, 8, rows), F32),
            pltpu.VMEM((rows, feats), F32),
            pltpu.VMEM((rows, hid), F32),
            pltpu.VMEM((rows, hid), F32),
            pltpu.VMEM((rows, hid), F32),
            dma((4, CHUNKS)),
            dma((4, CHUNKS)),
            dma((4, CHUNKS)),
            dma((4, CHUNKS)),
            dma((3,)),
            dma((3,)),
            dma((7,)),
        ],
        compiler_params=pltpu.CompilerParams(
            collective_id=2, has_side_effects=True, vmem_limit_bytes=VMEM_BYTES
        ),
        name="ffn_forward",
    )(lens, mixed, cot, squares, gains, tok_full, wout, w_gate, w_up, w_down)


class Scatter:
    def __init__(self, share, keep, out1, in1, out2, in2, sems):
        self.share, self.keep = share, keep
        self.out1, self.in1, self.out2, self.in2 = out1, in1, out2, in2
        self.send1, self.recv1, self.send2, self.recv2 = sems
        self.t, xn, yn, self.dg = neighbours()
        self.order = ((xn, yn), (yn, xn))
        self.slots = keep.shape[0]
        self.outs = out1.shape[0]
        self.half = keep.shape[3]
        self.count = self.half // 32

    def hop1(self, c, h):
        return pltpu.make_async_remote_copy(
            self.out1.at[c % self.outs, h],
            self.in1.at[c, h],
            self.send1.at[h, c],
            self.recv1.at[h, c],
            device_id={"tensor": self.order[h][0]},
            device_id_type=MESH,
        )

    def hop2(self, c, h):
        return pltpu.make_async_remote_copy(
            self.out2.at[c % self.outs, h],
            self.in2.at[c, h],
            self.send2.at[h, c],
            self.recv2.at[h, c],
            device_id={"tensor": self.order[h][1]},
            device_id_type=MESH,
        )

    def begin(self, c):
        slot, place = c % self.slots, c % self.outs

        @pl.when(c >= self.outs)
        def _():
            for h in range(2):
                self.hop1(c - self.outs, h).wait_send()

        for h in range(2):
            one, two = self.order[h]

            def move(i, h=h, one=one, two=two):
                here = block(i, 32)
                there = block(h * self.count + i, 32)
                self.out1[place, h, 0, here, :] = self.share[one, there, :].astype(BF16)
                self.out1[place, h, 1, here, :] = self.share[self.dg, there, :].astype(BF16)
                self.keep[slot, h, 0, here, :] = self.share[self.t, there, :]
                self.keep[slot, h, 1, here, :] = self.share[two, there, :]

            each(self.count, move)
        for h in range(2):
            self.hop1(c, h).start()

    def middle(self, c):
        slot, place = c % self.slots, c % self.outs

        @pl.when(c >= self.outs)
        def _():
            for h in range(2):
                self.hop2(c - self.outs, h).wait_send()

        for h in range(2):
            self.hop1(c, h).wait_recv()

            def add(i, h=h):
                here = block(i, 32)
                self.out2[place, h, here, :] = (
                    self.keep[slot, h, 1, here, :] + self.in1[c, h, 1, here, :].astype(F32)
                ).astype(BF16)
                self.keep[slot, h, 0, here, :] += self.in1[c, h, 0, here, :].astype(F32)

            each(self.count, add)
        for h in range(2):
            self.hop2(c, h).start()

    def end(self, c, use):
        slot = c % self.slots
        for h in range(2):
            self.hop2(c, h).wait_recv()

            def give(i, h=h):
                here = block(i, 32)
                use(
                    h * self.count + i,
                    self.keep[slot, h, 0, here, :] + self.in2[c, h, here, :].astype(F32),
                )

            each(self.count, give)

    def drain(self, chunks):
        for c in range(max(chunks - self.outs, 0), chunks):
            for h in range(2):
                self.hop1(c, h).wait_send()
                self.hop2(c, h).wait_send()

    @staticmethod
    def scratch(chunks, rows, width):
        dma = pltpu.SemaphoreType.DMA
        return [
            pltpu.VMEM((4, rows, width), F32),
            pltpu.VMEM((3, 2, 2, rows // 2, width), F32),
            pltpu.VMEM((3, 2, 2, rows // 2, width), BF16),
            pltpu.VMEM((chunks, 2, 2, rows // 2, width), BF16),
            pltpu.VMEM((3, 2, rows // 2, width), BF16),
            pltpu.VMEM((chunks, 2, rows // 2, width), BF16),
            dma((2, chunks)),
            dma((2, chunks)),
            dma((2, chunks)),
            dma((2, chunks)),
        ]


def scan_rows_back(decay, source, state, product, carry):
    planes, rows, _ = decay.shape
    seg = rows // 8

    def first(n, held):
        j = seg - 1 - n
        out = []
        for q in range(planes):
            now, prod = held[q]
            here = pl.ds(j, 8, stride=seg)
            d = decay[q, here, :]
            now = source[q, here, :] + now
            state[q, here, :] = now
            product[q, here, :] = prod
            out.append((d * now, d * prod))
        return tuple(out)

    zero, one = jnp.zeros((8, LANES), F32), jnp.ones((8, LANES), F32)
    ends = lax.fori_loop(0, seg, first, ((zero, one),) * planes, unroll=4)
    entries = []
    for q in range(planes):
        last, prod = ends[q]
        value = carry[q, 0:1, :]
        parts = []
        for s in range(7, -1, -1):
            parts.append(value)
            value = prod[s : s + 1] * value + last[s : s + 1]
        entries.append(jnp.concatenate(parts[::-1], axis=0))
        carry[q, 0:1, :] = value

    def second(j, held):
        for q in range(planes):
            here = pl.ds(j, 8, stride=seg)
            state[q, here, :] += product[q, here, :] * entries[q]
        return held

    lax.fori_loop(0, seg, second, 0, unroll=4)


def fold_rows(value):
    return value[0:8] + value[8:16] + value[16:24] + value[24:32]


STAGES = 4


SITES = (1, 1, 1, 2, 1)


def spend(chain, base, sites, n):
    each(sites[n], lambda j: chain.tick(base + sum(sites[:n]) + j))


def back_kernel(dp, spans, *refs):
    arrays = len(spans)
    (
        g_gate, g_up, w_gate, w_up, w_out, gains, gain_gate, lower,
        cot, mix, tok, scale_mid, scale_gate, pre_in, pre_for, pre_gp, state, diff,
    ) = refs[:18]
    refs = refs[18:]
    grads, refs = refs[:arrays], refs[arrays:]
    g_mix, g_resid, g_pre, mixed, inner, sums_out = refs[:6]
    refs = refs[6:]
    totals, lows, highs, peer_refs = (refs[k * arrays : (k + 1) * arrays] for k in range(4))
    refs = refs[4 * arrays :]
    (
        vgate, vup, vout, full, line, dots, gm, dec, src, prod, adj, carry, sum_mid, sum_gate, sum_low,
        share, keep, out1, in1, out2, in2, send1, recv1, send2, recv2, send, recv, lsem,
    ) = refs[:28]
    chain = Chain(grads, spans, totals, lows, highs, peer_refs, refs[28], refs[29:], dp)
    s = pl.program_id(0)
    chunks = pl.num_programs(0) - STAGES
    rows, width = g_resid.shape
    feats = full.shape[1]
    t, xn, yn, dg = neighbours()
    peers = ({"tensor": xn}, {"tensor": yn})
    base = s * sum(SITES)
    gather = Gather(None, full, send, recv, rows, width)
    scatter = Scatter(share, keep, out1, in1, out2, in2, (send1, recv1, send2, recv2))
    loads = (
        pltpu.make_async_copy(w_gate, vgate, lsem.at[0]),
        pltpu.make_async_copy(w_up, vup, lsem.at[1]),
        pltpu.make_async_copy(w_out, vout, lsem.at[2]),
    )

    def place(c):
        return chunks - 1 - c

    def at_stage(n, act):
        @pl.when((s >= n) & (s - n < chunks))
        def _():
            act(s - n)

    @pl.when(s == 0)
    def _():
        for load in loads:
            load.start()
        greet(peers + tuple(chain.near()))
        chain.begin()
        carry[...] = jnp.zeros(carry.shape, F32)
        sum_mid[...] = jnp.zeros(sum_mid.shape, F32)
        sum_gate[...] = jnp.zeros(sum_gate.shape, F32)
        sum_low[...] = jnp.zeros(sum_low.shape, F32)
        for load in loads:
            load.wait()

    spend(chain, base, SITES, 0)
    at_stage(3, lambda c: gather.forward(place(c)))

    def summed(c):
        def use(i, value):
            full[block(place(c) * (rows // 32) + i, 32), block(t, width)] = value.astype(BF16)

        scatter.end(c, use)
        gather.start(place(c))

    at_stage(2, summed)
    spend(chain, base, SITES, 1)
    at_stage(1, scatter.middle)
    spend(chain, base, SITES, 2)

    def terms(c):
        def part(b):
            here = block(b, width)
            share[b] = back_dot(g_gate[...], vgate[here, :]) + back_dot(g_up[...], vup[here, :])

        each(feats // width, part)
        scatter.begin(c)

    at_stage(0, terms)
    spend(chain, base, SITES, 3)

    def finish(c):
        p = place(c)
        gather.finish(p)
        gain_mid = gains[1:2, :]
        gain = gain_gate[...]
        low = lower[...]

        def resid_rows(i):
            here = block(i, 32)
            g = full[block(p * (rows // 32) + i, 32), :].astype(F32)
            m = mix[here, :].astype(F32)
            r = tok[here, :].astype(F32) + m
            mid = scale_mid[here, 0:1]
            weighted = g * gain_mid
            total = jnp.sum(weighted * r, axis=1, keepdims=True) / feats
            grad = cot[here, :].astype(F32) + mid * weighted - r * (mid * mid * mid * total)
            low_grad = grad.astype(BF16)
            g_mix[here, :] = low_grad
            line[...] = grad
            g_resid[here, :] = line[:, block(t, width)]
            dots[here, :] = jnp.broadcast_to(
                jnp.sum(low_grad.astype(F32) * m, axis=1, keepdims=True), (32, 128)
            )
            sum_mid[...] += fold_rows(g * r * mid)

        each(rows // 32, resid_rows)
        gm[...] = back_dot(g_mix[...], vout[...])

        def state_rows(i):
            here = block(i, 32)
            h = state[here, :]
            scale = scale_gate[here, 0:1]
            ns = h * scale
            gp = pre_gp[here, :]
            sigma = jax.nn.sigmoid(gp)
            swish = gp * sigma
            grad = gm[here, :]
            sum_gate[...] += fold_rows(grad * ns * swish)
            g_pre[here, 2 * width :] = (grad * ns * gain * (sigma * (1.0 + gp * (1.0 - sigma)))).astype(BF16)
            mixed[here, :] = (ns * gain * swish).astype(BF16)
            factor = scale * scale * dots[here, 0:1] / feats
            to_planes(src, here, scale * (grad * gain * swish) - h * factor)
            to_planes(dec, here, low + (1.0 - low) * jax.nn.sigmoid(pre_for[here, :]))

        each(rows // 32, state_rows)
        scan_rows_back(dec, src, adj, prod, carry)

        def gate_rows(i):
            here = block(i, 32)
            a = from_planes(adj, here)
            x, f = pre_in[here, :], pre_for[here, :]
            sig = jax.nn.sigmoid(f)
            decay = low + (1.0 - low) * sig
            grad_decay = a * diff[here, :]
            gi = (a * (1.0 - decay) * silu_slope(x)).astype(BF16)
            gf = (grad_decay * (1.0 - low) * sig * (1.0 - sig)).astype(BF16)
            g_pre[here, 0:width] = gi
            g_pre[here, width : 2 * width] = gf
            sum_low[...] += fold_rows(grad_decay * (1.0 - sig))
            gm[here, :] = (
                gi.astype(F32) * x + gf.astype(F32) * f + g_pre[here, 2 * width :].astype(F32) * pre_gp[here, :]
            )

        each(rows // 32, gate_rows)
        inner[0] = rows_to_lanes(gm[...])

    at_stage(STAGES, finish)
    spend(chain, base, SITES, 4)

    @pl.when(s == pl.num_programs(0) - 1)
    def _():
        each(chunks, gather.drain)
        scatter.drain(CHUNKS)
        chain.close(base + sum(SITES))
        sums_out[0] = sum_mid[:, block(t, width)]
        sums_out[1] = sum_gate[...]
        sums_out[2] = sum_low[...]


def backward(
    dp, grads, spans, g_gate, g_up, w_gate, w_up, w_out, gains, gain_gate, lower,
    cot, mix, tok, scale_mid, scale_gate, pre_in, pre_for, pre_gp, state, diff,
):
    total, hid = g_gate.shape
    feats, width = mix.shape[1], pre_in.shape[1]
    rows = total // CHUNKS

    def early(s):
        return (CHUNKS - 1 - jnp.minimum(s, CHUNKS - 1), 0)

    def late(s):
        return (CHUNKS - 1 - jnp.maximum(s - STAGES, 0), 0)

    def out(n, dtype):
        return jax.ShapeDtypeStruct((total, n), dtype), pl.BlockSpec((rows, n), late)

    outs = [
        out(feats, BF16),
        out(width, F32),
        out(3 * width, BF16),
        out(width, BF16),
        (
            jax.ShapeDtypeStruct((CHUNKS, 8, rows), F32),
            pl.BlockSpec((1, 8, rows), lambda s: late(s) + (0,)),
        ),
        (jax.ShapeDtypeStruct((3, 8, width), F32), WHOLE),
    ] + [(jax.ShapeDtypeStruct(g.shape, BF16), ANY) for g in grads] * 4
    planes = width // LANES
    dma = pltpu.SemaphoreType.DMA
    return pl.pallas_call(
        functools.partial(back_kernel, dp, spans),
        grid=(CHUNKS + STAGES,),
        out_shape=[o[0] for o in outs],
        out_specs=[o[1] for o in outs],
        in_specs=[
            pl.BlockSpec((rows, hid), early),
            pl.BlockSpec((rows, hid), early),
            ANY, ANY, ANY, WHOLE, WHOLE, WHOLE,
            pl.BlockSpec((rows, feats), late),
            pl.BlockSpec((rows, feats), late),
            pl.BlockSpec((rows, feats), late),
            pl.BlockSpec((rows, 128), late),
            pl.BlockSpec((rows, 128), late),
        ]
        + [pl.BlockSpec((rows, width), late)] * 5
        + [ANY] * len(grads),
        scratch_shapes=[
            pltpu.VMEM((feats, hid), BF16),
            pltpu.VMEM((feats, hid), BF16),
            pltpu.VMEM((width, feats), BF16),
            pltpu.VMEM((total, feats), BF16),
            pltpu.VMEM((32, feats), F32),
            pltpu.VMEM((rows, 128), F32),
            pltpu.VMEM((rows, width), F32),
            pltpu.VMEM((planes, rows, LANES), F32),
            pltpu.VMEM((planes, rows, LANES), F32),
            pltpu.VMEM((planes, rows, LANES), F32),
            pltpu.VMEM((planes, rows, LANES), F32),
            pltpu.VMEM((planes, 8, LANES), F32),
            pltpu.VMEM((8, feats), F32),
            pltpu.VMEM((8, width), F32),
            pltpu.VMEM((8, width), F32),
        ]
        + Scatter.scratch(CHUNKS, rows, width)
        + [dma((4, CHUNKS)), dma((4, CHUNKS)), dma((3,))]
        + Chain.scratch(grads, spans),
        compiler_params=pltpu.CompilerParams(
            collective_id=3, has_side_effects=True, vmem_limit_bytes=VMEM_BYTES
        ),
        name="backward",
    )(
        g_gate, g_up, w_gate, w_up, w_out, gains, gain_gate, lower,
        cot, mix, tok, scale_mid, scale_gate, pre_in, pre_for, pre_gp, state, diff, *grads,
    )


LAST_SITES = (2, 1, 1, 2, 2)


def last_kernel(dp, spans, *refs):
    arrays = len(spans)
    g_pre, w_in, w_for, w_gp, hidden, w_down, inner, gain_in, sums_in, tok, scale_in, g_resid, resid = refs[:13]
    refs = refs[13:]
    grads, refs = refs[:arrays], refs[arrays:]
    out, g_tok, small = refs[:3]
    refs = refs[3:]
    totals, lows, highs, peer_refs = (refs[k * arrays : (k + 1) * arrays] for k in range(4))
    refs = refs[4 * arrays :]
    (
        vpre, vdown, ibuf, col, sum_in, mine, others,
        share, keep, out1, in1, out2, in2, send1, recv1, send2, recv2,
        fshare, fkeep, fout1, fin1, fout2, fin2, fsend1, frecv1, fsend2, frecv2,
        isend, irecv, lsem, osend, orecv,
    ) = refs[:32]
    chain = Chain(grads, spans, totals, lows, highs, peer_refs, refs[32], refs[33:], dp)
    me = lax.axis_index("dp")
    s = pl.program_id(0)
    base = s * sum(LAST_SITES)
    chunks = pl.num_programs(0) - 2
    rows, width = out.shape
    feats = w_down.shape[1]
    t, xn, yn, dg = neighbours()
    peers = ({"tensor": xn}, {"tensor": yn}, {"tensor": dg})
    scatter = Scatter(share, keep, out1, in1, out2, in2, (send1, recv1, send2, recv2))
    fscatter = Scatter(fshare, fkeep, fout1, fin1, fout2, fin2, (fsend1, frecv1, fsend2, frecv2))

    def inner_copy(k):
        return pltpu.make_async_remote_copy(
            inner, ibuf.at[t], isend.at[k], irecv.at[k], device_id=peers[k], device_id_type=MESH
        )

    def other(d):
        return pltpu.make_async_remote_copy(
            mine, others.at[me], osend.at[d], orecv.at[d],
            device_id={"dp": (me + d) % dp}, device_id_type=MESH,
        )

    loads = (
        pltpu.make_async_copy(w_in, vpre.at[:, 0:width], lsem.at[0]),
        pltpu.make_async_copy(w_for, vpre.at[:, width : 2 * width], lsem.at[1]),
        pltpu.make_async_copy(w_gp, vpre.at[:, 2 * width :], lsem.at[2]),
        pltpu.make_async_copy(w_down, vdown, lsem.at[3]),
        pltpu.make_async_copy(inner, ibuf.at[t], lsem.at[4]),
    )

    def at_stage(n, act):
        @pl.when((s >= n) & (s - n < chunks))
        def _():
            act(s - n)

    @pl.when(s == 0)
    def _():
        for load in loads:
            load.start()
        greet(peers + tuple({"dp": (me + d) % dp} for d in range(1, dp)))
        chain.begin()
        for k in range(3):
            inner_copy(k).start()
        sum_in[...] = jnp.zeros(sum_in.shape, F32)
        for load in loads:
            load.wait()

    @pl.when(s == 2)
    def _():
        for k in range(3):
            inner_copy(k).wait_recv()

    def finish(c):
        total = ibuf[0, c] + ibuf[1, c] + ibuf[2, c] + ibuf[3, c]
        col[...] = jnp.broadcast_to(lanes_to_rows(total) / feats, (rows, 128))
        gain = gain_in[...]

        def give(i, value):
            here = block(i, 32)
            x = tok[here, :].astype(F32)
            scale = scale_in[here, 0:1]
            g_tok[here, :] = (
                g_resid[here, :] + scale * (value * gain) - x * (scale * scale * col[here, 0:1])
            )
            sum_in[...] += fold_rows(value * x * scale)

        scatter.end(c, give)

        def give_out(i, value):
            here = block(i, 32)
            out[here, :] = (resid[here, :] + value).astype(BF16)

        fscatter.end(c, give_out)

    spend(chain, base, LAST_SITES, 0)
    at_stage(2, finish)
    spend(chain, base, LAST_SITES, 1)

    def middle(c):
        scatter.middle(c)
        fscatter.middle(c)

    at_stage(1, middle)
    spend(chain, base, LAST_SITES, 2)

    def terms(c):
        def part(b):
            share[b] = back_dot(g_pre[...], vpre[block(b, width), :])

        each(feats // width, part)
        scatter.begin(c)

    at_stage(0, terms)
    spend(chain, base, LAST_SITES, 3)

    def fterms(c):
        def fpart(b):
            fshare[b] = plain_dot(hidden[...], vdown[:, block(b, width)])

        each(feats // width, fpart)
        fscatter.begin(c)

    at_stage(0, fterms)
    spend(chain, base, LAST_SITES, 4)

    @pl.when(s == pl.num_programs(0) - 1)
    def _():
        mine[...] = jnp.zeros(mine.shape, F32)
        mine[0:1, :] = jnp.sum(sum_in[...], axis=0, keepdims=True)
        for k in range(3):
            mine[1 + k : 2 + k, :] = jnp.sum(sums_in[k], axis=0, keepdims=True)
        scatter.drain(CHUNKS)
        fscatter.drain(CHUNKS)
        for d in range(1, dp):
            other(d).start()
        chain.close(base + sum(LAST_SITES))
        others[me] = mine[...]
        for d in range(1, dp):
            other(d).wait()
        total = others[0]
        for d in range(1, dp):
            total += others[d]
        small[...] = total
        for k in range(3):
            inner_copy(k).wait_send()


def last_sums(
    dp, grads, spans, g_pre, w_in, w_for, w_gp, hidden, w_down, inner, gain_in, sums, tok, scale_in, g_resid, resid
):
    total, hid = hidden.shape
    feats, width = w_in.shape
    rows = total // CHUNKS

    def early(s):
        return (jnp.minimum(s, CHUNKS - 1), 0)

    def late(s):
        return (jnp.maximum(s - 2, 0), 0)

    far = pl.BlockSpec((rows, width), late)
    dma = pltpu.SemaphoreType.DMA
    return pl.pallas_call(
        functools.partial(last_kernel, dp, spans),
        grid=(CHUNKS + 2,),
        out_shape=[
            jax.ShapeDtypeStruct((total, width), BF16),
            jax.ShapeDtypeStruct((total, width), F32),
            jax.ShapeDtypeStruct((8, width), F32),
        ]
        + [jax.ShapeDtypeStruct(g.shape, BF16) for g in grads] * 4,
        out_specs=[far, far, WHOLE] + [ANY] * (4 * len(grads)),
        in_specs=[
            pl.BlockSpec((rows, 3 * width), early),
            ANY, ANY, ANY,
            pl.BlockSpec((rows, hid), early),
            ANY, WHOLE, WHOLE, WHOLE, far,
            pl.BlockSpec((rows, 128), late),
            far, far,
        ]
        + [ANY] * len(grads),
        scratch_shapes=[
            pltpu.VMEM((feats, 3 * width), BF16),
            pltpu.VMEM((hid, feats), BF16),
            pltpu.VMEM((4, CHUNKS, 8, rows), F32),
            pltpu.VMEM((rows, 128), F32),
            pltpu.VMEM((8, width), F32),
            pltpu.VMEM((8, width), F32),
            pltpu.VMEM((dp, 8, width), F32),
        ]
        + Scatter.scratch(CHUNKS, rows, width)
        + Scatter.scratch(CHUNKS, rows, width)
        + [dma((3,)), dma((3,)), dma((5,)), dma((dp,)), dma((dp,))]
        + Chain.scratch(grads, spans),
        compiler_params=pltpu.CompilerParams(
            collective_id=4, has_side_effects=True, vmem_limit_bytes=VMEM_BYTES
        ),
        name="last_sums",
    )(g_pre, w_in, w_for, w_gp, hidden, w_down, inner, gain_in, sums, tok, scale_in, g_resid, resid, *grads)


def on_device(
    dp, tokens, lengths, cotangent, w_norm_in, w_input, w_forget, w_gproj, lower_bound, w_gate_norm,
    w_output, w_norm_mid, w_gate, w_up, w_down,
):
    channels = w_input.shape[1]
    gain_in = w_norm_in.astype(F32)[None]
    gains = jnp.concatenate([gain_in, w_norm_mid.astype(F32)[None], jnp.zeros((6, channels), F32)], 0)
    lower = lower_bound.astype(F32)[None]
    gain_gate = w_gate_norm.astype(F32)[None]
    (
        normed_in, tok_full, wout_full, gains_full, scale_in, pre_in, pre_for, pre_gp, state, diff, raw, squares,
    ) = mixer_forward(tokens, w_output, gains, w_input, w_forget, w_gproj, lower, gain_gate)
    normed_mid, hidden, g_gate, g_up, cot, mix, scale_gate, scale_mid, resid = ffn_forward(
        lengths, raw, cotangent, squares, gains_full, tok_full, wout_full, w_gate, w_up, w_down
    )
    d_gate, d_up, d_down = (
        trans_dot(a, b).astype(BF16) for a, b in ((normed_mid, g_gate), (normed_mid, g_up), (hidden, cot))
    )
    d_gate, d_up, d_down, g_gate = lax.optimization_barrier((d_gate, d_up, d_down, g_gate))
    g_mix, g_resid, g_pre, mixed, inner, sums, s_gate, s_up = backward(
        dp, (d_gate, d_up), tuple((0, d.shape[0] // (2 * UNIT)) for d in (d_gate, d_up)), g_gate, g_up, w_gate, w_up, w_output, gains_full, gain_gate, lower,
        cot, mix, tok_full, scale_mid, scale_gate, pre_in, pre_for, pre_gp, state, diff,
    )[:8]
    d_pre, d_out = (trans_dot(a, b).astype(BF16) for a, b in ((normed_in, g_pre), (mixed, g_mix)))
    output, g_tok, small, s_down, s_pre, s_out = last_sums(
        dp, (d_down, d_pre, d_out), tuple((0, d.shape[0] // (2 * UNIT)) for d in (d_down, d_pre, d_out)), g_pre, w_input, w_forget, w_gproj, hidden, w_down, inner, gain_in, sums,
        tokens, scale_in, g_resid, resid,
    )[:6]
    pre = [s_pre[:, k * channels : (k + 1) * channels].astype(F32) for k in range(3)]
    return (
        output, g_tok, small[0], pre[0], pre[1], pre[2], small[3], small[2], s_out.astype(F32), small[1],
        s_gate.astype(F32), s_up.astype(F32), s_down.astype(F32),
    )


def solution(mesh):
    rows, cols, vec = P(None, "tensor"), P("tensor", None), P("tensor")
    both = P("dp", "tensor")
    in_specs = (both, P("dp"), both, vec, rows, rows, rows, vec, vec, cols, vec, rows, rows, cols)
    out_specs = (both, both, vec, rows, rows, rows, vec, vec, cols, vec, rows, rows, cols)
    return jax.shard_map(
        functools.partial(on_device, mesh.shape["dp"]), mesh=mesh, in_specs=in_specs, out_specs=out_specs,
        check_vma=False,
    )
```

```python
import functools

import jax
import jax.numpy as jnp
from jax import lax
from jax.experimental import pallas as pl
from jax.experimental.pallas import tpu as pltpu
from jax.sharding import PartitionSpec as P

EPSILON = 1e-06
MESH = pl.DeviceIdType.MESH
CHUNKS = 8
FRONT = 16
BACK = 8
AHEAD = 2
VMEM_BYTES = 67_000_000
F32 = jnp.float32
BF16 = jnp.bfloat16
ANY = pl.BlockSpec(memory_space=pl.ANY)
WHOLE = pl.BlockSpec(memory_space=pltpu.VMEM)


def silu_slope(value):
    sigma = jax.nn.sigmoid(value)
    return sigma * (1.0 + value * (1.0 - sigma))


def plain_dot(left, right):
    return jnp.dot(left, right, preferred_element_type=F32)


def trans_dot(left, right):
    return lax.dot_general(left, right, (((0,), (0,)), ((), ())), preferred_element_type=F32)


def back_dot(left, right):
    return lax.dot_general(left, right, (((1,), (1,)), ((), ())), preferred_element_type=F32)


def rows_to_lanes(values):
    ones = jnp.ones((8, values.shape[1]), F32)
    return lax.dot_general(
        ones, values, (((1,), (1,)), ((), ())), precision=lax.Precision.HIGHEST,
        preferred_element_type=F32,
    )


def lanes_to_rows(values):
    ones = jnp.full((8, 128), 0.125, F32)
    wide = lax.dot_general(
        values, ones, (((0,), (0,)), ((), ())), precision=lax.Precision.HIGHEST,
        preferred_element_type=F32,
    )
    return wide[:, :1]


def neighbours():
    t = lax.axis_index("tensor")
    return t, t + 1 - 2 * (t % 2), t + 2 - 4 * (t // 2), 3 - t


def block(start, size):
    return pl.ds(pl.multiple_of(start * size, size), size)


def greet(devices):
    barrier = pltpu.get_barrier_semaphore()
    for device in devices:
        pl.semaphore_signal(barrier, inc=1, device_id=device, device_id_type=MESH)
    pl.semaphore_wait(barrier, len(devices))


def each(count, step):
    def body(i, carry):
        step(i)
        return carry

    lax.fori_loop(0, count, body, 0)


class Gather:
    def __init__(self, source, full, send, recv, rows, width):
        self.source, self.full, self.send, self.recv = source, full, send, recv
        self.rows, self.width = rows, width
        self.t, self.xn, self.yn, self.dg = neighbours()

    def direct(self, c, k):
        rows = block(c, self.rows)
        place = self.full.at[rows, block(self.t, self.width)]
        return pltpu.make_async_remote_copy(
            place if self.source is None else self.source.at[rows, :],
            place,
            self.send.at[k, c],
            self.recv.at[k, c],
            device_id={"tensor": self.xn if k == 0 else self.yn},
            device_id_type=MESH,
        )

    def relay(self, c, k):
        rows = block(2 * c + k, self.rows // 2)
        part = self.full.at[rows, block(self.xn if k == 0 else self.yn, self.width)]
        return pltpu.make_async_remote_copy(
            part,
            part,
            self.send.at[2 + k, c],
            self.recv.at[2 + k, c],
            device_id={"tensor": self.yn if k == 0 else self.xn},
            device_id_type=MESH,
        )

    def start(self, c):
        self.direct(c, 0).start()
        self.direct(c, 1).start()

    def forward(self, c):
        for k in range(2):
            self.direct(c, k).wait_recv()
            self.relay(c, k).start()

    def finish(self, c):
        self.relay(c, 0).wait_recv()
        self.relay(c, 1).wait_recv()

    def drain(self, c):
        for k in range(2):
            self.direct(c, k).wait_send()
            self.relay(c, k).wait_send()


LANES = 128


def scan_rows(decay, source, state, product, head):
    planes, rows, _ = decay.shape
    seg = rows // 8

    def first(j, held):
        out = []
        for q in range(planes):
            now, prod = held[q]
            d = decay[q, pl.ds(j, 8, stride=seg), :]
            now = d * now + source[q, pl.ds(j, 8, stride=seg), :]
            prod = d * prod
            state[q, pl.ds(head + j, 8, stride=seg), :] = now
            product[q, pl.ds(j, 8, stride=seg), :] = prod
            out.append((now, prod))
        return tuple(out)

    zero, one = jnp.zeros((8, LANES), F32), jnp.ones((8, LANES), F32)
    ends = lax.fori_loop(0, seg, first, ((zero, one),) * planes, unroll=4)
    entries = []
    for q in range(planes):
        last, prod = ends[q]
        carry = state[q, head - 1 : head, :]
        parts = []
        for s in range(8):
            parts.append(carry)
            carry = prod[s : s + 1] * carry + last[s : s + 1]
        entries.append(jnp.concatenate(parts, axis=0))

    def second(j, held):
        for q in range(planes):
            state[q, pl.ds(head + j, 8, stride=seg), :] += (
                product[q, pl.ds(j, 8, stride=seg), :] * entries[q]
            )
        return held

    lax.fori_loop(0, seg, second, 0, unroll=4)


def to_planes(ref, rows, value):
    for q in range(value.shape[1] // LANES):
        ref[q, rows, :] = value[:, q * LANES : (q + 1) * LANES]


def from_planes(ref, rows):
    return jnp.concatenate([ref[q, rows, :] for q in range(ref.shape[0])], axis=1)


LAG = 3


class Chain:
    def __init__(self, grads, units, sums, lows, highs, peers, buf, sems, count):
        self.grads, self.counts, self.sums, self.peers, self.buf = grads, units, sums, peers, buf
        self.unit = buf.shape[2]
        self.parts = (lows, highs)
        (
            self.part_send, self.low_recv, self.high_recv,
            self.low_send, self.up_send, self.fin_recv, self.twin_send, self.twin_recv, self.load_sem, self.put_sem,
        ) = sems
        me = lax.axis_index("dp")
        self.core = me % 2
        self.z = me // 2
        self.chips = count // 2
        self.left = {"dp": (me + count - 2) % count}
        self.right = {"dp": (me + 2) % count}
        self.twin = {"dp": me + 1 - 2 * self.core}
        self.first = []
        start = 0
        for n in units:
            self.first.append(start)
            start += n
        self.units = start
        self.far = self.chips // 2
        self.ticks = 2 * ((self.units - 1) // 2 + 2 * LAG * self.far + 4)

    def near(self):
        return [self.left, self.right, self.twin]

    def rows(self, i, u, core):
        return block(core * self.counts[i] + u - self.first[i], self.unit)

    def inside(self, i, u):
        return (u >= self.first[i]) & (u < self.first[i] + self.counts[i])

    def slot(self, i, u, k):
        return self.buf.at[u % 4, k, :, 0 : self.grads[i].shape[1]]

    def partial(self, i, u, way):
        rows = self.rows(i, u, self.core)
        return pltpu.make_async_remote_copy(
            self.slot(i, u, 4), self.parts[way][i].at[rows, :], self.part_send.at[u],
            (self.low_recv, self.high_recv)[way].at[u],
            device_id=(self.right, self.left)[way], device_id_type=MESH,
        )

    def final(self, i, u, way, staged):
        rows = self.rows(i, u, self.core)
        place = self.sums[i].at[rows, :]
        return pltpu.make_async_remote_copy(
            self.slot(i, u, 4) if staged else place, place,
            (self.up_send, self.low_send)[way].at[u], self.fin_recv.at[u],
            device_id=(self.right, self.left)[way], device_id_type=MESH,
        )

    def share(self, i, u, staged):
        rows = self.rows(i, u, self.core)
        place = self.sums[i].at[rows, :]
        return pltpu.make_async_remote_copy(
            self.slot(i, u, 4) if staged else place, place, self.twin_send.at[u], self.twin_recv.at[u],
            device_id=self.twin, device_id_type=MESH,
        )

    def load(self, i, u, k):
        rows = self.rows(i, u, self.core)
        refs = (self.grads[i], self.peers[i], self.parts[0][i], self.parts[1][i])
        return pltpu.make_async_copy(refs[k].at[rows, :], self.slot(i, u, k), self.load_sem.at[u % 4, k])

    def put(self, i, u):
        return pltpu.make_async_copy(
            self.slot(i, u, 4), self.sums[i].at[self.rows(i, u, self.core), :], self.put_sem.at[u % 4]
        )

    def over(self, act):
        for i, n in enumerate(self.counts):
            each(n, lambda j, i=i: act(i, self.first[i] + j))

    def owner(self, u):
        return self.chips // 2 - 1 + u % 2

    def from_low(self, u):
        return (self.z > 0) & (self.z <= self.owner(u))

    def from_high(self, u):
        return (self.z < self.chips - 1) & (self.z >= self.owner(u))

    def fetch(self, i, u):
        self.load(i, u, 0).start()
        self.load(i, u, 1).start()

        @pl.when(self.from_low(u))
        def _():
            self.partial(i, u, 0).wait_recv()
            self.load(i, u, 2).start()

        @pl.when(self.from_high(u))
        def _():
            self.partial(i, u, 1).wait_recv()
            self.load(i, u, 3).start()

    def settle(self, i, u):
        o = self.owner(u)

        @pl.when(self.z != o)
        def _():
            self.partial(i, u, 0).wait_send()

        @pl.when(self.z == o)
        def _():
            @pl.when(self.z < self.chips - 1)
            def _():
                self.final(i, u, 0, True).wait_send()

            @pl.when(self.z > 0)
            def _():
                self.final(i, u, 1, True).wait_send()

            self.share(i, u, True).wait_send()
            self.put(i, u).wait()

    def reduce(self, i, u):
        o = self.owner(u)
        self.load(i, u, 0).wait()
        self.load(i, u, 1).wait()
        width = self.grads[i].shape[1]
        here = u % 4

        def value(k, r):
            return self.buf[here, k, r, 0:width].astype(F32)

        def total(ks):
            def add(j):
                r = block(j, 16)
                self.buf[here, 4, r, 0:width] = sum(value(k, r) for k in ks).astype(BF16)

            each(self.unit // 16, add)

        low, high = self.from_low(u), self.from_high(u)

        @pl.when(low)
        def _():
            self.load(i, u, 2).wait()

        @pl.when(high)
        def _():
            self.load(i, u, 3).wait()

        @pl.when(low & high)
        def _():
            total((0, 1, 2, 3))

        @pl.when(low != high)
        def _():
            total((0, 1, 3 - low.astype(jnp.int32)))

        @pl.when(jnp.logical_not(low | high))
        def _():
            total((0, 1))

        @pl.when(self.z < o)
        def _():
            self.partial(i, u, 0).start()

        @pl.when(self.z > o)
        def _():
            self.partial(i, u, 1).start()

        @pl.when(self.z == o)
        def _():
            @pl.when(self.z < self.chips - 1)
            def _():
                self.final(i, u, 0, True).start()

            @pl.when(self.z > 0)
            def _():
                self.final(i, u, 1, True).start()

            self.share(i, u, True).start()
            self.put(i, u).start()

    def pass_on(self, i, u):
        o = self.owner(u)
        self.final(i, u, 0, False).wait_recv()

        @pl.when((self.z < o) & (self.z > 0))
        def _():
            self.final(i, u, 1, False).start()

        @pl.when((self.z > o) & (self.z < self.chips - 1))
        def _():
            self.final(i, u, 0, False).start()

        self.share(i, u, False).start()

    def tick(self, tau):
        stream = tau % 2
        k = tau // 2 - 1
        away = jnp.abs(self.z - self.owner(stream))
        now = 2 * (k - LAG * (self.far - away)) + stream
        back = 2 * (k - LAG * (self.far + away)) + stream

        def pick(u, act, also=True):
            for i in range(len(self.grads)):

                @pl.when(self.inside(i, u) & also)
                def _(i=i):
                    act(i, u)

        pick(now - 4, self.settle)
        pick(now, self.reduce)
        pick(back, self.pass_on, away > 0)
        pick(now + 2, self.fetch)

    def close(self, tau):
        each(self.ticks - tau, lambda j: self.tick(tau + j))

        def done(i, u):
            o = self.owner(u)

            @pl.when(self.z != o)
            def _():
                self.share(i, u, False).wait_send()

            @pl.when((self.z < o) & (self.z > 0))
            def _():
                self.final(i, u, 1, False).wait_send()

            @pl.when((self.z > o) & (self.z < self.chips - 1))
            def _():
                self.final(i, u, 0, False).wait_send()

            rows = self.rows(i, u, 1 - self.core)
            place = self.sums[i].at[rows, :]
            pltpu.make_async_remote_copy(
                place, place, self.twin_send.at[u], self.twin_recv.at[u],
                device_id=self.twin, device_id_type=MESH,
            ).wait_recv()

        self.over(done)

    @staticmethod
    def scratch(width, unit, units):
        dma = pltpu.SemaphoreType.DMA
        return [pltpu.VMEM((4, 5, unit, width), BF16)] + [dma((sum(units),))] * 8 + [dma((4, 4)), dma((4,))]


TILE = 256


class Tiles:
    def __init__(self, lhs, rhs, ready, grads, peers, lbuf, xbuf, stage, sems):
        self.lhs, self.rhs, self.ready, self.grads, self.peers = lhs, rhs, ready, grads, peers
        self.lbuf, self.xbuf, self.stage = lbuf, xbuf, stage
        self.load_sem, self.put_sem, self.send_sem, self.recv_sem = sems
        me = lax.axis_index("dp")
        self.core = me % 2
        self.twin = {"dp": me + 1 - 2 * self.core}
        self.counts = [g.shape[0] // (2 * TILE) for g in grads]
        self.first = [sum(self.counts[:i]) for i in range(len(grads))]
        self.pairs = sum(self.counts)

    def rows(self, i, p, core):
        return block(core * self.counts[i] + p - self.first[i], TILE)

    def load(self, i, p, h):
        core = self.core if h else 1 - self.core
        return pltpu.make_async_copy(
            self.lhs[i].at[:, self.rows(i, p, core)], self.lbuf.at[h], self.load_sem.at[h]
        )

    def send(self, i, p):
        rows = self.rows(i, p, 1 - self.core)
        return pltpu.make_async_remote_copy(
            self.stage.at[0, :, 0 : self.grads[i].shape[1]], self.peers[i].at[rows, :],
            self.send_sem.at[p], self.recv_sem.at[p], device_id=self.twin, device_id_type=MESH,
        )

    def put(self, i, p):
        rows = self.rows(i, p, self.core)
        return pltpu.make_async_copy(
            self.stage.at[1, :, 0 : self.grads[i].shape[1]], self.grads[i].at[rows, :], self.put_sem.at[p]
        )

    def pick(self, p, act):
        for i in range(len(self.grads)):

            @pl.when((p >= self.first[i]) & (p < self.first[i] + self.counts[i]))
            def _(i=i):
                act(i)

    def begin(self):
        self.load(0, 0, 0).start()
        self.load(0, 0, 1).start()

    def settle(self, p):
        def act(i):
            self.send(i, p).wait()
            self.put(i, p).wait()

        self.pick(p, act)

    def work(self, p, hook):
        total = self.xbuf.shape[1]

        def pair(i):
            @pl.when(p == self.first[i])
            def _():
                self.ready[i]()

            width = self.grads[i].shape[1]

            def tile(h):
                @pl.when(h == 0)
                def _():
                    self.load(i, p, 0).wait()

                @pl.when(h == 1)
                def _():
                    self.load(i, p, 1).wait()

                def turn(k):
                    r = block(k, TILE)
                    self.xbuf[:, r] = self.lbuf[h, r, :].T

                each(total // TILE, turn)
                hook(2 * h)

                @pl.when(h == 0)
                def _():
                    self.pick(p + 1, lambda n: self.load(n, p + 1, 0).start())

                @pl.when(h == 1)
                def _():
                    self.pick(p + 1, lambda n: self.load(n, p + 1, 1).start())

                step = next(w for w in (1408, 1024, 768, 512) if width % w == 0)

                def part(b):
                    cols = block(b, step)
                    self.stage[h, :, cols] = plain_dot(self.xbuf[...], self.rhs[i][:, cols]).astype(BF16)

                each(width // step, part)

                @pl.when(h == 0)
                def _():
                    self.send(i, p).start()

                @pl.when(h == 1)
                def _():
                    self.put(i, p).start()

                hook(2 * h + 1)

            each(2, tile)

        self.settle(p - 1)
        self.pick(p, pair)

        @pl.when(p >= self.pairs)
        def _():
            each(4, hook)

    @staticmethod
    def scratch(rows, width, pairs):
        dma = pltpu.SemaphoreType.DMA
        return [
            pltpu.VMEM((2, rows, TILE), BF16),
            pltpu.VMEM((TILE, rows), BF16),
            pltpu.VMEM((2, TILE, width), BF16),
            dma((2,)),
            dma((pairs,)),
            dma((pairs,)),
            dma((pairs,)),
        ]


def mixer_kernel(
    tok, wout, gains, w_in, w_for, w_gp, lower, gain_gate,
    normed, tok_full, wout_full, gains_full, scale_in, pre_in, pre_for, pre_gp, state, diff, mixed, squares,
    full, wfull, vin, vfor, vgp, gbuf, dec, src, prod, hbuf,
    send, recv, wsend, wrecv, xsend, xrecv, gsend, grecv, lsem, osem,
):
    s = pl.program_id(0)
    chunks = pl.num_programs(0) - 1
    rows, width = pre_in.shape
    feats = full.shape[1]
    t, xn, yn, dg = neighbours()
    me = lax.axis_index("dp")
    core = me % 2
    partner = {"dp": me + 1 - 2 * core}
    peers = ({"tensor": xn}, {"tensor": yn}, {"tensor": dg})
    gather = Gather(tok, full, send, recv, rows, width)
    planes = width // LANES
    half = width // 2
    piece = width // 4

    def w_direct(k, p):
        return pltpu.make_async_remote_copy(
            wout.at[block(2 * core + p, piece), :],
            wfull.at[block(4 * t + 2 * core + p, piece), :],
            wsend.at[k, p],
            wrecv.at[k, p],
            device_id=peers[k],
            device_id_type=MESH,
        )

    def w_relay(k):
        part = wfull.at[block(4 * (xn if k == 0 else yn) + 2 * core + k, piece), :]
        return pltpu.make_async_remote_copy(
            part, part, wsend.at[2, k], wrecv.at[2, k], device_id=peers[1 - k], device_id_type=MESH
        )

    def w_swap(k):
        part = wfull.at[block(2 * (xn, yn, dg)[k] + core, half), :]
        return pltpu.make_async_remote_copy(
            part, part, xsend.at[k], xrecv.at[k], device_id=partner, device_id_type=MESH
        )

    def gain_copy(k):
        return pltpu.make_async_remote_copy(
            gains, gbuf.at[t], gsend.at[k], grecv.at[k], device_id=peers[k], device_id_type=MESH
        )

    loads = (
        pltpu.make_async_copy(tok, full.at[:, block(t, width)], lsem.at[0]),
        pltpu.make_async_copy(wout, wfull.at[block(t, width), :], lsem.at[1]),
        pltpu.make_async_copy(w_in, vin, lsem.at[2]),
        pltpu.make_async_copy(w_for, vfor, lsem.at[3]),
        pltpu.make_async_copy(w_gp, vgp, lsem.at[4]),
        pltpu.make_async_copy(gains, gbuf.at[t], lsem.at[5]),
    )

    def tok_out(c):
        return pltpu.make_async_copy(
            full.at[block(c, rows), :], tok_full.at[block(c, rows), :], osem.at[c]
        )

    w_out = pltpu.make_async_copy(wfull, wout_full, lsem.at[6])

    @pl.when(s == 0)
    def _():
        for load in loads:
            load.start()
        greet(peers + (partner,))
        for k in range(3):
            gain_copy(k).start()
        for p in range(2):
            w_direct(0, p).start()
            w_direct(1, p).start()
        for c in range(AHEAD):
            gather.start(c)
        hbuf[:, 0:8, :] = jnp.zeros((planes, 8, LANES), F32)
        for p in range(2):
            w_direct(0, p).wait_recv()
            w_direct(1, p).wait_recv()
        w_relay(0).start()
        w_relay(1).start()
        w_swap(0).start()
        w_swap(1).start()
        for load in loads:
            load.wait()
        for k in range(3):
            gain_copy(k).wait_recv()
        for j in range(4):
            gains_full[:, j * width : (j + 1) * width] = gbuf[j]

    @pl.when(s == 2)
    def _():
        w_relay(0).wait_recv()
        w_relay(1).wait_recv()
        w_swap(2).start()

    @pl.when(s == chunks - 1)
    def _():
        for k in range(3):
            w_swap(k).wait_recv()
        w_out.start()

    @pl.when(s < chunks)
    def _():
        gather.forward(s)

        @pl.when(s + AHEAD < chunks)
        def _():
            gather.start(s + AHEAD)

    @pl.when(s >= 1)
    def _():
        c = s - 1
        gather.finish(c)
        tok_out(c).start()
        gain_in = gains_full[0:1, :]
        low = lower[...]
        gain = gain_gate[...]

        def norm_rows(i):
            x = full[block(c * (rows // 32) + i, 32), :].astype(F32)
            scale = lax.rsqrt(jnp.sum(x * x, axis=1, keepdims=True) / feats + EPSILON)
            here = block(i, 32)
            normed[here, :] = (x * scale * gain_in).astype(BF16)
            scale_in[here, :] = jnp.broadcast_to(scale, (32, 128))

        each(rows // 32, norm_rows)
        pre_in[...] = plain_dot(normed[...], vin[...])
        pre_for[...] = plain_dot(normed[...], vfor[...])
        pre_gp[...] = plain_dot(normed[...], vgp[...])

        def gate_rows(i):
            here = block(i, 32)
            decay = low + (1.0 - low) * jax.nn.sigmoid(pre_for[here, :])
            to_planes(dec, here, decay)
            to_planes(src, here, (1.0 - decay) * jax.nn.silu(pre_in[here, :]))

        each(rows // 32, gate_rows)
        scan_rows(dec, src, hbuf, prod, 8)
        diff[...] = from_planes(hbuf, slice(7, 7 + rows))

        def mix_rows(i):
            here = block(i, 32)
            h = from_planes(hbuf, pl.ds(pl.multiple_of(8 + i * 32, 8), 32))
            state[here, :] = h
            diff[here, :] -= jax.nn.silu(pre_in[here, :])
            mixed[here, :] = (h * gain * jax.nn.silu(pre_gp[here, :])).astype(BF16)

        each(rows // 32, mix_rows)
        h = state[...]
        squares[0] = rows_to_lanes(h * h)
        hbuf[:, 7:8, :] = hbuf[:, 7 + rows : 8 + rows, :]

    @pl.when(s == chunks)
    def _():
        each(chunks, gather.drain)
        each(chunks, lambda c: tok_out(c).wait())
        for k in range(3):
            gain_copy(k).wait_send()
            w_swap(k).wait_send()
        for p in range(2):
            w_direct(0, p).wait_send()
            w_direct(1, p).wait_send()
            w_relay(p).wait_send()
        w_out.wait()


def later(s):
    return (jnp.maximum(s - 1, 0), 0)


def mixer_forward(tok, wout, gains, w_in, w_for, w_gp, lower, gain_gate):
    total, width = tok.shape
    feats = w_in.shape[0]
    rows = total // FRONT

    def out(n, dtype):
        return jax.ShapeDtypeStruct((total, n), dtype), pl.BlockSpec((rows, n), later)

    outs = [
        out(feats, BF16),
        (jax.ShapeDtypeStruct((total, feats), BF16), ANY),
        (jax.ShapeDtypeStruct((feats, feats), BF16), ANY),
        (jax.ShapeDtypeStruct((8, feats), F32), WHOLE),
        out(128, F32),
        out(width, F32),
        out(width, F32),
        out(width, F32),
        out(width, F32),
        out(width, F32),
        out(width, BF16),
        (
            jax.ShapeDtypeStruct((FRONT, 8, rows), F32),
            pl.BlockSpec((1, 8, rows), lambda s: (jnp.maximum(s - 1, 0), 0, 0)),
        ),
    ]
    dma = pltpu.SemaphoreType.DMA
    return pl.pallas_call(
        mixer_kernel,
        grid=(FRONT + 1,),
        out_shape=[o[0] for o in outs],
        out_specs=[o[1] for o in outs],
        in_specs=[ANY, ANY, WHOLE, ANY, ANY, ANY, WHOLE, WHOLE],
        scratch_shapes=[
            pltpu.VMEM((total, feats), BF16),
            pltpu.VMEM((feats, feats), BF16),
            pltpu.VMEM((feats, width), BF16),
            pltpu.VMEM((feats, width), BF16),
            pltpu.VMEM((feats, width), BF16),
            pltpu.VMEM((4, 8, width), F32),
            pltpu.VMEM((width // LANES, rows, LANES), F32),
            pltpu.VMEM((width // LANES, rows, LANES), F32),
            pltpu.VMEM((width // LANES, rows, LANES), F32),
            pltpu.VMEM((width // LANES, rows + 8, LANES), F32),
            dma((4, FRONT)),
            dma((4, FRONT)),
            dma((3, 2)),
            dma((3, 2)),
            dma((3,)),
            dma((3,)),
            dma((3,)),
            dma((3,)),
            dma((7,)),
            dma((FRONT,)),
        ],
        compiler_params=pltpu.CompilerParams(
            collective_id=1, has_side_effects=True, vmem_limit_bytes=VMEM_BYTES
        ),
        name="mixer_forward",
    )(tok, wout, gains, w_in, w_for, w_gp, lower, gain_gate)


def ffn_kernel(
    lens, mixed, cot, squares, gains, tok_full, wout, w_gate, w_up, w_down,
    normed, hidden, g_both, cot_out, mix_out, scale_gate, scale_mid, resid,
    mfull, cfull, vout, vgate, vup, vdown, sbuf, mo, gbuf, ubuf, hbuf,
    send, recv, csend, crecv, ssend, srecv, lsem,
):
    s = pl.program_id(0)
    chunks = pl.num_programs(0) - 1
    width = mixed.shape[1]
    rows, feats = normed.shape
    hid = hidden.shape[1]
    t, xn, yn, dg = neighbours()
    peers = ({"tensor": xn}, {"tensor": yn}, {"tensor": dg})
    gather = Gather(mixed, mfull, send, recv, rows, width)
    cgather = Gather(cot, cfull, csend, crecv, rows, width)

    def square_copy(k):
        return pltpu.make_async_remote_copy(
            squares, sbuf.at[t], ssend.at[k], srecv.at[k], device_id=peers[k], device_id_type=MESH
        )

    loads = (
        pltpu.make_async_copy(mixed, mfull.at[:, block(t, width)], lsem.at[0]),
        pltpu.make_async_copy(cot, cfull.at[:, block(t, width)], lsem.at[1]),
        pltpu.make_async_copy(squares, sbuf.at[t], lsem.at[2]),
        pltpu.make_async_copy(wout, vout, lsem.at[3]),
        pltpu.make_async_copy(w_gate, vgate, lsem.at[4]),
        pltpu.make_async_copy(w_up, vup, lsem.at[5]),
        pltpu.make_async_copy(w_down, vdown, lsem.at[6]),
    )

    @pl.when(s == 0)
    def _():
        greet(peers)
        for k in range(3):
            square_copy(k).start()
        for c in range(AHEAD):
            gather.start(c)
            cgather.start(c)
        for load in loads:
            load.start()
        for load in loads:
            load.wait()
        for k in range(3):
            square_copy(k).wait_recv()

    @pl.when(s < chunks)
    def _():
        gather.forward(s)
        cgather.forward(s)

        @pl.when(s + AHEAD < chunks)
        def _():
            gather.start(s + AHEAD)
            cgather.start(s + AHEAD)

    @pl.when(s >= 1)
    def _():
        c = s - 1
        gain_mid = gains[1:2, :]
        gather.finish(c)
        here = block(c, rows)
        each(
            feats // width,
            lambda b: mo.__setitem__(
                (slice(None), block(b, width)), plain_dot(mfull[here, :], vout[:, block(b, width)])
            ),
        )
        total = sbuf[0, c] + sbuf[1, c] + sbuf[2, c] + sbuf[3, c]
        scale = lax.rsqrt(lanes_to_rows(total) / feats + EPSILON)
        scale_gate[...] = jnp.broadcast_to(scale, (rows, 128))

        def norm_rows(i):
            part = block(i, 32)
            m = mo[part, :] * scale_gate[part, 0:1]
            mix_out[part, :] = m.astype(BF16)
            r = m + tok_full[part, :].astype(F32)
            mid = lax.rsqrt(jnp.sum(r * r, axis=1, keepdims=True) / feats + EPSILON)
            scale_mid[part, :] = jnp.broadcast_to(mid, (32, 128))
            normed[part, :] = (r * mid * gain_mid).astype(BF16)
            mo[part, :] = r

        each(rows // 32, norm_rows)
        resid[...] = mo[:, block(t, width)]
        gbuf[...] = plain_dot(normed[...], vgate[...])
        ubuf[...] = plain_dot(normed[...], vup[...])
        cgather.finish(c)
        length = lens[0]

        def mask_rows(i):
            part = block(i, 32)
            position = c * rows + i * 32 + lax.broadcasted_iota(jnp.int32, (32, feats), 0)
            value = cfull[block(c * (rows // 32) + i, 32), :]
            cot_out[part, :] = jnp.where(position < length, value.astype(F32), 0.0).astype(BF16)

        each(rows // 32, mask_rows)
        hbuf[...] = back_dot(cot_out[...], vdown[...])

        def ffn_rows(i):
            part = block(i, 16)
            g = gbuf[part, :]
            u = ubuf[part, :]
            back = hbuf[part, :]
            sigma = jax.nn.sigmoid(g)
            act = g * sigma
            hidden[part, :] = (act * u).astype(BF16)
            g_both[part, 0:hid] = (back * u * (sigma * (1.0 + g * (1.0 - sigma)))).astype(BF16)
            g_both[part, hid:] = (back * act).astype(BF16)

        each(rows // 16, ffn_rows)

    @pl.when(s == chunks)
    def _():
        each(chunks, gather.drain)
        each(chunks, cgather.drain)
        for k in range(3):
            square_copy(k).wait_send()


def ffn_forward(lens, mixed, cot, squares, gains, tok_full, wout, w_gate, w_up, w_down):
    total, width = mixed.shape
    feats, hid = w_gate.shape
    rows = total // FRONT

    def out(n, dtype):
        return jax.ShapeDtypeStruct((total, n), dtype), pl.BlockSpec((rows, n), later)

    outs = [
        out(feats, BF16),
        out(hid, BF16),
        out(2 * hid, BF16),
        out(feats, BF16),
        out(feats, BF16),
        out(128, F32),
        out(128, F32),
        out(width, F32),
    ]
    dma = pltpu.SemaphoreType.DMA
    return pl.pallas_call(
        ffn_kernel,
        grid=(FRONT + 1,),
        out_shape=[o[0] for o in outs],
        out_specs=[o[1] for o in outs],
        in_specs=[
            pl.BlockSpec(memory_space=pltpu.SMEM),
            ANY, ANY, WHOLE, WHOLE,
            pl.BlockSpec((rows, feats), later),
            ANY, ANY, ANY, ANY,
        ],
        scratch_shapes=[
            pltpu.VMEM((total, feats), BF16),
            pltpu.VMEM((total, feats), BF16),
            pltpu.VMEM((feats, feats), BF16),
            pltpu.VMEM((feats, hid), BF16),
            pltpu.VMEM((feats, hid), BF16),
            pltpu.VMEM((hid, feats), BF16),
            pltpu.VMEM((4, FRONT, 8, rows), F32),
            pltpu.VMEM((rows, feats), F32),
            pltpu.VMEM((rows, hid), F32),
            pltpu.VMEM((rows, hid), F32),
            pltpu.VMEM((rows, hid), F32),
            dma((4, FRONT)),
            dma((4, FRONT)),
            dma((4, FRONT)),
            dma((4, FRONT)),
            dma((3,)),
            dma((3,)),
            dma((7,)),
        ],
        compiler_params=pltpu.CompilerParams(
            collective_id=2, has_side_effects=True, vmem_limit_bytes=VMEM_BYTES
        ),
        name="ffn_forward",
    )(lens, mixed, cot, squares, gains, tok_full, wout, w_gate, w_up, w_down)


class Scatter:
    def __init__(self, share, keep, out1, in1, out2, in2, sems):
        self.share, self.keep = share, keep
        self.out1, self.in1, self.out2, self.in2 = out1, in1, out2, in2
        self.send1, self.recv1, self.send2, self.recv2 = sems
        self.t, xn, yn, self.dg = neighbours()
        self.order = ((xn, yn), (yn, xn))
        self.slots = keep.shape[0]
        self.outs = out1.shape[0]
        self.half = keep.shape[3]
        self.count = self.half // 32

    def hop1(self, c, h):
        return pltpu.make_async_remote_copy(
            self.out1.at[c % self.outs, h],
            self.in1.at[c, h],
            self.send1.at[h, c],
            self.recv1.at[h, c],
            device_id={"tensor": self.order[h][0]},
            device_id_type=MESH,
        )

    def hop2(self, c, h):
        return pltpu.make_async_remote_copy(
            self.out2.at[c % self.outs, h],
            self.in2.at[c, h],
            self.send2.at[h, c],
            self.recv2.at[h, c],
            device_id={"tensor": self.order[h][1]},
            device_id_type=MESH,
        )

    def begin(self, c):
        slot, place = c % self.slots, c % self.outs

        @pl.when(c >= self.outs)
        def _():
            for h in range(2):
                self.hop1(c - self.outs, h).wait_send()

        for h in range(2):
            one, two = self.order[h]

            def move(i, h=h, one=one, two=two):
                here = block(i, 32)
                there = block(h * self.count + i, 32)
                self.out1[place, h, 0, here, :] = self.share[one, there, :].astype(BF16)
                self.out1[place, h, 1, here, :] = self.share[self.dg, there, :].astype(BF16)
                self.keep[slot, h, 0, here, :] = self.share[self.t, there, :]
                self.keep[slot, h, 1, here, :] = self.share[two, there, :]

            each(self.count, move)
        for h in range(2):
            self.hop1(c, h).start()

    def middle(self, c):
        slot, place = c % self.slots, c % self.outs

        @pl.when(c >= self.outs)
        def _():
            for h in range(2):
                self.hop2(c - self.outs, h).wait_send()

        for h in range(2):
            self.hop1(c, h).wait_recv()

            def add(i, h=h):
                here = block(i, 32)
                self.out2[place, h, here, :] = (
                    self.keep[slot, h, 1, here, :] + self.in1[c, h, 1, here, :].astype(F32)
                ).astype(BF16)
                self.keep[slot, h, 0, here, :] += self.in1[c, h, 0, here, :].astype(F32)

            each(self.count, add)
        for h in range(2):
            self.hop2(c, h).start()

    def end(self, c, use):
        slot = c % self.slots
        for h in range(2):
            self.hop2(c, h).wait_recv()

            def give(i, h=h):
                here = block(i, 32)
                use(
                    h * self.count + i,
                    self.keep[slot, h, 0, here, :] + self.in2[c, h, here, :].astype(F32),
                )

            each(self.count, give)

    def drain(self, chunks):
        for c in range(max(chunks - self.outs, 0), chunks):
            for h in range(2):
                self.hop1(c, h).wait_send()
                self.hop2(c, h).wait_send()

    @staticmethod
    def scratch(chunks, rows, width):
        dma = pltpu.SemaphoreType.DMA
        return [
            pltpu.VMEM((4, rows, width), F32),
            pltpu.VMEM((3, 2, 2, rows // 2, width), F32),
            pltpu.VMEM((3, 2, 2, rows // 2, width), BF16),
            pltpu.VMEM((chunks, 2, 2, rows // 2, width), BF16),
            pltpu.VMEM((3, 2, rows // 2, width), BF16),
            pltpu.VMEM((chunks, 2, rows // 2, width), BF16),
            dma((2, chunks)),
            dma((2, chunks)),
            dma((2, chunks)),
            dma((2, chunks)),
        ]


def scan_rows_back(decay, source, state, product, carry):
    planes, rows, _ = decay.shape
    seg = rows // 8

    def first(n, held):
        j = seg - 1 - n
        out = []
        for q in range(planes):
            now, prod = held[q]
            here = pl.ds(j, 8, stride=seg)
            d = decay[q, here, :]
            now = source[q, here, :] + now
            state[q, here, :] = now
            product[q, here, :] = prod
            out.append((d * now, d * prod))
        return tuple(out)

    zero, one = jnp.zeros((8, LANES), F32), jnp.ones((8, LANES), F32)
    ends = lax.fori_loop(0, seg, first, ((zero, one),) * planes, unroll=4)
    entries = []
    for q in range(planes):
        last, prod = ends[q]
        value = carry[q, 0:1, :]
        parts = []
        for s in range(7, -1, -1):
            parts.append(value)
            value = prod[s : s + 1] * value + last[s : s + 1]
        entries.append(jnp.concatenate(parts[::-1], axis=0))
        carry[q, 0:1, :] = value

    def second(j, held):
        for q in range(planes):
            here = pl.ds(j, 8, stride=seg)
            state[q, here, :] += product[q, here, :] * entries[q]
        return held

    lax.fori_loop(0, seg, second, 0, unroll=4)


def fold_rows(value):
    return value[0:8] + value[8:16] + value[16:24] + value[24:32]


STAGES = 4
SITES = (1, 1, 1, 1, 1, 1, 1, 1)


def spend(chain, base, sites, n):
    each(sites[n], lambda j: chain.tick(base + sum(sites[:n]) + j))


def back_kernel(
    dp, units,
    g_both, w_gate, w_up, w_out, gains, gain_gate, lower,
    cot, mix, tok, scale_mid, scale_gate, pre_in, pre_for, pre_gp, state, diff, d_both, peer,
    g_mix, g_resid, g_pre, mixed, inner, sums_out, total_both, low_part, high_part,
    vboth, vout, full, line, dots, gm, dec, src, prod, adj, carry, sum_mid, sum_gate, sum_low,
    share, keep, out1, in1, out2, in2, send1, recv1, send2, recv2, send, recv, lsem,
    buf, *sems,
):
    chain = Chain([d_both], units, [total_both], [low_part], [high_part], [peer], buf, sems, dp)
    s = pl.program_id(0)
    chunks = pl.num_programs(0) - STAGES
    rows, width = g_resid.shape
    feats = full.shape[1]
    hid = w_gate.shape[1]
    t, xn, yn, dg = neighbours()
    peers = ({"tensor": xn}, {"tensor": yn})
    base = s * sum(SITES)
    gather = Gather(None, full, send, recv, rows, width)
    scatter = Scatter(share, keep, out1, in1, out2, in2, (send1, recv1, send2, recv2))
    loads = (
        pltpu.make_async_copy(w_gate, vboth.at[:, 0:hid], lsem.at[0]),
        pltpu.make_async_copy(w_up, vboth.at[:, hid : 2 * hid], lsem.at[1]),
        pltpu.make_async_copy(w_out, vout, lsem.at[2]),
    )

    def place(c):
        return chunks - 1 - c

    def at_stage(n, act):
        @pl.when((s >= n) & (s - n < chunks))
        def _():
            act(s - n)

    @pl.when(s == 0)
    def _():
        for load in loads:
            load.start()
        greet(peers + tuple(chain.near()))
        carry[...] = jnp.zeros(carry.shape, F32)
        sum_mid[...] = jnp.zeros(sum_mid.shape, F32)
        sum_gate[...] = jnp.zeros(sum_gate.shape, F32)
        sum_low[...] = jnp.zeros(sum_low.shape, F32)
        for load in loads:
            load.wait()

    spend(chain, base, SITES, 0)
    at_stage(3, lambda c: gather.forward(place(c)))

    def summed(c):
        def use(i, value):
            full[block(place(c) * (rows // 32) + i, 32), block(t, width)] = value.astype(BF16)

        scatter.end(c, use)
        gather.start(place(c))

    at_stage(2, summed)
    spend(chain, base, SITES, 1)
    at_stage(1, scatter.middle)
    spend(chain, base, SITES, 2)

    def terms(c, part):
        for b in (2 * part, 2 * part + 1):
            share[b] = back_dot(g_both[...], vboth[b * width : (b + 1) * width, :])

    at_stage(0, lambda c: terms(c, 0))
    spend(chain, base, SITES, 3)

    def last_terms(c):
        terms(c, 1)
        scatter.begin(c)

    at_stage(0, last_terms)
    spend(chain, base, SITES, 4)
    gain_mid = gains[1:2, :]
    gain = gain_gate[...]
    low = lower[...]

    def finish(c):
        p = place(c)
        gather.finish(p)

        def resid_rows(i):
            here = block(i, 32)
            g = full[block(p * (rows // 32) + i, 32), :].astype(F32)
            m = mix[here, :].astype(F32)
            r = tok[here, :].astype(F32) + m
            mid = scale_mid[here, 0:1]
            weighted = g * gain_mid
            total = jnp.sum(weighted * r, axis=1, keepdims=True) / feats
            grad = cot[here, :].astype(F32) + mid * weighted - r * (mid * mid * mid * total)
            low_grad = grad.astype(BF16)
            g_mix[here, :] = low_grad
            line[...] = grad
            g_resid[here, :] = line[:, block(t, width)]
            dots[here, :] = jnp.broadcast_to(
                jnp.sum(low_grad.astype(F32) * m, axis=1, keepdims=True), (32, 128)
            )
            sum_mid[...] += fold_rows(g * r * mid)

        each(rows // 32, resid_rows)
        gm[...] = back_dot(g_mix[...], vout[...])

    at_stage(STAGES, finish)
    spend(chain, base, SITES, 5)

    def finish_states(c):
        def state_rows(i):
            here = block(i, 32)
            h = state[here, :]
            scale = scale_gate[here, 0:1]
            ns = h * scale
            gp = pre_gp[here, :]
            sigma = jax.nn.sigmoid(gp)
            swish = gp * sigma
            grad = gm[here, :]
            sum_gate[...] += fold_rows(grad * ns * swish)
            g_pre[here, 2 * width :] = (grad * ns * gain * (sigma * (1.0 + gp * (1.0 - sigma)))).astype(BF16)
            mixed[here, :] = (ns * gain * swish).astype(BF16)
            factor = scale * scale * dots[here, 0:1] / feats
            to_planes(src, here, scale * (grad * gain * swish) - h * factor)
            to_planes(dec, here, low + (1.0 - low) * jax.nn.sigmoid(pre_for[here, :]))

        each(rows // 32, state_rows)
        scan_rows_back(dec, src, adj, prod, carry)

    at_stage(STAGES, finish_states)
    spend(chain, base, SITES, 6)

    def finish_gates(c):
        def gate_rows(i):
            here = block(i, 32)
            a = from_planes(adj, here)
            x, f = pre_in[here, :], pre_for[here, :]
            sig = jax.nn.sigmoid(f)
            decay = low + (1.0 - low) * sig
            grad_decay = a * diff[here, :]
            gi = (a * (1.0 - decay) * silu_slope(x)).astype(BF16)
            gf = (grad_decay * (1.0 - low) * sig * (1.0 - sig)).astype(BF16)
            g_pre[here, 0:width] = gi
            g_pre[here, width : 2 * width] = gf
            sum_low[...] += fold_rows(grad_decay * (1.0 - sig))
            gm[here, :] = (
                gi.astype(F32) * x + gf.astype(F32) * f + g_pre[here, 2 * width :].astype(F32) * pre_gp[here, :]
            )

        each(rows // 32, gate_rows)
        inner[0] = rows_to_lanes(gm[...])

    at_stage(STAGES, finish_gates)
    spend(chain, base, SITES, 7)

    @pl.when(s == pl.num_programs(0) - 1)
    def _():
        each(chunks, gather.drain)
        scatter.drain(BACK)
        chain.close(base + sum(SITES))
        sums_out[0] = sum_mid[:, block(t, width)]
        sums_out[1] = sum_gate[...]
        sums_out[2] = sum_low[...]


def backward(
    dp, d_both, peer, g_both, w_gate, w_up, w_out, gains, gain_gate, lower,
    cot, mix, tok, scale_mid, scale_gate, pre_in, pre_for, pre_gp, state, diff,
):
    total, hid = g_both.shape[0], w_gate.shape[1]
    unit = 16
    units = (d_both.shape[0] // (2 * unit),)
    feats, width = mix.shape[1], pre_in.shape[1]
    rows = total // BACK

    def early(s):
        return (BACK - 1 - jnp.minimum(s, BACK - 1), 0)

    def late(s):
        return (BACK - 1 - jnp.maximum(s - STAGES, 0), 0)

    def out(n, dtype):
        return jax.ShapeDtypeStruct((total, n), dtype), pl.BlockSpec((rows, n), late)

    outs = [
        out(feats, BF16),
        out(width, F32),
        out(3 * width, BF16),
        out(width, BF16),
        (
            jax.ShapeDtypeStruct((BACK, 8, rows), F32),
            pl.BlockSpec((1, 8, rows), lambda s: late(s) + (0,)),
        ),
        (jax.ShapeDtypeStruct((3, 8, width), F32), WHOLE),
    ] + [(jax.ShapeDtypeStruct(d_both.shape, BF16), ANY)] * 3
    planes = width // LANES
    dma = pltpu.SemaphoreType.DMA
    return pl.pallas_call(
        functools.partial(back_kernel, dp, units),
        grid=(BACK + STAGES,),
        out_shape=[o[0] for o in outs],
        out_specs=[o[1] for o in outs],
        in_specs=[
            pl.BlockSpec((rows, 2 * hid), early),
            ANY, ANY, ANY, WHOLE, WHOLE, WHOLE,
            pl.BlockSpec((rows, feats), late),
            pl.BlockSpec((rows, feats), late),
            pl.BlockSpec((rows, feats), late),
            pl.BlockSpec((rows, 128), late),
            pl.BlockSpec((rows, 128), late),
        ]
        + [pl.BlockSpec((rows, width), late)] * 5
        + [ANY, ANY],
        scratch_shapes=[
            pltpu.VMEM((feats, 2 * hid), BF16),
            pltpu.VMEM((width, feats), BF16),
            pltpu.VMEM((total, feats), BF16),
            pltpu.VMEM((32, feats), F32),
            pltpu.VMEM((rows, 128), F32),
            pltpu.VMEM((rows, width), F32),
            pltpu.VMEM((planes, rows, LANES), F32),
            pltpu.VMEM((planes, rows, LANES), F32),
            pltpu.VMEM((planes, rows, LANES), F32),
            pltpu.VMEM((planes, rows, LANES), F32),
            pltpu.VMEM((planes, 8, LANES), F32),
            pltpu.VMEM((8, feats), F32),
            pltpu.VMEM((8, width), F32),
            pltpu.VMEM((8, width), F32),
        ]
        + Scatter.scratch(BACK, rows, width)
        + [dma((4, BACK)), dma((4, BACK)), dma((3,))]
        + Chain.scratch(2 * hid, unit, units),
        compiler_params=pltpu.CompilerParams(
            collective_id=3, has_side_effects=True, vmem_limit_bytes=VMEM_BYTES
        ),
        name="backward",
    )(
        g_both, w_gate, w_up, w_out, gains, gain_gate, lower,
        cot, mix, tok, scale_mid, scale_gate, pre_in, pre_for, pre_gp, state, diff, d_both, peer,
    )


KW_HOOK = 2
KW_TICKS = 4 + 4 * KW_HOOK


def ffn_grad_kernel(
    dp, units,
    hidden, w_down, g_both, cot, normed, resid,
    out, total_down, d_both, peer_both, d_down, peer_down, low_part, high_part,
    vhid, vdown, vg,
    share, keep, out1, in1, out2, in2, send1, recv1, send2, recv2, lsem,
    lbuf, xbuf, stage, tsem0, tsem1, tsem2, tsem3, buf, *sems,
):
    s = pl.program_id(0)
    chunks = pl.num_programs(0) - 2
    rows, width = out.shape
    feats = vdown.shape[1]
    hid = vhid.shape[1]
    t, xn, yn, dg = neighbours()
    peers = ({"tensor": xn}, {"tensor": yn})
    scatter = Scatter(share, keep, out1, in1, out2, in2, (send1, recv1, send2, recv2))
    loads = (
        pltpu.make_async_copy(hidden, vhid, lsem.at[0]),
        pltpu.make_async_copy(w_down, vdown, lsem.at[1]),
        pltpu.make_async_copy(g_both, vg, lsem.at[2]),
    )
    tiles = Tiles(
        (cot, normed), (vhid, vg), (lambda: None, loads[2].wait), (d_down, d_both), (peer_down, peer_both),
        lbuf, xbuf, stage, (tsem0, tsem1, tsem2, tsem3),
    )
    chain = Chain([d_down], units, [total_down], [low_part], [high_part], [peer_down], buf, sems, dp)

    def at_stage(n, act):
        @pl.when((s >= n) & (s - n < chunks))
        def _():
            act(s - n)

    @pl.when(s == 0)
    def _():
        for load in loads:
            load.start()
        tiles.begin()
        greet(peers + tuple(chain.near()))
        loads[0].wait()
        loads[1].wait()

    base = (s - 1) * KW_TICKS - 4

    def terms(c):
        def part(b):
            share[b] = plain_dot(vhid[block(c, rows), :], vdown[:, block(b, width)])
            chain.tick(base + b)

        each(feats // width, part)
        scatter.begin(c)

    def finish(c):
        def give(i, value):
            here = block(i, 32)
            out[here, :] = (resid[here, :] + value).astype(BF16)

        scatter.end(c, give)

    at_stage(2, finish)
    at_stage(1, scatter.middle)
    at_stage(0, terms)

    @pl.when(s >= chunks)
    def _():
        each(4, lambda j: chain.tick(base + j))

    tiles.work(s, lambda k: each(KW_HOOK, lambda j: chain.tick(base + 4 + KW_HOOK * k + j)))

    @pl.when(s == pl.num_programs(0) - 1)
    def _():
        scatter.drain(CHUNKS)
        chain.close(base + KW_TICKS)


def ffn_grads(dp, hidden, w_down, g_both, cot, normed, resid):
    total, hid = hidden.shape
    feats, width = w_down.shape[1], resid.shape[1]
    rows = total // CHUNKS
    unit = 16
    units = (feats // (2 * unit),)

    def late(s):
        return (jnp.maximum(s - 2, 0), 0)

    far = pl.BlockSpec((rows, width), late)
    down = jax.ShapeDtypeStruct((feats, hid), BF16)
    both = jax.ShapeDtypeStruct((feats, 2 * hid), BF16)
    dma = pltpu.SemaphoreType.DMA
    return pl.pallas_call(
        functools.partial(ffn_grad_kernel, dp, units),
        grid=(CHUNKS + 2,),
        out_shape=[jax.ShapeDtypeStruct((total, width), BF16), down, both, both, down, down, down, down],
        out_specs=[far] + [ANY] * 7,
        in_specs=[ANY] * 5 + [far],
        scratch_shapes=[
            pltpu.VMEM((total, hid), BF16),
            pltpu.VMEM((hid, feats), BF16),
            pltpu.VMEM((total, 2 * hid), BF16),
        ]
        + Scatter.scratch(CHUNKS, rows, width)
        + [dma((3,))]
        + Tiles.scratch(total, 2 * hid, feats // TILE)
        + Chain.scratch(hid, unit, units),
        compiler_params=pltpu.CompilerParams(
            collective_id=5, has_side_effects=True, vmem_limit_bytes=VMEM_BYTES
        ),
        name="ffn_grads",
    )(hidden, w_down, g_both, cot, normed, resid)


LAST_PAIRS = 2
LAST_TICKS = 14


def last_kernel(
    dp, units,
    g_pre, w_in, w_for, w_gp, g_mix, normed, mixed, inner, gain_in, sums_in, tok, scale_in, g_resid,
    g_tok, small, total_pre, total_out, d_pre, d_out, peer_pre, peer_out, low_pre, low_out, high_pre, high_out,
    vg, vpre, vmix, ibuf, col, sum_in, mine, others,
    share, keep, out1, in1, out2, in2, send1, recv1, send2, recv2,
    isend, irecv, lsem, osend, orecv,
    lbuf, xbuf, stage, tsem0, tsem1, tsem2, tsem3, buf, *sems,
):
    me = lax.axis_index("dp")
    s = pl.program_id(0)
    chunks = pl.num_programs(0) - 2
    rows, width = g_tok.shape
    feats = w_in.shape[0]
    t, xn, yn, dg = neighbours()
    peers = ({"tensor": xn}, {"tensor": yn}, {"tensor": dg})
    scatter = Scatter(share, keep, out1, in1, out2, in2, (send1, recv1, send2, recv2))

    def inner_copy(k):
        return pltpu.make_async_remote_copy(
            inner, ibuf.at[t], isend.at[k], irecv.at[k], device_id=peers[k], device_id_type=MESH
        )

    def other(d):
        return pltpu.make_async_remote_copy(
            mine, others.at[me], osend.at[d], orecv.at[d],
            device_id={"dp": (me + d) % dp}, device_id_type=MESH,
        )

    loads = (
        pltpu.make_async_copy(g_pre, vg, lsem.at[0]),
        pltpu.make_async_copy(w_in, vpre.at[:, 0:width], lsem.at[1]),
        pltpu.make_async_copy(w_for, vpre.at[:, width : 2 * width], lsem.at[2]),
        pltpu.make_async_copy(w_gp, vpre.at[:, 2 * width :], lsem.at[3]),
        pltpu.make_async_copy(inner, ibuf.at[t], lsem.at[4]),
        pltpu.make_async_copy(g_mix, vmix, lsem.at[5]),
    )
    tiles = Tiles(
        (normed, mixed), (vg, vmix), (lambda: None, loads[5].wait), (d_pre, d_out), (peer_pre, peer_out),
        lbuf, xbuf, stage, (tsem0, tsem1, tsem2, tsem3),
    )
    chain = Chain(
        [d_pre, d_out], units, [total_pre, total_out], [low_pre, low_out], [high_pre, high_out],
        [peer_pre, peer_out], buf, sems, dp,
    )

    def at_stage(n, act):
        @pl.when((s >= n) & (s - n < chunks))
        def _():
            act(s - n)

    @pl.when(s == 0)
    def _():
        for load in loads:
            load.start()
        tiles.begin()
        greet(peers + tuple({"dp": (me + d) % dp} for d in range(1, dp)))
        for k in range(3):
            inner_copy(k).start()
        sum_in[...] = jnp.zeros(sum_in.shape, F32)
        for load in loads[:5]:
            load.wait()

    @pl.when(s == 2)
    def _():
        for k in range(3):
            inner_copy(k).wait_recv()

    def finish(c):
        total = ibuf[0, c] + ibuf[1, c] + ibuf[2, c] + ibuf[3, c]
        col[...] = jnp.broadcast_to(lanes_to_rows(total) / feats, (rows, 128))
        gain = gain_in[...]

        def give(i, value):
            here = block(i, 32)
            x = tok[here, :].astype(F32)
            scale = scale_in[here, 0:1]
            g_tok[here, :] = (
                g_resid[here, :] + scale * (value * gain) - x * (scale * scale * col[here, 0:1])
            )
            sum_in[...] += fold_rows(value * x * scale)

        scatter.end(c, give)

    base = (s - 1) * LAST_TICKS

    def terms(c):
        def part(b):
            share[b] = back_dot(vg[block(c, rows), :], vpre[block(b, width), :])
            chain.tick(base + 2 + b)

        each(feats // width, part)
        scatter.begin(c)

    at_stage(2, finish)
    chain.tick(base)
    at_stage(1, scatter.middle)
    chain.tick(base + 1)
    at_stage(0, terms)

    @pl.when(s >= chunks)
    def _():
        each(4, lambda j: chain.tick(base + 2 + j))

    each(LAST_PAIRS, lambda j: tiles.work(s * LAST_PAIRS + j, lambda k: chain.tick(base + 6 + 4 * j + k)))

    @pl.when(s == pl.num_programs(0) - 1)
    def _():
        mine[...] = jnp.zeros(mine.shape, F32)
        mine[0:1, :] = jnp.sum(sum_in[...], axis=0, keepdims=True)
        for k in range(3):
            mine[1 + k : 2 + k, :] = jnp.sum(sums_in[k], axis=0, keepdims=True)
        scatter.drain(CHUNKS)
        for d in range(1, dp):
            other(d).start()
        chain.close(base + LAST_TICKS)
        others[me] = mine[...]
        for d in range(1, dp):
            other(d).wait()
        total = others[0]
        for d in range(1, dp):
            total += others[d]
        small[...] = total
        for k in range(3):
            inner_copy(k).wait_send()


def last_sums(dp, g_pre, w_in, w_for, w_gp, g_mix, normed, mixed, inner, gain_in, sums, tok, scale_in, g_resid):
    feats, width = w_in.shape
    total = g_pre.shape[0]
    rows = total // CHUNKS
    unit = 16
    pre = jax.ShapeDtypeStruct((feats, 3 * width), BF16)
    mix = jax.ShapeDtypeStruct((width, feats), BF16)
    units = (feats // (2 * unit), width // (2 * unit))

    def late(s):
        return (jnp.maximum(s - 2, 0), 0)

    far = pl.BlockSpec((rows, width), late)
    dma = pltpu.SemaphoreType.DMA
    return pl.pallas_call(
        functools.partial(last_kernel, dp, units),
        grid=(CHUNKS + 2,),
        out_shape=[jax.ShapeDtypeStruct((total, width), F32), jax.ShapeDtypeStruct((8, width), F32)]
        + [pre, mix] * 5,
        out_specs=[far, WHOLE] + [ANY] * 10,
        in_specs=[ANY] * 7 + [WHOLE, WHOLE, WHOLE, far, pl.BlockSpec((rows, 128), late), far],
        scratch_shapes=[
            pltpu.VMEM((total, 3 * width), BF16),
            pltpu.VMEM((feats, 3 * width), BF16),
            pltpu.VMEM((total, feats), BF16),
            pltpu.VMEM((4, CHUNKS, 8, rows), F32),
            pltpu.VMEM((rows, 128), F32),
            pltpu.VMEM((8, width), F32),
            pltpu.VMEM((8, width), F32),
            pltpu.VMEM((dp, 8, width), F32),
        ]
        + Scatter.scratch(CHUNKS, rows, width)
        + [dma((3,)), dma((3,)), dma((6,)), dma((dp,)), dma((dp,))]
        + Tiles.scratch(total, feats, feats // (2 * TILE) + width // (2 * TILE))
        + Chain.scratch(feats, unit, units),
        compiler_params=pltpu.CompilerParams(
            collective_id=4, has_side_effects=True, vmem_limit_bytes=VMEM_BYTES
        ),
        name="last_sums",
    )(g_pre, w_in, w_for, w_gp, g_mix, normed, mixed, inner, gain_in, sums, tok, scale_in, g_resid)


def turn_kernel(value, out):
    def part(k):
        rows = block(k, LANES)
        out[rows, :] = value[:, rows].T.astype(F32)

    each(out.shape[0] // LANES, part)


def turned(value):
    rows, cols = value.shape
    return pl.pallas_call(
        turn_kernel,
        grid=(rows // TILE,),
        out_shape=jax.ShapeDtypeStruct((cols, rows), F32),
        in_specs=[pl.BlockSpec((TILE, cols), lambda s: (s, 0))],
        out_specs=pl.BlockSpec((cols, TILE), lambda s: (0, s)),
        name="turned",
    )(value)


def on_device(
    dp, tokens, lengths, cotangent, w_norm_in, w_input, w_forget, w_gproj, lower_bound, w_gate_norm,
    w_output, w_norm_mid, w_gate, w_up, w_down,
):
    channels, hid = w_input.shape[1], w_gate.shape[1]
    gain_in = w_norm_in.astype(F32)[None]
    gains = jnp.concatenate([gain_in, w_norm_mid.astype(F32)[None], jnp.zeros((6, channels), F32)], 0)
    lower = lower_bound.astype(F32)[None]
    gain_gate = w_gate_norm.astype(F32)[None]
    (
        normed_in, tok_full, wout_full, gains_full, scale_in, pre_in, pre_for, pre_gp, state, diff, raw, squares,
    ) = mixer_forward(tokens, w_output, gains, w_input, w_forget, w_gproj, lower, gain_gate)
    normed_mid, hidden, g_both, cot, mix, scale_gate, scale_mid, resid = ffn_forward(
        lengths, raw, cotangent, squares, gains_full, tok_full, wout_full, w_gate, w_up, w_down
    )
    output, s_down, d_both, peer_both = ffn_grads(dp, hidden, w_down, g_both, cot, normed_mid, resid)[:4]
    g_mix, g_resid, g_pre, mixed, inner, sums, s_both = backward(
        dp, d_both, peer_both, g_both, w_gate, w_up, w_output, gains_full, gain_gate, lower,
        cot, mix, tok_full, scale_mid, scale_gate, pre_in, pre_for, pre_gp, state, diff,
    )[:7]
    if BACK != CHUNKS:
        inner = inner.reshape(CHUNKS, BACK // CHUNKS, 8, -1).swapaxes(1, 2).reshape(CHUNKS, 8, -1)
    g_tok, small, s_pre, s_out = last_sums(
        dp, g_pre, w_input, w_forget, w_gproj, g_mix, normed_in, mixed, inner, gain_in, sums, tokens, scale_in, g_resid
    )[:4]
    pre = [s_pre[:, k * channels : (k + 1) * channels].astype(F32) for k in range(3)]
    return (
        output, g_tok, small[0], pre[0], pre[1], pre[2], small[3], small[2], s_out.astype(F32), small[1],
        s_both[:, :hid].astype(F32), s_both[:, hid:].astype(F32), turned(s_down),
    )


D = 2048
SLOTS = 2048


def linear_scan(decay, source):

    def compose(earlier, later):
        return (earlier[0] * later[0], later[0] * earlier[1] + later[1])

    return lax.associative_scan(compose, (decay, source), axis=1)[1]


def any_plane(
    tokens,
    lengths,
    cotangent,
    w_norm_in,
    w_input,
    w_forget,
    w_gproj,
    lower_bound,
    w_gate_norm,
    w_output,
    w_norm_mid,
    w_gate,
    w_up,
    w_down,
):
    row_count = tokens.shape[0]
    seq_count = row_count // SLOTS
    channels = w_input.shape[1]
    block_shape = (seq_count, SLOTS, channels)
    gathered, gain_rows = (
        lax.all_gather(tokens, "tensor", axis=1, tiled=True),
        lax.all_gather(w_norm_in[None, :], "tensor", axis=1, tiled=True),
    )
    whole_rows = gathered.astype(jnp.float32)
    gain_in_full = gain_rows[0].astype(jnp.float32)
    scale_in = lax.rsqrt(jnp.mean(whole_rows * whole_rows, axis=1, keepdims=True) + EPSILON)
    normed_in = (whole_rows * scale_in * gain_in_full).astype(jnp.bfloat16)
    in_pre = plain_dot(normed_in, w_input)
    forget_pre = plain_dot(normed_in, w_forget)
    gate_pre = plain_dot(normed_in, w_gproj)
    inner = jax.nn.silu(in_pre)
    forget_sig = jax.nn.sigmoid(forget_pre)
    lower = lower_bound.astype(jnp.float32)
    decay = lower + (1.0 - lower) * forget_sig
    decay_blocks = decay.reshape(block_shape)
    state = linear_scan(decay_blocks, ((1.0 - decay) * inner).reshape(block_shape)).reshape(
        row_count, channels
    )
    state_total = lax.psum(jnp.sum(state * state, axis=1), "tensor")
    gate_scale = lax.rsqrt(state_total / D + EPSILON)[:, None]
    normed_state = state * gate_scale
    swish_gate = jax.nn.silu(gate_pre)
    gain_gate = w_gate_norm.astype(jnp.float32)
    mixed = (normed_state * gain_gate * swish_gate).astype(jnp.bfloat16)
    mix_share = lax.psum_scatter(
        plain_dot(mixed, w_output), "tensor", scatter_dimension=1, tiled=True
    )
    token_share = tokens.astype(jnp.float32)
    resid = token_share + mix_share
    resid_total = lax.psum(jnp.sum(resid * resid, axis=1), "tensor")
    scale_mid = lax.rsqrt(resid_total / D + EPSILON)[:, None]
    gain_mid = w_norm_mid.astype(jnp.float32)
    normed_part = (resid * scale_mid * gain_mid).astype(jnp.bfloat16)
    normed_mid = lax.all_gather(normed_part, "tensor", axis=1, tiled=True)
    ffn_gate = plain_dot(normed_mid, w_gate)
    ffn_up = plain_dot(normed_mid, w_up)
    gate_act = jax.nn.silu(ffn_gate)
    hidden = (gate_act * ffn_up).astype(jnp.bfloat16)
    ffn_share = lax.psum_scatter(
        plain_dot(hidden, w_down).astype(jnp.bfloat16), "tensor", scatter_dimension=1, tiled=True
    ).astype(jnp.float32)
    output = (resid + ffn_share).astype(jnp.bfloat16)
    positions = jnp.arange(SLOTS, dtype=jnp.int32)
    valid = (positions[None, :] < lengths[:, None]).reshape(row_count, 1)
    masked_cot = cotangent * valid.astype(jnp.bfloat16)
    cot_full = lax.all_gather(masked_cot, "tensor", axis=1, tiled=True)
    grad_down_w = trans_dot(hidden, cot_full)
    grad_hidden = back_dot(cot_full, w_down)
    grad_ffn_gate = (grad_hidden * ffn_up * silu_slope(ffn_gate)).astype(jnp.bfloat16)
    grad_ffn_up = (grad_hidden * gate_act).astype(jnp.bfloat16)
    grad_gate_w = trans_dot(normed_mid, grad_ffn_gate)
    grad_up_w = trans_dot(normed_mid, grad_ffn_up)
    grad_normed_mid = lax.psum_scatter(
        back_dot(grad_ffn_gate, w_gate) + back_dot(grad_ffn_up, w_up),
        "tensor",
        scatter_dimension=1,
        tiled=True,
    )
    grad_gain_mid = jnp.sum(grad_normed_mid * resid * scale_mid, axis=0)
    weighted_mid = grad_normed_mid * gain_mid
    mid_total = lax.psum(jnp.sum(weighted_mid * resid, axis=1), "tensor")
    grad_resid = (
        masked_cot.astype(jnp.float32)
        + scale_mid * weighted_mid
        - resid * scale_mid**3 * (mid_total / D)[:, None]
    )
    ffn_terms = (grad_gain_mid, grad_gate_w, grad_up_w, grad_down_w)
    grad_mix = lax.all_gather(grad_resid.astype(jnp.bfloat16), "tensor", axis=1, tiled=True)
    grad_output_w = trans_dot(mixed, grad_mix)
    grad_mixed = back_dot(grad_mix, w_output)
    grad_gain_gate = jnp.sum(grad_mixed * normed_state * swish_gate, axis=0)
    grad_gate_pre = (grad_mixed * normed_state * gain_gate * silu_slope(gate_pre)).astype(
        jnp.bfloat16
    )
    grad_normed_state = grad_mixed * gain_gate * swish_gate
    state_inner = lax.psum(jnp.sum(grad_normed_state * state, axis=1), "tensor")
    grad_state = gate_scale * grad_normed_state - state * gate_scale**3 * (state_inner / D)[:, None]
    state_blocks = state.reshape(block_shape)
    next_decay = jnp.concatenate(
        [decay_blocks[:, 1:], jnp.zeros((seq_count, 1, channels), jnp.float32)], axis=1
    )
    adjoint = jnp.flip(
        linear_scan(jnp.flip(next_decay, 1), jnp.flip(grad_state.reshape(block_shape), 1)), 1
    ).reshape(row_count, channels)
    prev_state = jnp.concatenate(
        [jnp.zeros((seq_count, 1, channels), jnp.float32), state_blocks[:, :-1]], axis=1
    ).reshape(row_count, channels)
    grad_decay = adjoint * (prev_state - inner)
    grad_in_pre = (adjoint * (1.0 - decay) * silu_slope(in_pre)).astype(jnp.bfloat16)
    grad_forget_pre = (grad_decay * (1.0 - lower) * forget_sig * (1.0 - forget_sig)).astype(
        jnp.bfloat16
    )
    grad_lower = jnp.sum(grad_decay * (1.0 - forget_sig), axis=0)
    grad_input_w = trans_dot(normed_in, grad_in_pre)
    grad_forget_w = trans_dot(normed_in, grad_forget_pre)
    grad_gproj_w = trans_dot(normed_in, grad_gate_pre)
    grad_normed_in = lax.psum_scatter(
        (
            back_dot(grad_in_pre, w_input)
            + back_dot(grad_forget_pre, w_forget)
            + back_dot(grad_gate_pre, w_gproj)
        ).astype(jnp.bfloat16),
        "tensor",
        scatter_dimension=1,
        tiled=True,
    ).astype(jnp.float32)
    gain_in_share = w_norm_in.astype(jnp.float32)
    grad_gain_in = jnp.sum(grad_normed_in * token_share * scale_in, axis=0)
    weighted_in = grad_normed_in * gain_in_share
    in_total = lax.psum(jnp.sum(weighted_in * token_share, axis=1), "tensor")
    grad_tokens = (
        grad_resid + scale_in * weighted_in - token_share * scale_in**3 * (in_total / D)[:, None]
    )
    mixer_terms = (
        grad_gain_in,
        grad_input_w,
        grad_forget_w,
        grad_gproj_w,
        grad_lower,
        grad_gain_gate,
        grad_output_w,
    )
    summed = lax.psum(mixer_terms + ffn_terms, "dp")
    mixer_terms = summed[:7]
    ffn_terms = summed[7:]
    return (
        output,
        grad_tokens,
        mixer_terms[0],
        mixer_terms[1],
        mixer_terms[2],
        mixer_terms[3],
        mixer_terms[4],
        mixer_terms[5],
        mixer_terms[6],
        ffn_terms[0],
        ffn_terms[1],
        ffn_terms[2],
        ffn_terms[3],
    )


def solution(mesh):
    rows, cols, vec = P(None, "tensor"), P("tensor", None), P("tensor")
    both = P("dp", "tensor")
    in_specs = (both, P("dp"), both, vec, rows, rows, rows, vec, vec, cols, vec, rows, rows, cols)
    out_specs = (both, both, vec, rows, rows, rows, vec, vec, cols, vec, rows, rows, cols)
    square = mesh.shape["tensor"] == 4 and mesh.shape["dp"] % 2 == 0
    body = functools.partial(on_device, mesh.shape["dp"]) if square else any_plane
    return jax.shard_map(
        body, mesh=mesh, in_specs=in_specs, out_specs=out_specs,
        check_vma=False,
    )
```

```python
import functools

import jax
import jax.numpy as jnp
from jax import lax
from jax.experimental import pallas as pl
from jax.experimental.pallas import tpu as pltpu
from jax.sharding import PartitionSpec as P

EPSILON = 1e-06
MESH = pl.DeviceIdType.MESH
CHUNKS = 8
FRONT = 16
BACK = 8
AHEAD = 2
VMEM_BYTES = 67_000_000
F32 = jnp.float32
BF16 = jnp.bfloat16
ANY = pl.BlockSpec(memory_space=pl.ANY)
WHOLE = pl.BlockSpec(memory_space=pltpu.VMEM)


def silu_slope(value):
    sigma = jax.nn.sigmoid(value)
    return sigma * (1.0 + value * (1.0 - sigma))


def plain_dot(left, right):
    return jnp.dot(left, right, preferred_element_type=F32)


def trans_dot(left, right):
    return lax.dot_general(left, right, (((0,), (0,)), ((), ())), preferred_element_type=F32)


def back_dot(left, right):
    return lax.dot_general(left, right, (((1,), (1,)), ((), ())), preferred_element_type=F32)


def rows_to_lanes(values):
    ones = jnp.ones((8, values.shape[1]), F32)
    return lax.dot_general(
        ones, values, (((1,), (1,)), ((), ())), precision=lax.Precision.HIGHEST,
        preferred_element_type=F32,
    )


def lanes_to_rows(values):
    ones = jnp.full((8, 128), 0.125, F32)
    wide = lax.dot_general(
        values, ones, (((0,), (0,)), ((), ())), precision=lax.Precision.HIGHEST,
        preferred_element_type=F32,
    )
    return wide[:, :1]


def neighbours():
    t = lax.axis_index("tensor")
    return t, t + 1 - 2 * (t % 2), t + 2 - 4 * (t // 2), 3 - t


def block(start, size):
    return pl.ds(pl.multiple_of(start * size, size), size)


def greet(devices):
    barrier = pltpu.get_barrier_semaphore()
    for device in devices:
        pl.semaphore_signal(barrier, inc=1, device_id=device, device_id_type=MESH)
    pl.semaphore_wait(barrier, len(devices))


def each(count, step):
    def body(i, carry):
        step(i)
        return carry

    lax.fori_loop(0, count, body, 0)


class Gather:
    def __init__(self, source, full, send, recv, rows, width):
        self.source, self.full, self.send, self.recv = source, full, send, recv
        self.rows, self.width = rows, width
        self.t, self.xn, self.yn, self.dg = neighbours()

    def direct(self, c, k):
        rows = block(c, self.rows)
        place = self.full.at[rows, block(self.t, self.width)]
        return pltpu.make_async_remote_copy(
            place if self.source is None else self.source.at[rows, :],
            place,
            self.send.at[k, c],
            self.recv.at[k, c],
            device_id={"tensor": self.xn if k == 0 else self.yn},
            device_id_type=MESH,
        )

    def relay(self, c, k):
        rows = block(2 * c + k, self.rows // 2)
        part = self.full.at[rows, block(self.xn if k == 0 else self.yn, self.width)]
        return pltpu.make_async_remote_copy(
            part,
            part,
            self.send.at[2 + k, c],
            self.recv.at[2 + k, c],
            device_id={"tensor": self.yn if k == 0 else self.xn},
            device_id_type=MESH,
        )

    def start(self, c):
        self.direct(c, 0).start()
        self.direct(c, 1).start()

    def forward(self, c):
        for k in range(2):
            self.direct(c, k).wait_recv()
            self.relay(c, k).start()

    def finish(self, c):
        self.relay(c, 0).wait_recv()
        self.relay(c, 1).wait_recv()

    def drain(self, c):
        for k in range(2):
            self.direct(c, k).wait_send()
            self.relay(c, k).wait_send()


LANES = 128


def scan_rows(decay, source, state, product, head):
    planes, rows, _ = decay.shape
    seg = rows // 8

    def first(j, held):
        out = []
        for q in range(planes):
            now, prod = held[q]
            d = decay[q, pl.ds(j, 8, stride=seg), :]
            now = d * now + source[q, pl.ds(j, 8, stride=seg), :]
            prod = d * prod
            state[q, pl.ds(head + j, 8, stride=seg), :] = now
            product[q, pl.ds(j, 8, stride=seg), :] = prod
            out.append((now, prod))
        return tuple(out)

    zero, one = jnp.zeros((8, LANES), F32), jnp.ones((8, LANES), F32)
    ends = lax.fori_loop(0, seg, first, ((zero, one),) * planes, unroll=4)
    entries = []
    for q in range(planes):
        last, prod = ends[q]
        carry = state[q, head - 1 : head, :]
        parts = []
        for s in range(8):
            parts.append(carry)
            carry = prod[s : s + 1] * carry + last[s : s + 1]
        entries.append(jnp.concatenate(parts, axis=0))

    def second(j, held):
        for q in range(planes):
            state[q, pl.ds(head + j, 8, stride=seg), :] += (
                product[q, pl.ds(j, 8, stride=seg), :] * entries[q]
            )
        return held

    lax.fori_loop(0, seg, second, 0, unroll=4)


def to_planes(ref, rows, value):
    for q in range(value.shape[1] // LANES):
        ref[q, rows, :] = value[:, q * LANES : (q + 1) * LANES]


def from_planes(ref, rows):
    return jnp.concatenate([ref[q, rows, :] for q in range(ref.shape[0])], axis=1)


LAG = 3


class Chain:
    def __init__(self, grads, units, sums, lows, highs, peers, buf, sems, count, lag):
        self.grads, self.counts, self.sums, self.peers, self.buf = grads, units, sums, peers, buf
        self.unit = buf.shape[2]
        self.parts = (lows, highs)
        (
            self.part_send, self.low_recv, self.high_recv,
            self.low_send, self.up_send, self.fin_recv, self.twin_send, self.twin_recv, self.load_sem, self.put_sem,
        ) = sems
        me = lax.axis_index("dp")
        self.core = me % 2
        self.z = me // 2
        self.chips = count // 2
        self.left = {"dp": (me + count - 2) % count}
        self.right = {"dp": (me + 2) % count}
        self.twin = {"dp": me + 1 - 2 * self.core}
        self.first = []
        start = 0
        for n in units:
            self.first.append(start)
            start += n
        self.units = start
        self.far = self.chips // 2
        self.lag = lag
        self.ticks = 2 * ((self.units - 1) // 2 + 2 * lag * self.far + 4)

    def near(self):
        return [self.left, self.right, self.twin]

    def rows(self, i, u, core):
        return block(core * self.counts[i] + u - self.first[i], self.unit)

    def inside(self, i, u):
        return (u >= self.first[i]) & (u < self.first[i] + self.counts[i])

    def slot(self, i, u, k):
        return self.buf.at[u % 4, k, :, 0 : self.grads[i].shape[1]]

    def partial(self, i, u, way):
        rows = self.rows(i, u, self.core)
        return pltpu.make_async_remote_copy(
            self.slot(i, u, 4), self.parts[way][i].at[rows, :], self.part_send.at[u],
            (self.low_recv, self.high_recv)[way].at[u],
            device_id=(self.right, self.left)[way], device_id_type=MESH,
        )

    def final(self, i, u, way, staged):
        rows = self.rows(i, u, self.core)
        place = self.sums[i].at[rows, :]
        return pltpu.make_async_remote_copy(
            self.slot(i, u, 4) if staged else place, place,
            (self.up_send, self.low_send)[way].at[u], self.fin_recv.at[u],
            device_id=(self.right, self.left)[way], device_id_type=MESH,
        )

    def share(self, i, u, staged):
        rows = self.rows(i, u, self.core)
        place = self.sums[i].at[rows, :]
        return pltpu.make_async_remote_copy(
            self.slot(i, u, 4) if staged else place, place, self.twin_send.at[u], self.twin_recv.at[u],
            device_id=self.twin, device_id_type=MESH,
        )

    def load(self, i, u, k):
        rows = self.rows(i, u, self.core)
        refs = (self.grads[i], self.peers[i], self.parts[0][i], self.parts[1][i])
        return pltpu.make_async_copy(refs[k].at[rows, :], self.slot(i, u, k), self.load_sem.at[u % 4, k])

    def put(self, i, u):
        return pltpu.make_async_copy(
            self.slot(i, u, 4), self.sums[i].at[self.rows(i, u, self.core), :], self.put_sem.at[u % 4]
        )

    def over(self, act):
        for i, n in enumerate(self.counts):
            each(n, lambda j, i=i: act(i, self.first[i] + j))

    def owner(self, u):
        return self.chips // 2 - 1 + u % 2

    def from_low(self, u):
        return (self.z > 0) & (self.z <= self.owner(u))

    def from_high(self, u):
        return (self.z < self.chips - 1) & (self.z >= self.owner(u))

    def fetch(self, i, u):
        self.load(i, u, 0).start()
        self.load(i, u, 1).start()

        @pl.when(self.from_low(u))
        def _():
            self.partial(i, u, 0).wait_recv()
            self.load(i, u, 2).start()

        @pl.when(self.from_high(u))
        def _():
            self.partial(i, u, 1).wait_recv()
            self.load(i, u, 3).start()

    def settle(self, i, u):
        o = self.owner(u)

        @pl.when(self.z != o)
        def _():
            self.partial(i, u, 0).wait_send()

        @pl.when(self.z == o)
        def _():
            @pl.when(self.z < self.chips - 1)
            def _():
                self.final(i, u, 0, True).wait_send()

            @pl.when(self.z > 0)
            def _():
                self.final(i, u, 1, True).wait_send()

            self.share(i, u, True).wait_send()
            self.put(i, u).wait()

    def reduce(self, i, u):
        o = self.owner(u)
        self.load(i, u, 0).wait()
        self.load(i, u, 1).wait()
        width = self.grads[i].shape[1]
        here = u % 4

        def value(k, r):
            return self.buf[here, k, r, 0:width].astype(F32)

        def total(ks):
            def add(j):
                r = block(j, 16)
                self.buf[here, 4, r, 0:width] = sum(value(k, r) for k in ks).astype(BF16)

            each(self.unit // 16, add)

        low, high = self.from_low(u), self.from_high(u)

        @pl.when(low)
        def _():
            self.load(i, u, 2).wait()

        @pl.when(high)
        def _():
            self.load(i, u, 3).wait()

        @pl.when(low & high)
        def _():
            total((0, 1, 2, 3))

        @pl.when(low != high)
        def _():
            total((0, 1, 3 - low.astype(jnp.int32)))

        @pl.when(jnp.logical_not(low | high))
        def _():
            total((0, 1))

        @pl.when(self.z < o)
        def _():
            self.partial(i, u, 0).start()

        @pl.when(self.z > o)
        def _():
            self.partial(i, u, 1).start()

        @pl.when(self.z == o)
        def _():
            @pl.when(self.z < self.chips - 1)
            def _():
                self.final(i, u, 0, True).start()

            @pl.when(self.z > 0)
            def _():
                self.final(i, u, 1, True).start()

            self.share(i, u, True).start()
            self.put(i, u).start()

    def pass_on(self, i, u):
        o = self.owner(u)
        self.final(i, u, 0, False).wait_recv()

        @pl.when((self.z < o) & (self.z > 0))
        def _():
            self.final(i, u, 1, False).start()

        @pl.when((self.z > o) & (self.z < self.chips - 1))
        def _():
            self.final(i, u, 0, False).start()

        self.share(i, u, False).start()

    def tick(self, tau):
        stream = tau % 2
        k = tau // 2 - 1
        away = jnp.abs(self.z - self.owner(stream))
        now = 2 * (k - self.lag * (self.far - away)) + stream
        back = 2 * (k - self.lag * (self.far + away)) + stream

        def pick(u, act, also=True):
            for i in range(len(self.grads)):

                @pl.when(self.inside(i, u) & also)
                def _(i=i):
                    act(i, u)

        pick(now - 4, self.settle)
        pick(now, self.reduce)
        pick(back, self.pass_on, away > 0)
        pick(now + 2, self.fetch)

    def close(self, tau):
        each(self.ticks - tau, lambda j: self.tick(tau + j))

        def done(i, u):
            o = self.owner(u)

            @pl.when(self.z != o)
            def _():
                self.share(i, u, False).wait_send()

            @pl.when((self.z < o) & (self.z > 0))
            def _():
                self.final(i, u, 1, False).wait_send()

            @pl.when((self.z > o) & (self.z < self.chips - 1))
            def _():
                self.final(i, u, 0, False).wait_send()

            rows = self.rows(i, u, 1 - self.core)
            place = self.sums[i].at[rows, :]
            pltpu.make_async_remote_copy(
                place, place, self.twin_send.at[u], self.twin_recv.at[u],
                device_id=self.twin, device_id_type=MESH,
            ).wait_recv()

        self.over(done)

    @staticmethod
    def scratch(width, unit, units):
        dma = pltpu.SemaphoreType.DMA
        return [pltpu.VMEM((4, 5, unit, width), BF16)] + [dma((sum(units),))] * 8 + [dma((4, 4)), dma((4,))]


TILE = 256


class Tiles:
    def __init__(self, lhs, rhs, ready, grads, peers, lbuf, xbuf, stage, sems):
        self.lhs, self.rhs, self.ready, self.grads, self.peers = lhs, rhs, ready, grads, peers
        self.lbuf, self.xbuf, self.stage = lbuf, xbuf, stage
        self.load_sem, self.put_sem, self.send_sem, self.recv_sem = sems
        me = lax.axis_index("dp")
        self.core = me % 2
        self.twin = {"dp": me + 1 - 2 * self.core}
        self.counts = [g.shape[0] // (2 * TILE) for g in grads]
        self.first = [sum(self.counts[:i]) for i in range(len(grads))]
        self.pairs = sum(self.counts)

    def rows(self, i, p, core):
        return block(core * self.counts[i] + p - self.first[i], TILE)

    def load(self, i, p, h):
        core = self.core if h else 1 - self.core
        return pltpu.make_async_copy(
            self.lhs[i].at[:, self.rows(i, p, core)], self.lbuf.at[h], self.load_sem.at[h]
        )

    def send(self, i, p):
        rows = self.rows(i, p, 1 - self.core)
        return pltpu.make_async_remote_copy(
            self.stage.at[0, :, 0 : self.grads[i].shape[1]], self.peers[i].at[rows, :],
            self.send_sem.at[p], self.recv_sem.at[p], device_id=self.twin, device_id_type=MESH,
        )

    def put(self, i, p):
        rows = self.rows(i, p, self.core)
        return pltpu.make_async_copy(
            self.stage.at[1, :, 0 : self.grads[i].shape[1]], self.grads[i].at[rows, :], self.put_sem.at[p]
        )

    def pick(self, p, act):
        for i in range(len(self.grads)):

            @pl.when((p >= self.first[i]) & (p < self.first[i] + self.counts[i]))
            def _(i=i):
                act(i)

    def begin(self):
        self.load(0, 0, 0).start()
        self.load(0, 0, 1).start()

    def settle(self, p):
        def act(i):
            self.send(i, p).wait()
            self.put(i, p).wait()

        self.pick(p, act)

    def work(self, p, hook):
        total = self.xbuf.shape[1]

        def pair(i):
            @pl.when(p == self.first[i])
            def _():
                self.ready[i]()

            width = self.grads[i].shape[1]

            def tile(h):
                @pl.when(h == 0)
                def _():
                    self.load(i, p, 0).wait()

                @pl.when(h == 1)
                def _():
                    self.load(i, p, 1).wait()

                def turn(k):
                    r = block(k, TILE)
                    self.xbuf[:, r] = self.lbuf[h, r, :].T

                each(total // TILE, turn)
                hook(2 * h)

                @pl.when(h == 0)
                def _():
                    self.pick(p + 1, lambda n: self.load(n, p + 1, 0).start())

                @pl.when(h == 1)
                def _():
                    self.pick(p + 1, lambda n: self.load(n, p + 1, 1).start())

                step = next(w for w in (1408, 1024, 768, 512) if width % w == 0)

                def part(b):
                    cols = block(b, step)
                    self.stage[h, :, cols] = plain_dot(self.xbuf[...], self.rhs[i][:, cols]).astype(BF16)

                each(width // step, part)

                @pl.when(h == 0)
                def _():
                    self.send(i, p).start()

                @pl.when(h == 1)
                def _():
                    self.put(i, p).start()

                hook(2 * h + 1)

            each(2, tile)

        self.settle(p - 1)
        self.pick(p, pair)

        @pl.when(p >= self.pairs)
        def _():
            each(4, hook)

    @staticmethod
    def scratch(rows, width, pairs):
        dma = pltpu.SemaphoreType.DMA
        return [
            pltpu.VMEM((2, rows, TILE), BF16),
            pltpu.VMEM((TILE, rows), BF16),
            pltpu.VMEM((2, TILE, width), BF16),
            dma((2,)),
            dma((pairs,)),
            dma((pairs,)),
            dma((pairs,)),
        ]


def mixer_kernel(
    tok, wout, gains, w_in, w_for, w_gp, lower, gain_gate,
    normed, tok_full, wout_full, gains_full, scale_in, pre_in, pre_for, pre_gp, state, diff, mixed, squares,
    full, wfull, vin, vfor, vgp, gbuf, dec, src, prod, hbuf,
    send, recv, wsend, wrecv, xsend, xrecv, gsend, grecv, lsem, osem,
):
    s = pl.program_id(0)
    chunks = pl.num_programs(0) - 1
    rows, width = pre_in.shape
    feats = full.shape[1]
    t, xn, yn, dg = neighbours()
    me = lax.axis_index("dp")
    core = me % 2
    partner = {"dp": me + 1 - 2 * core}
    peers = ({"tensor": xn}, {"tensor": yn}, {"tensor": dg})
    gather = Gather(tok, full, send, recv, rows, width)
    planes = width // LANES
    half = width // 2
    piece = width // 4

    def w_direct(k, p):
        return pltpu.make_async_remote_copy(
            wout.at[block(2 * core + p, piece), :],
            wfull.at[block(4 * t + 2 * core + p, piece), :],
            wsend.at[k, p],
            wrecv.at[k, p],
            device_id=peers[k],
            device_id_type=MESH,
        )

    def w_relay(k):
        part = wfull.at[block(4 * (xn if k == 0 else yn) + 2 * core + k, piece), :]
        return pltpu.make_async_remote_copy(
            part, part, wsend.at[2, k], wrecv.at[2, k], device_id=peers[1 - k], device_id_type=MESH
        )

    def w_swap(k):
        part = wfull.at[block(2 * (xn, yn, dg)[k] + core, half), :]
        return pltpu.make_async_remote_copy(
            part, part, xsend.at[k], xrecv.at[k], device_id=partner, device_id_type=MESH
        )

    def gain_copy(k):
        return pltpu.make_async_remote_copy(
            gains, gbuf.at[t], gsend.at[k], grecv.at[k], device_id=peers[k], device_id_type=MESH
        )

    loads = (
        pltpu.make_async_copy(tok, full.at[:, block(t, width)], lsem.at[0]),
        pltpu.make_async_copy(wout, wfull.at[block(t, width), :], lsem.at[1]),
        pltpu.make_async_copy(w_in, vin, lsem.at[2]),
        pltpu.make_async_copy(w_for, vfor, lsem.at[3]),
        pltpu.make_async_copy(w_gp, vgp, lsem.at[4]),
        pltpu.make_async_copy(gains, gbuf.at[t], lsem.at[5]),
    )

    def tok_out(c):
        return pltpu.make_async_copy(
            full.at[block(c, rows), :], tok_full.at[block(c, rows), :], osem.at[c]
        )

    w_out = pltpu.make_async_copy(wfull, wout_full, lsem.at[6])

    @pl.when(s == 0)
    def _():
        for load in loads:
            load.start()
        greet(peers + (partner,))
        for k in range(3):
            gain_copy(k).start()
        for p in range(2):
            w_direct(0, p).start()
            w_direct(1, p).start()
        for c in range(AHEAD):
            gather.start(c)
        hbuf[:, 0:8, :] = jnp.zeros((planes, 8, LANES), F32)
        for p in range(2):
            w_direct(0, p).wait_recv()
            w_direct(1, p).wait_recv()
        w_relay(0).start()
        w_relay(1).start()
        w_swap(0).start()
        w_swap(1).start()
        for load in loads:
            load.wait()
        for k in range(3):
            gain_copy(k).wait_recv()
        for j in range(4):
            gains_full[:, j * width : (j + 1) * width] = gbuf[j]

    @pl.when(s == 2)
    def _():
        w_relay(0).wait_recv()
        w_relay(1).wait_recv()
        w_swap(2).start()

    @pl.when(s == chunks - 1)
    def _():
        for k in range(3):
            w_swap(k).wait_recv()
        w_out.start()

    @pl.when(s < chunks)
    def _():
        gather.forward(s)

        @pl.when(s + AHEAD < chunks)
        def _():
            gather.start(s + AHEAD)

    @pl.when(s >= 1)
    def _():
        c = s - 1
        gather.finish(c)
        tok_out(c).start()
        gain_in = gains_full[0:1, :]
        low = lower[...]
        gain = gain_gate[...]

        def norm_rows(i):
            x = full[block(c * (rows // 32) + i, 32), :].astype(F32)
            scale = lax.rsqrt(jnp.sum(x * x, axis=1, keepdims=True) / feats + EPSILON)
            here = block(i, 32)
            normed[here, :] = (x * scale * gain_in).astype(BF16)
            scale_in[here, :] = jnp.broadcast_to(scale, (32, 128))

        each(rows // 32, norm_rows)
        pre_in[...] = plain_dot(normed[...], vin[...])
        pre_for[...] = plain_dot(normed[...], vfor[...])
        pre_gp[...] = plain_dot(normed[...], vgp[...])

        def gate_rows(i):
            here = block(i, 32)
            decay = low + (1.0 - low) * jax.nn.sigmoid(pre_for[here, :])
            to_planes(dec, here, decay)
            to_planes(src, here, (1.0 - decay) * jax.nn.silu(pre_in[here, :]))

        each(rows // 32, gate_rows)
        scan_rows(dec, src, hbuf, prod, 8)
        diff[...] = from_planes(hbuf, slice(7, 7 + rows))

        def mix_rows(i):
            here = block(i, 32)
            h = from_planes(hbuf, pl.ds(pl.multiple_of(8 + i * 32, 8), 32))
            state[here, :] = h
            diff[here, :] -= jax.nn.silu(pre_in[here, :])
            mixed[here, :] = (h * gain * jax.nn.silu(pre_gp[here, :])).astype(BF16)

        each(rows // 32, mix_rows)
        h = state[...]
        squares[0] = rows_to_lanes(h * h)
        hbuf[:, 7:8, :] = hbuf[:, 7 + rows : 8 + rows, :]

    @pl.when(s == chunks)
    def _():
        each(chunks, gather.drain)
        each(chunks, lambda c: tok_out(c).wait())
        for k in range(3):
            gain_copy(k).wait_send()
            w_swap(k).wait_send()
        for p in range(2):
            w_direct(0, p).wait_send()
            w_direct(1, p).wait_send()
            w_relay(p).wait_send()
        w_out.wait()


def later(s):
    return (jnp.maximum(s - 1, 0), 0)


def mixer_forward(tok, wout, gains, w_in, w_for, w_gp, lower, gain_gate):
    total, width = tok.shape
    feats = w_in.shape[0]
    rows = total // FRONT

    def out(n, dtype):
        return jax.ShapeDtypeStruct((total, n), dtype), pl.BlockSpec((rows, n), later)

    outs = [
        out(feats, BF16),
        (jax.ShapeDtypeStruct((total, feats), BF16), ANY),
        (jax.ShapeDtypeStruct((feats, feats), BF16), ANY),
        (jax.ShapeDtypeStruct((8, feats), F32), WHOLE),
        out(128, F32),
        out(width, F32),
        out(width, F32),
        out(width, F32),
        out(width, F32),
        out(width, F32),
        out(width, BF16),
        (
            jax.ShapeDtypeStruct((FRONT, 8, rows), F32),
            pl.BlockSpec((1, 8, rows), lambda s: (jnp.maximum(s - 1, 0), 0, 0)),
        ),
    ]
    dma = pltpu.SemaphoreType.DMA
    return pl.pallas_call(
        mixer_kernel,
        grid=(FRONT + 1,),
        out_shape=[o[0] for o in outs],
        out_specs=[o[1] for o in outs],
        in_specs=[ANY, ANY, WHOLE, ANY, ANY, ANY, WHOLE, WHOLE],
        scratch_shapes=[
            pltpu.VMEM((total, feats), BF16),
            pltpu.VMEM((feats, feats), BF16),
            pltpu.VMEM((feats, width), BF16),
            pltpu.VMEM((feats, width), BF16),
            pltpu.VMEM((feats, width), BF16),
            pltpu.VMEM((4, 8, width), F32),
            pltpu.VMEM((width // LANES, rows, LANES), F32),
            pltpu.VMEM((width // LANES, rows, LANES), F32),
            pltpu.VMEM((width // LANES, rows, LANES), F32),
            pltpu.VMEM((width // LANES, rows + 8, LANES), F32),
            dma((4, FRONT)),
            dma((4, FRONT)),
            dma((3, 2)),
            dma((3, 2)),
            dma((3,)),
            dma((3,)),
            dma((3,)),
            dma((3,)),
            dma((7,)),
            dma((FRONT,)),
        ],
        compiler_params=pltpu.CompilerParams(
            collective_id=1, has_side_effects=True, vmem_limit_bytes=VMEM_BYTES
        ),
        name="mixer_forward",
    )(tok, wout, gains, w_in, w_for, w_gp, lower, gain_gate)


def ffn_kernel(
    lens, mixed, cot, squares, gains, tok_full, wout, w_gate, w_up, w_down,
    normed, hidden, g_both, cot_out, mix_out, scale_gate, scale_mid, resid,
    mfull, cfull, vout, vgate, vup, vdown, sbuf, mo, gbuf, ubuf, hbuf,
    send, recv, csend, crecv, ssend, srecv, lsem,
):
    s = pl.program_id(0)
    chunks = pl.num_programs(0) - 1
    width = mixed.shape[1]
    rows, feats = normed.shape
    hid = hidden.shape[1]
    t, xn, yn, dg = neighbours()
    peers = ({"tensor": xn}, {"tensor": yn}, {"tensor": dg})
    gather = Gather(mixed, mfull, send, recv, rows, width)
    cgather = Gather(cot, cfull, csend, crecv, rows, width)

    def square_copy(k):
        return pltpu.make_async_remote_copy(
            squares, sbuf.at[t], ssend.at[k], srecv.at[k], device_id=peers[k], device_id_type=MESH
        )

    loads = (
        pltpu.make_async_copy(mixed, mfull.at[:, block(t, width)], lsem.at[0]),
        pltpu.make_async_copy(cot, cfull.at[:, block(t, width)], lsem.at[1]),
        pltpu.make_async_copy(squares, sbuf.at[t], lsem.at[2]),
        pltpu.make_async_copy(wout, vout, lsem.at[3]),
        pltpu.make_async_copy(w_gate, vgate, lsem.at[4]),
        pltpu.make_async_copy(w_up, vup, lsem.at[5]),
        pltpu.make_async_copy(w_down, vdown, lsem.at[6]),
    )

    @pl.when(s == 0)
    def _():
        greet(peers)
        for k in range(3):
            square_copy(k).start()
        for c in range(AHEAD):
            gather.start(c)
            cgather.start(c)
        for load in loads:
            load.start()

    @pl.when(s < chunks)
    def _():
        gather.forward(s)
        cgather.forward(s)

        @pl.when(s + AHEAD < chunks)
        def _():
            gather.start(s + AHEAD)
            cgather.start(s + AHEAD)

    @pl.when(s == 1)
    def _():
        for load in loads:
            load.wait()
        for k in range(3):
            square_copy(k).wait_recv()

    @pl.when(s >= 1)
    def _():
        c = s - 1
        gain_mid = gains[1:2, :]
        gather.finish(c)
        here = block(c, rows)
        each(
            feats // width,
            lambda b: mo.__setitem__(
                (slice(None), block(b, width)), plain_dot(mfull[here, :], vout[:, block(b, width)])
            ),
        )
        total = sbuf[0, c] + sbuf[1, c] + sbuf[2, c] + sbuf[3, c]
        scale = lax.rsqrt(lanes_to_rows(total) / feats + EPSILON)
        scale_gate[...] = jnp.broadcast_to(scale, (rows, 128))

        def norm_rows(i):
            part = block(i, 32)
            m = mo[part, :] * scale_gate[part, 0:1]
            mix_out[part, :] = m.astype(BF16)
            r = m + tok_full[part, :].astype(F32)
            mid = lax.rsqrt(jnp.sum(r * r, axis=1, keepdims=True) / feats + EPSILON)
            scale_mid[part, :] = jnp.broadcast_to(mid, (32, 128))
            normed[part, :] = (r * mid * gain_mid).astype(BF16)
            mo[part, :] = r

        each(rows // 32, norm_rows)
        resid[...] = mo[:, block(t, width)]
        gbuf[...] = plain_dot(normed[...], vgate[...])
        ubuf[...] = plain_dot(normed[...], vup[...])
        cgather.finish(c)
        length = lens[0]

        def mask_rows(i):
            part = block(i, 32)
            position = c * rows + i * 32 + lax.broadcasted_iota(jnp.int32, (32, feats), 0)
            value = cfull[block(c * (rows // 32) + i, 32), :]
            cot_out[part, :] = jnp.where(position < length, value.astype(F32), 0.0).astype(BF16)

        each(rows // 32, mask_rows)
        hbuf[...] = back_dot(cot_out[...], vdown[...])

        def ffn_rows(i):
            part = block(i, 16)
            g = gbuf[part, :]
            u = ubuf[part, :]
            back = hbuf[part, :]
            sigma = jax.nn.sigmoid(g)
            act = g * sigma
            hidden[part, :] = (act * u).astype(BF16)
            g_both[part, 0:hid] = (back * u * (sigma * (1.0 + g * (1.0 - sigma)))).astype(BF16)
            g_both[part, hid:] = (back * act).astype(BF16)

        each(rows // 16, ffn_rows)

    @pl.when(s == chunks)
    def _():
        each(chunks, gather.drain)
        each(chunks, cgather.drain)
        for k in range(3):
            square_copy(k).wait_send()


def ffn_forward(lens, mixed, cot, squares, gains, tok_full, wout, w_gate, w_up, w_down):
    total, width = mixed.shape
    feats, hid = w_gate.shape
    rows = total // FRONT

    def out(n, dtype):
        return jax.ShapeDtypeStruct((total, n), dtype), pl.BlockSpec((rows, n), later)

    outs = [
        out(feats, BF16),
        out(hid, BF16),
        out(2 * hid, BF16),
        out(feats, BF16),
        out(feats, BF16),
        out(128, F32),
        out(128, F32),
        out(width, F32),
    ]
    dma = pltpu.SemaphoreType.DMA
    return pl.pallas_call(
        ffn_kernel,
        grid=(FRONT + 1,),
        out_shape=[o[0] for o in outs],
        out_specs=[o[1] for o in outs],
        in_specs=[
            pl.BlockSpec(memory_space=pltpu.SMEM),
            ANY, ANY, WHOLE, WHOLE,
            pl.BlockSpec((rows, feats), later),
            ANY, ANY, ANY, ANY,
        ],
        scratch_shapes=[
            pltpu.VMEM((total, feats), BF16),
            pltpu.VMEM((total, feats), BF16),
            pltpu.VMEM((feats, feats), BF16),
            pltpu.VMEM((feats, hid), BF16),
            pltpu.VMEM((feats, hid), BF16),
            pltpu.VMEM((hid, feats), BF16),
            pltpu.VMEM((4, FRONT, 8, rows), F32),
            pltpu.VMEM((rows, feats), F32),
            pltpu.VMEM((rows, hid), F32),
            pltpu.VMEM((rows, hid), F32),
            pltpu.VMEM((rows, hid), F32),
            dma((4, FRONT)),
            dma((4, FRONT)),
            dma((4, FRONT)),
            dma((4, FRONT)),
            dma((3,)),
            dma((3,)),
            dma((7,)),
        ],
        compiler_params=pltpu.CompilerParams(
            collective_id=2, has_side_effects=True, vmem_limit_bytes=VMEM_BYTES
        ),
        name="ffn_forward",
    )(lens, mixed, cot, squares, gains, tok_full, wout, w_gate, w_up, w_down)


class Scatter:
    def __init__(self, share, keep, out1, in1, out2, in2, sems):
        self.share, self.keep = share, keep
        self.out1, self.in1, self.out2, self.in2 = out1, in1, out2, in2
        self.send1, self.recv1, self.send2, self.recv2 = sems
        self.t, xn, yn, self.dg = neighbours()
        self.order = ((xn, yn), (yn, xn))
        self.slots = keep.shape[0]
        self.outs = out1.shape[0]
        self.half = keep.shape[3]
        self.count = self.half // 32

    def hop1(self, c, h):
        return pltpu.make_async_remote_copy(
            self.out1.at[c % self.outs, h],
            self.in1.at[c, h],
            self.send1.at[h, c],
            self.recv1.at[h, c],
            device_id={"tensor": self.order[h][0]},
            device_id_type=MESH,
        )

    def hop2(self, c, h):
        return pltpu.make_async_remote_copy(
            self.out2.at[c % self.outs, h],
            self.in2.at[c, h],
            self.send2.at[h, c],
            self.recv2.at[h, c],
            device_id={"tensor": self.order[h][1]},
            device_id_type=MESH,
        )

    def begin(self, c):
        slot, place = c % self.slots, c % self.outs

        @pl.when(c >= self.outs)
        def _():
            for h in range(2):
                self.hop1(c - self.outs, h).wait_send()

        for h in range(2):
            one, two = self.order[h]

            def move(i, h=h, one=one, two=two):
                here = block(i, 32)
                there = block(h * self.count + i, 32)
                self.out1[place, h, 0, here, :] = self.share[one, there, :].astype(BF16)
                self.out1[place, h, 1, here, :] = self.share[self.dg, there, :].astype(BF16)
                self.keep[slot, h, 0, here, :] = self.share[self.t, there, :]
                self.keep[slot, h, 1, here, :] = self.share[two, there, :]

            each(self.count, move)
        for h in range(2):
            self.hop1(c, h).start()

    def middle(self, c):
        slot, place = c % self.slots, c % self.outs

        @pl.when(c >= self.outs)
        def _():
            for h in range(2):
                self.hop2(c - self.outs, h).wait_send()

        for h in range(2):
            self.hop1(c, h).wait_recv()

            def add(i, h=h):
                here = block(i, 32)
                self.out2[place, h, here, :] = (
                    self.keep[slot, h, 1, here, :] + self.in1[c, h, 1, here, :].astype(F32)
                ).astype(BF16)
                self.keep[slot, h, 0, here, :] += self.in1[c, h, 0, here, :].astype(F32)

            each(self.count, add)
        for h in range(2):
            self.hop2(c, h).start()

    def end(self, c, use):
        slot = c % self.slots
        for h in range(2):
            self.hop2(c, h).wait_recv()

            def give(i, h=h):
                here = block(i, 32)
                use(
                    h * self.count + i,
                    self.keep[slot, h, 0, here, :] + self.in2[c, h, here, :].astype(F32),
                )

            each(self.count, give)

    def drain(self, chunks):
        for c in range(max(chunks - self.outs, 0), chunks):
            for h in range(2):
                self.hop1(c, h).wait_send()
                self.hop2(c, h).wait_send()

    @staticmethod
    def scratch(chunks, rows, width):
        dma = pltpu.SemaphoreType.DMA
        return [
            pltpu.VMEM((4, rows, width), F32),
            pltpu.VMEM((3, 2, 2, rows // 2, width), F32),
            pltpu.VMEM((3, 2, 2, rows // 2, width), BF16),
            pltpu.VMEM((chunks, 2, 2, rows // 2, width), BF16),
            pltpu.VMEM((3, 2, rows // 2, width), BF16),
            pltpu.VMEM((chunks, 2, rows // 2, width), BF16),
            dma((2, chunks)),
            dma((2, chunks)),
            dma((2, chunks)),
            dma((2, chunks)),
        ]


def scan_rows_back(decay, source, state, product, carry):
    planes, rows, _ = decay.shape
    seg = rows // 8

    def first(n, held):
        j = seg - 1 - n
        out = []
        for q in range(planes):
            now, prod = held[q]
            here = pl.ds(j, 8, stride=seg)
            d = decay[q, here, :]
            now = source[q, here, :] + now
            state[q, here, :] = now
            product[q, here, :] = prod
            out.append((d * now, d * prod))
        return tuple(out)

    zero, one = jnp.zeros((8, LANES), F32), jnp.ones((8, LANES), F32)
    ends = lax.fori_loop(0, seg, first, ((zero, one),) * planes, unroll=4)
    entries = []
    for q in range(planes):
        last, prod = ends[q]
        value = carry[q, 0:1, :]
        parts = []
        for s in range(7, -1, -1):
            parts.append(value)
            value = prod[s : s + 1] * value + last[s : s + 1]
        entries.append(jnp.concatenate(parts[::-1], axis=0))
        carry[q, 0:1, :] = value

    def second(j, held):
        for q in range(planes):
            here = pl.ds(j, 8, stride=seg)
            state[q, here, :] += product[q, here, :] * entries[q]
        return held

    lax.fori_loop(0, seg, second, 0, unroll=4)


def fold_rows(value):
    return value[0:8] + value[8:16] + value[16:24] + value[24:32]


STAGES = 4
SITES = (1, 1, 1, 1, 1, 1, 1, 1)


def spend(chain, base, sites, n):
    each(sites[n], lambda j: chain.tick(base + sum(sites[:n]) + j))


def back_kernel(
    dp, units,
    g_both, w_gate, w_up, w_out, gains, gain_gate, lower,
    cot, mix, tok, scale_mid, scale_gate, pre_in, pre_for, pre_gp, state, diff, d_both, peer,
    g_mix, g_resid, g_pre, mixed, inner, sums_out, total_both, low_part, high_part,
    vboth, vout, full, line, dots, gm, dec, src, prod, adj, carry, sum_mid, sum_gate, sum_low,
    share, keep, out1, in1, out2, in2, send1, recv1, send2, recv2, send, recv, lsem,
    buf, *sems,
):
    chain = Chain([d_both], units, [total_both], [low_part], [high_part], [peer], buf, sems, dp, LAG + 1)
    s = pl.program_id(0)
    chunks = pl.num_programs(0) - STAGES
    rows, width = g_resid.shape
    feats = full.shape[1]
    hid = w_gate.shape[1]
    t, xn, yn, dg = neighbours()
    peers = ({"tensor": xn}, {"tensor": yn})
    base = s * sum(SITES)
    gather = Gather(None, full, send, recv, rows, width)
    scatter = Scatter(share, keep, out1, in1, out2, in2, (send1, recv1, send2, recv2))
    loads = (
        pltpu.make_async_copy(w_gate, vboth.at[:, 0:hid], lsem.at[0]),
        pltpu.make_async_copy(w_up, vboth.at[:, hid : 2 * hid], lsem.at[1]),
        pltpu.make_async_copy(w_out, vout, lsem.at[2]),
    )

    def place(c):
        return chunks - 1 - c

    def at_stage(n, act):
        @pl.when((s >= n) & (s - n < chunks))
        def _():
            act(s - n)

    @pl.when(s == 0)
    def _():
        for load in loads:
            load.start()
        greet(peers + tuple(chain.near()))
        carry[...] = jnp.zeros(carry.shape, F32)
        sum_mid[...] = jnp.zeros(sum_mid.shape, F32)
        sum_gate[...] = jnp.zeros(sum_gate.shape, F32)
        sum_low[...] = jnp.zeros(sum_low.shape, F32)
        for load in loads[:2]:
            load.wait()

    @pl.when(s == 1)
    def _():
        loads[2].wait()

    spend(chain, base, SITES, 0)
    at_stage(3, lambda c: gather.forward(place(c)))

    def summed(c):
        def use(i, value):
            full[block(place(c) * (rows // 32) + i, 32), block(t, width)] = value.astype(BF16)

        scatter.end(c, use)
        gather.start(place(c))

    at_stage(2, summed)
    spend(chain, base, SITES, 1)
    at_stage(1, scatter.middle)
    spend(chain, base, SITES, 2)

    def terms(c, part):
        for b in (2 * part, 2 * part + 1):
            share[b] = back_dot(g_both[...], vboth[b * width : (b + 1) * width, :])

    at_stage(0, lambda c: terms(c, 0))
    spend(chain, base, SITES, 3)

    def last_terms(c):
        terms(c, 1)
        scatter.begin(c)

    at_stage(0, last_terms)
    spend(chain, base, SITES, 4)
    gain_mid = gains[1:2, :]
    gain = gain_gate[...]
    low = lower[...]

    def finish(c):
        p = place(c)
        gather.finish(p)

        def resid_rows(i):
            here = block(i, 32)
            g = full[block(p * (rows // 32) + i, 32), :].astype(F32)
            m = mix[here, :].astype(F32)
            r = tok[here, :].astype(F32) + m
            mid = scale_mid[here, 0:1]
            weighted = g * gain_mid
            total = jnp.sum(weighted * r, axis=1, keepdims=True) / feats
            grad = cot[here, :].astype(F32) + mid * weighted - r * (mid * mid * mid * total)
            low_grad = grad.astype(BF16)
            g_mix[here, :] = low_grad
            line[...] = grad
            g_resid[here, :] = line[:, block(t, width)]
            dots[here, :] = jnp.broadcast_to(
                jnp.sum(low_grad.astype(F32) * m, axis=1, keepdims=True), (32, 128)
            )
            sum_mid[...] += fold_rows(g * r * mid)

        each(rows // 32, resid_rows)
        gm[...] = back_dot(g_mix[...], vout[...])

    at_stage(STAGES, finish)
    spend(chain, base, SITES, 5)

    def finish_states(c):
        def state_rows(i):
            here = block(i, 32)
            h = state[here, :]
            scale = scale_gate[here, 0:1]
            ns = h * scale
            gp = pre_gp[here, :]
            sigma = jax.nn.sigmoid(gp)
            swish = gp * sigma
            grad = gm[here, :]
            sum_gate[...] += fold_rows(grad * ns * swish)
            g_pre[here, 2 * width :] = (grad * ns * gain * (sigma * (1.0 + gp * (1.0 - sigma)))).astype(BF16)
            mixed[here, :] = (ns * gain * swish).astype(BF16)
            factor = scale * scale * dots[here, 0:1] / feats
            to_planes(src, here, scale * (grad * gain * swish) - h * factor)
            to_planes(dec, here, low + (1.0 - low) * jax.nn.sigmoid(pre_for[here, :]))

        each(rows // 32, state_rows)
        scan_rows_back(dec, src, adj, prod, carry)

    at_stage(STAGES, finish_states)
    spend(chain, base, SITES, 6)

    def finish_gates(c):
        def gate_rows(i):
            here = block(i, 32)
            a = from_planes(adj, here)
            x, f = pre_in[here, :], pre_for[here, :]
            sig = jax.nn.sigmoid(f)
            decay = low + (1.0 - low) * sig
            grad_decay = a * diff[here, :]
            gi = (a * (1.0 - decay) * silu_slope(x)).astype(BF16)
            gf = (grad_decay * (1.0 - low) * sig * (1.0 - sig)).astype(BF16)
            g_pre[here, 0:width] = gi
            g_pre[here, width : 2 * width] = gf
            sum_low[...] += fold_rows(grad_decay * (1.0 - sig))
            gm[here, :] = (
                gi.astype(F32) * x + gf.astype(F32) * f + g_pre[here, 2 * width :].astype(F32) * pre_gp[here, :]
            )

        each(rows // 32, gate_rows)
        inner[0] = rows_to_lanes(gm[...])

    at_stage(STAGES, finish_gates)
    spend(chain, base, SITES, 7)

    @pl.when(s == pl.num_programs(0) - 1)
    def _():
        each(chunks, gather.drain)
        scatter.drain(BACK)
        chain.close(base + sum(SITES))
        sums_out[0] = sum_mid[:, block(t, width)]
        sums_out[1] = sum_gate[...]
        sums_out[2] = sum_low[...]


def backward(
    dp, d_both, peer, g_both, w_gate, w_up, w_out, gains, gain_gate, lower,
    cot, mix, tok, scale_mid, scale_gate, pre_in, pre_for, pre_gp, state, diff,
):
    total, hid = g_both.shape[0], w_gate.shape[1]
    unit = 16
    units = (d_both.shape[0] // (2 * unit),)
    feats, width = mix.shape[1], pre_in.shape[1]
    rows = total // BACK

    def early(s):
        return (BACK - 1 - jnp.minimum(s, BACK - 1), 0)

    def late(s):
        return (BACK - 1 - jnp.maximum(s - STAGES, 0), 0)

    def out(n, dtype):
        return jax.ShapeDtypeStruct((total, n), dtype), pl.BlockSpec((rows, n), late)

    outs = [
        out(feats, BF16),
        out(width, F32),
        out(3 * width, BF16),
        out(width, BF16),
        (
            jax.ShapeDtypeStruct((BACK, 8, rows), F32),
            pl.BlockSpec((1, 8, rows), lambda s: late(s) + (0,)),
        ),
        (jax.ShapeDtypeStruct((3, 8, width), F32), WHOLE),
    ] + [(jax.ShapeDtypeStruct(d_both.shape, BF16), ANY)] * 3
    planes = width // LANES
    dma = pltpu.SemaphoreType.DMA
    return pl.pallas_call(
        functools.partial(back_kernel, dp, units),
        grid=(BACK + STAGES,),
        out_shape=[o[0] for o in outs],
        out_specs=[o[1] for o in outs],
        in_specs=[
            pl.BlockSpec((rows, 2 * hid), early),
            ANY, ANY, ANY, WHOLE, WHOLE, WHOLE,
            pl.BlockSpec((rows, feats), late),
            pl.BlockSpec((rows, feats), late),
            pl.BlockSpec((rows, feats), late),
            pl.BlockSpec((rows, 128), late),
            pl.BlockSpec((rows, 128), late),
        ]
        + [pl.BlockSpec((rows, width), late)] * 5
        + [ANY, ANY],
        scratch_shapes=[
            pltpu.VMEM((feats, 2 * hid), BF16),
            pltpu.VMEM((width, feats), BF16),
            pltpu.VMEM((total, feats), BF16),
            pltpu.VMEM((32, feats), F32),
            pltpu.VMEM((rows, 128), F32),
            pltpu.VMEM((rows, width), F32),
            pltpu.VMEM((planes, rows, LANES), F32),
            pltpu.VMEM((planes, rows, LANES), F32),
            pltpu.VMEM((planes, rows, LANES), F32),
            pltpu.VMEM((planes, rows, LANES), F32),
            pltpu.VMEM((planes, 8, LANES), F32),
            pltpu.VMEM((8, feats), F32),
            pltpu.VMEM((8, width), F32),
            pltpu.VMEM((8, width), F32),
        ]
        + Scatter.scratch(BACK, rows, width)
        + [dma((4, BACK)), dma((4, BACK)), dma((3,))]
        + Chain.scratch(2 * hid, unit, units),
        compiler_params=pltpu.CompilerParams(
            collective_id=3, has_side_effects=True, vmem_limit_bytes=VMEM_BYTES
        ),
        name="backward",
    )(
        g_both, w_gate, w_up, w_out, gains, gain_gate, lower,
        cot, mix, tok, scale_mid, scale_gate, pre_in, pre_for, pre_gp, state, diff, d_both, peer,
    )


KW_HOOK = 2
KW_TICKS = 4 + 4 * KW_HOOK


def ffn_grad_kernel(
    dp, units,
    hidden, w_down, g_both, cot, normed, resid,
    out, total_down, d_both, peer_both, d_down, peer_down, low_part, high_part,
    vhid, vdown, vg,
    share, keep, out1, in1, out2, in2, send1, recv1, send2, recv2, lsem,
    lbuf, xbuf, stage, tsem0, tsem1, tsem2, tsem3, buf, *sems,
):
    s = pl.program_id(0)
    chunks = pl.num_programs(0) - 2
    rows, width = out.shape
    feats = vdown.shape[1]
    hid = vhid.shape[1]
    t, xn, yn, dg = neighbours()
    peers = ({"tensor": xn}, {"tensor": yn})
    scatter = Scatter(share, keep, out1, in1, out2, in2, (send1, recv1, send2, recv2))
    loads = (
        pltpu.make_async_copy(hidden, vhid, lsem.at[0]),
        pltpu.make_async_copy(w_down, vdown, lsem.at[1]),
        pltpu.make_async_copy(g_both, vg, lsem.at[2]),
    )
    tiles = Tiles(
        (cot, normed), (vhid, vg), (lambda: None, loads[2].wait), (d_down, d_both), (peer_down, peer_both),
        lbuf, xbuf, stage, (tsem0, tsem1, tsem2, tsem3),
    )
    chain = Chain([d_down], units, [total_down], [low_part], [high_part], [peer_down], buf, sems, dp, LAG + 1)

    def at_stage(n, act):
        @pl.when((s >= n) & (s - n < chunks))
        def _():
            act(s - n)

    @pl.when(s == 0)
    def _():
        for load in loads:
            load.start()
        tiles.begin()
        greet(peers + tuple(chain.near()))
        loads[0].wait()
        loads[1].wait()

    base = (s - 1) * KW_TICKS - 4

    def terms(c):
        def part(b):
            share[b] = plain_dot(vhid[block(c, rows), :], vdown[:, block(b, width)])
            chain.tick(base + b)

        each(feats // width, part)
        scatter.begin(c)

    def finish(c):
        def give(i, value):
            here = block(i, 32)
            out[here, :] = (resid[here, :] + value).astype(BF16)

        scatter.end(c, give)

    at_stage(2, finish)
    at_stage(1, scatter.middle)
    at_stage(0, terms)

    @pl.when(s >= chunks)
    def _():
        each(4, lambda j: chain.tick(base + j))

    tiles.work(s, lambda k: each(KW_HOOK, lambda j: chain.tick(base + 4 + KW_HOOK * k + j)))

    @pl.when(s == pl.num_programs(0) - 1)
    def _():
        scatter.drain(CHUNKS)
        chain.close(base + KW_TICKS)


def ffn_grads(dp, hidden, w_down, g_both, cot, normed, resid):
    total, hid = hidden.shape
    feats, width = w_down.shape[1], resid.shape[1]
    rows = total // CHUNKS
    unit = 16
    units = (feats // (2 * unit),)

    def late(s):
        return (jnp.maximum(s - 2, 0), 0)

    far = pl.BlockSpec((rows, width), late)
    down = jax.ShapeDtypeStruct((feats, hid), BF16)
    both = jax.ShapeDtypeStruct((feats, 2 * hid), BF16)
    dma = pltpu.SemaphoreType.DMA
    return pl.pallas_call(
        functools.partial(ffn_grad_kernel, dp, units),
        grid=(CHUNKS + 2,),
        out_shape=[jax.ShapeDtypeStruct((total, width), BF16), down, both, both, down, down, down, down],
        out_specs=[far] + [ANY] * 7,
        in_specs=[ANY] * 5 + [far],
        scratch_shapes=[
            pltpu.VMEM((total, hid), BF16),
            pltpu.VMEM((hid, feats), BF16),
            pltpu.VMEM((total, 2 * hid), BF16),
        ]
        + Scatter.scratch(CHUNKS, rows, width)
        + [dma((3,))]
        + Tiles.scratch(total, 2 * hid, feats // TILE)
        + Chain.scratch(hid, unit, units),
        compiler_params=pltpu.CompilerParams(
            collective_id=5, has_side_effects=True, vmem_limit_bytes=VMEM_BYTES
        ),
        name="ffn_grads",
    )(hidden, w_down, g_both, cot, normed, resid)


LAST_TICKS = 14


def last_kernel(
    dp, units,
    g_pre, w_in, w_for, w_gp, g_mix, normed, mixed, inner, gain_in, sums_in, tok, scale_in, g_resid,
    g_tok, small, total_pre, total_out, d_pre, d_out, peer_pre, peer_out, low_pre, low_out, high_pre, high_out,
    vg, vpre, vmix, ibuf, col, sum_in, mine, others,
    share, keep, out1, in1, out2, in2, send1, recv1, send2, recv2,
    isend, irecv, lsem, osend, orecv,
    lbuf, xbuf, stage, tsem0, tsem1, tsem2, tsem3, buf, *sems,
):
    me = lax.axis_index("dp")
    s = pl.program_id(0)
    chunks = pl.num_programs(0) - 2
    rows, width = g_tok.shape
    feats = w_in.shape[0]
    t, xn, yn, dg = neighbours()
    peers = ({"tensor": xn}, {"tensor": yn}, {"tensor": dg})
    scatter = Scatter(share, keep, out1, in1, out2, in2, (send1, recv1, send2, recv2))

    def inner_copy(k):
        return pltpu.make_async_remote_copy(
            inner, ibuf.at[t], isend.at[k], irecv.at[k], device_id=peers[k], device_id_type=MESH
        )

    def other(d):
        return pltpu.make_async_remote_copy(
            mine, others.at[me], osend.at[d], orecv.at[d],
            device_id={"dp": (me + d) % dp}, device_id_type=MESH,
        )

    loads = (
        pltpu.make_async_copy(g_pre, vg, lsem.at[0]),
        pltpu.make_async_copy(w_in, vpre.at[:, 0:width], lsem.at[1]),
        pltpu.make_async_copy(w_for, vpre.at[:, width : 2 * width], lsem.at[2]),
        pltpu.make_async_copy(w_gp, vpre.at[:, 2 * width :], lsem.at[3]),
        pltpu.make_async_copy(inner, ibuf.at[t], lsem.at[4]),
        pltpu.make_async_copy(g_mix, vmix, lsem.at[5]),
    )
    tiles = Tiles(
        (normed, mixed), (vg, vmix), (lambda: None, loads[5].wait), (d_pre, d_out), (peer_pre, peer_out),
        lbuf, xbuf, stage, (tsem0, tsem1, tsem2, tsem3),
    )
    chain = Chain(
        [d_pre, d_out], units, [total_pre, total_out], [low_pre, low_out], [high_pre, high_out],
        [peer_pre, peer_out], buf, sems, dp, LAG,
    )

    def at_stage(n, act):
        @pl.when((s >= n) & (s - n < chunks))
        def _():
            act(s - n)

    @pl.when(s == 0)
    def _():
        for load in loads:
            load.start()
        tiles.begin()
        greet(peers + tuple({"dp": (me + d) % dp} for d in range(1, dp)))
        for k in range(3):
            inner_copy(k).start()
        sum_in[...] = jnp.zeros(sum_in.shape, F32)
        for load in loads[:5]:
            load.wait()

    @pl.when(s == 2)
    def _():
        for k in range(3):
            inner_copy(k).wait_recv()

    def finish(c):
        total = ibuf[0, c] + ibuf[1, c] + ibuf[2, c] + ibuf[3, c]
        col[...] = jnp.broadcast_to(lanes_to_rows(total) / feats, (rows, 128))
        gain = gain_in[...]

        def give(i, value):
            here = block(i, 32)
            x = tok[here, :].astype(F32)
            scale = scale_in[here, 0:1]
            g_tok[here, :] = (
                g_resid[here, :] + scale * (value * gain) - x * (scale * scale * col[here, 0:1])
            )
            sum_in[...] += fold_rows(value * x * scale)

        scatter.end(c, give)

    base = (s - 1) * LAST_TICKS - 6

    def terms(c):
        def part(b):
            share[b] = back_dot(vg[block(c, rows), :], vpre[block(b, width), :])
            chain.tick(base + 2 + b)

        each(feats // width, part)
        scatter.begin(c)

    at_stage(2, finish)
    chain.tick(base)
    at_stage(1, scatter.middle)
    chain.tick(base + 1)
    at_stage(0, terms)

    @pl.when(s >= chunks)
    def _():
        each(4, lambda j: chain.tick(base + 2 + j))

    tiles.work(s, lambda k: each(2, lambda j: chain.tick(base + 6 + 2 * k + j)))

    @pl.when(s == pl.num_programs(0) - 1)
    def _():
        mine[...] = jnp.zeros(mine.shape, F32)
        mine[0:1, :] = jnp.sum(sum_in[...], axis=0, keepdims=True)
        for k in range(3):
            mine[1 + k : 2 + k, :] = jnp.sum(sums_in[k], axis=0, keepdims=True)
        scatter.drain(CHUNKS)
        for d in range(1, dp):
            other(d).start()
        chain.close(base + LAST_TICKS)
        others[me] = mine[...]
        for d in range(1, dp):
            other(d).wait()
        total = others[0]
        for d in range(1, dp):
            total += others[d]
        small[...] = total
        for k in range(3):
            inner_copy(k).wait_send()


def last_sums(dp, g_pre, w_in, w_for, w_gp, g_mix, normed, mixed, inner, gain_in, sums, tok, scale_in, g_resid):
    feats, width = w_in.shape
    total = g_pre.shape[0]
    rows = total // CHUNKS
    unit = 16
    pre = jax.ShapeDtypeStruct((feats, 3 * width), BF16)
    mix = jax.ShapeDtypeStruct((width, feats), BF16)
    units = (feats // (2 * unit), width // (2 * unit))

    def late(s):
        return (jnp.maximum(s - 2, 0), 0)

    far = pl.BlockSpec((rows, width), late)
    dma = pltpu.SemaphoreType.DMA
    return pl.pallas_call(
        functools.partial(last_kernel, dp, units),
        grid=(CHUNKS + 2,),
        out_shape=[jax.ShapeDtypeStruct((total, width), F32), jax.ShapeDtypeStruct((8, width), F32)]
        + [pre, mix] * 5,
        out_specs=[far, WHOLE] + [ANY] * 10,
        in_specs=[ANY] * 7 + [WHOLE, WHOLE, WHOLE, far, pl.BlockSpec((rows, 128), late), far],
        scratch_shapes=[
            pltpu.VMEM((total, 3 * width), BF16),
            pltpu.VMEM((feats, 3 * width), BF16),
            pltpu.VMEM((total, feats), BF16),
            pltpu.VMEM((4, CHUNKS, 8, rows), F32),
            pltpu.VMEM((rows, 128), F32),
            pltpu.VMEM((8, width), F32),
            pltpu.VMEM((8, width), F32),
            pltpu.VMEM((dp, 8, width), F32),
        ]
        + Scatter.scratch(CHUNKS, rows, width)
        + [dma((3,)), dma((3,)), dma((6,)), dma((dp,)), dma((dp,))]
        + Tiles.scratch(total, feats, feats // (2 * TILE) + width // (2 * TILE))
        + Chain.scratch(feats, unit, units),
        compiler_params=pltpu.CompilerParams(
            collective_id=4, has_side_effects=True, vmem_limit_bytes=VMEM_BYTES
        ),
        name="last_sums",
    )(g_pre, w_in, w_for, w_gp, g_mix, normed, mixed, inner, gain_in, sums, tok, scale_in, g_resid)


def turn_kernel(value, out):
    def part(k):
        rows = block(k, LANES)
        out[rows, :] = value[:, rows].T.astype(F32)

    each(out.shape[0] // LANES, part)


def turned(value):
    rows, cols = value.shape
    return pl.pallas_call(
        turn_kernel,
        grid=(rows // TILE,),
        out_shape=jax.ShapeDtypeStruct((cols, rows), F32),
        in_specs=[pl.BlockSpec((TILE, cols), lambda s: (s, 0))],
        out_specs=pl.BlockSpec((cols, TILE), lambda s: (0, s)),
        name="turned",
    )(value)


def on_device(
    dp, tokens, lengths, cotangent, w_norm_in, w_input, w_forget, w_gproj, lower_bound, w_gate_norm,
    w_output, w_norm_mid, w_gate, w_up, w_down,
):
    channels, hid = w_input.shape[1], w_gate.shape[1]
    gain_in = w_norm_in.astype(F32)[None]
    gains = jnp.concatenate([gain_in, w_norm_mid.astype(F32)[None], jnp.zeros((6, channels), F32)], 0)
    lower = lower_bound.astype(F32)[None]
    gain_gate = w_gate_norm.astype(F32)[None]
    (
        normed_in, tok_full, wout_full, gains_full, scale_in, pre_in, pre_for, pre_gp, state, diff, raw, squares,
    ) = mixer_forward(tokens, w_output, gains, w_input, w_forget, w_gproj, lower, gain_gate)
    normed_mid, hidden, g_both, cot, mix, scale_gate, scale_mid, resid = ffn_forward(
        lengths, raw, cotangent, squares, gains_full, tok_full, wout_full, w_gate, w_up, w_down
    )
    output, s_down, d_both, peer_both = ffn_grads(dp, hidden, w_down, g_both, cot, normed_mid, resid)[:4]
    g_mix, g_resid, g_pre, mixed, inner, sums, s_both = backward(
        dp, d_both, peer_both, g_both, w_gate, w_up, w_output, gains_full, gain_gate, lower,
        cot, mix, tok_full, scale_mid, scale_gate, pre_in, pre_for, pre_gp, state, diff,
    )[:7]
    if BACK != CHUNKS:
        inner = inner.reshape(CHUNKS, BACK // CHUNKS, 8, -1).swapaxes(1, 2).reshape(CHUNKS, 8, -1)
    g_tok, small, s_pre, s_out = last_sums(
        dp, g_pre, w_input, w_forget, w_gproj, g_mix, normed_in, mixed, inner, gain_in, sums, tokens, scale_in, g_resid
    )[:4]
    pre = [s_pre[:, k * channels : (k + 1) * channels].astype(F32) for k in range(3)]
    return (
        output, g_tok, small[0], pre[0], pre[1], pre[2], small[3], small[2], s_out.astype(F32), small[1],
        s_both[:, :hid].astype(F32), s_both[:, hid:].astype(F32), turned(s_down),
    )


D = 2048
SLOTS = 2048


def linear_scan(decay, source):

    def compose(earlier, later):
        return (earlier[0] * later[0], later[0] * earlier[1] + later[1])

    return lax.associative_scan(compose, (decay, source), axis=1)[1]


def any_plane(
    tokens,
    lengths,
    cotangent,
    w_norm_in,
    w_input,
    w_forget,
    w_gproj,
    lower_bound,
    w_gate_norm,
    w_output,
    w_norm_mid,
    w_gate,
    w_up,
    w_down,
):
    row_count = tokens.shape[0]
    seq_count = row_count // SLOTS
    channels = w_input.shape[1]
    block_shape = (seq_count, SLOTS, channels)
    gathered, gain_rows = (
        lax.all_gather(tokens, "tensor", axis=1, tiled=True),
        lax.all_gather(w_norm_in[None, :], "tensor", axis=1, tiled=True),
    )
    whole_rows = gathered.astype(jnp.float32)
    gain_in_full = gain_rows[0].astype(jnp.float32)
    scale_in = lax.rsqrt(jnp.mean(whole_rows * whole_rows, axis=1, keepdims=True) + EPSILON)
    normed_in = (whole_rows * scale_in * gain_in_full).astype(jnp.bfloat16)
    in_pre = plain_dot(normed_in, w_input)
    forget_pre = plain_dot(normed_in, w_forget)
    gate_pre = plain_dot(normed_in, w_gproj)
    inner = jax.nn.silu(in_pre)
    forget_sig = jax.nn.sigmoid(forget_pre)
    lower = lower_bound.astype(jnp.float32)
    decay = lower + (1.0 - lower) * forget_sig
    decay_blocks = decay.reshape(block_shape)
    state = linear_scan(decay_blocks, ((1.0 - decay) * inner).reshape(block_shape)).reshape(
        row_count, channels
    )
    state_total = lax.psum(jnp.sum(state * state, axis=1), "tensor")
    gate_scale = lax.rsqrt(state_total / D + EPSILON)[:, None]
    normed_state = state * gate_scale
    swish_gate = jax.nn.silu(gate_pre)
    gain_gate = w_gate_norm.astype(jnp.float32)
    mixed = (normed_state * gain_gate * swish_gate).astype(jnp.bfloat16)
    mix_share = lax.psum_scatter(
        plain_dot(mixed, w_output), "tensor", scatter_dimension=1, tiled=True
    )
    token_share = tokens.astype(jnp.float32)
    resid = token_share + mix_share
    resid_total = lax.psum(jnp.sum(resid * resid, axis=1), "tensor")
    scale_mid = lax.rsqrt(resid_total / D + EPSILON)[:, None]
    gain_mid = w_norm_mid.astype(jnp.float32)
    normed_part = (resid * scale_mid * gain_mid).astype(jnp.bfloat16)
    normed_mid = lax.all_gather(normed_part, "tensor", axis=1, tiled=True)
    ffn_gate = plain_dot(normed_mid, w_gate)
    ffn_up = plain_dot(normed_mid, w_up)
    gate_act = jax.nn.silu(ffn_gate)
    hidden = (gate_act * ffn_up).astype(jnp.bfloat16)
    ffn_share = lax.psum_scatter(
        plain_dot(hidden, w_down).astype(jnp.bfloat16), "tensor", scatter_dimension=1, tiled=True
    ).astype(jnp.float32)
    output = (resid + ffn_share).astype(jnp.bfloat16)
    positions = jnp.arange(SLOTS, dtype=jnp.int32)
    valid = (positions[None, :] < lengths[:, None]).reshape(row_count, 1)
    masked_cot = cotangent * valid.astype(jnp.bfloat16)
    cot_full = lax.all_gather(masked_cot, "tensor", axis=1, tiled=True)
    grad_down_w = trans_dot(hidden, cot_full)
    grad_hidden = back_dot(cot_full, w_down)
    grad_ffn_gate = (grad_hidden * ffn_up * silu_slope(ffn_gate)).astype(jnp.bfloat16)
    grad_ffn_up = (grad_hidden * gate_act).astype(jnp.bfloat16)
    grad_gate_w = trans_dot(normed_mid, grad_ffn_gate)
    grad_up_w = trans_dot(normed_mid, grad_ffn_up)
    grad_normed_mid = lax.psum_scatter(
        back_dot(grad_ffn_gate, w_gate) + back_dot(grad_ffn_up, w_up),
        "tensor",
        scatter_dimension=1,
        tiled=True,
    )
    grad_gain_mid = jnp.sum(grad_normed_mid * resid * scale_mid, axis=0)
    weighted_mid = grad_normed_mid * gain_mid
    mid_total = lax.psum(jnp.sum(weighted_mid * resid, axis=1), "tensor")
    grad_resid = (
        masked_cot.astype(jnp.float32)
        + scale_mid * weighted_mid
        - resid * scale_mid**3 * (mid_total / D)[:, None]
    )
    ffn_terms = (grad_gain_mid, grad_gate_w, grad_up_w, grad_down_w)
    grad_mix = lax.all_gather(grad_resid.astype(jnp.bfloat16), "tensor", axis=1, tiled=True)
    grad_output_w = trans_dot(mixed, grad_mix)
    grad_mixed = back_dot(grad_mix, w_output)
    grad_gain_gate = jnp.sum(grad_mixed * normed_state * swish_gate, axis=0)
    grad_gate_pre = (grad_mixed * normed_state * gain_gate * silu_slope(gate_pre)).astype(
        jnp.bfloat16
    )
    grad_normed_state = grad_mixed * gain_gate * swish_gate
    state_inner = lax.psum(jnp.sum(grad_normed_state * state, axis=1), "tensor")
    grad_state = gate_scale * grad_normed_state - state * gate_scale**3 * (state_inner / D)[:, None]
    state_blocks = state.reshape(block_shape)
    next_decay = jnp.concatenate(
        [decay_blocks[:, 1:], jnp.zeros((seq_count, 1, channels), jnp.float32)], axis=1
    )
    adjoint = jnp.flip(
        linear_scan(jnp.flip(next_decay, 1), jnp.flip(grad_state.reshape(block_shape), 1)), 1
    ).reshape(row_count, channels)
    prev_state = jnp.concatenate(
        [jnp.zeros((seq_count, 1, channels), jnp.float32), state_blocks[:, :-1]], axis=1
    ).reshape(row_count, channels)
    grad_decay = adjoint * (prev_state - inner)
    grad_in_pre = (adjoint * (1.0 - decay) * silu_slope(in_pre)).astype(jnp.bfloat16)
    grad_forget_pre = (grad_decay * (1.0 - lower) * forget_sig * (1.0 - forget_sig)).astype(
        jnp.bfloat16
    )
    grad_lower = jnp.sum(grad_decay * (1.0 - forget_sig), axis=0)
    grad_input_w = trans_dot(normed_in, grad_in_pre)
    grad_forget_w = trans_dot(normed_in, grad_forget_pre)
    grad_gproj_w = trans_dot(normed_in, grad_gate_pre)
    grad_normed_in = lax.psum_scatter(
        (
            back_dot(grad_in_pre, w_input)
            + back_dot(grad_forget_pre, w_forget)
            + back_dot(grad_gate_pre, w_gproj)
        ).astype(jnp.bfloat16),
        "tensor",
        scatter_dimension=1,
        tiled=True,
    ).astype(jnp.float32)
    gain_in_share = w_norm_in.astype(jnp.float32)
    grad_gain_in = jnp.sum(grad_normed_in * token_share * scale_in, axis=0)
    weighted_in = grad_normed_in * gain_in_share
    in_total = lax.psum(jnp.sum(weighted_in * token_share, axis=1), "tensor")
    grad_tokens = (
        grad_resid + scale_in * weighted_in - token_share * scale_in**3 * (in_total / D)[:, None]
    )
    mixer_terms = (
        grad_gain_in,
        grad_input_w,
        grad_forget_w,
        grad_gproj_w,
        grad_lower,
        grad_gain_gate,
        grad_output_w,
    )
    summed = lax.psum(mixer_terms + ffn_terms, "dp")
    mixer_terms = summed[:7]
    ffn_terms = summed[7:]
    return (
        output,
        grad_tokens,
        mixer_terms[0],
        mixer_terms[1],
        mixer_terms[2],
        mixer_terms[3],
        mixer_terms[4],
        mixer_terms[5],
        mixer_terms[6],
        ffn_terms[0],
        ffn_terms[1],
        ffn_terms[2],
        ffn_terms[3],
    )


def solution(mesh):
    rows, cols, vec = P(None, "tensor"), P("tensor", None), P("tensor")
    both = P("dp", "tensor")
    in_specs = (both, P("dp"), both, vec, rows, rows, rows, vec, vec, cols, vec, rows, rows, cols)
    out_specs = (both, both, vec, rows, rows, rows, vec, vec, cols, vec, rows, rows, cols)
    square = mesh.shape["tensor"] == 4 and mesh.shape["dp"] % 2 == 0
    body = functools.partial(on_device, mesh.shape["dp"]) if square else any_plane
    return jax.shard_map(
        body, mesh=mesh, in_specs=in_specs, out_specs=out_specs,
        check_vma=False,
    )
```
